128 devices in a mesh: basis: 16 (over x, z_lo, core), orb: 8 (over z_hi, y).
Axes of the slice: x: 4, y: 4, z: 4 (z_hi: 2, z_lo: 2; z = z_hi * 2 + z_lo), core: 2. Of those that a mesh axis runs over, the one named last changes fastest.
Arguments:
- cont_orbitals: bfloat16 [65536, 2048], P('basis', 'orb'), may hold values from -6 to 6
- target_orbitals: bfloat16 [65536, 1024], P('basis'), may hold values from -0.09375 to 0.09375
- margin_blocks: bfloat16 [256, 4, 256, 256], P('basis'), may hold values from -0.1875 to 0.1875
- dipole_blocks: bfloat16 [256, 4, 256, 256], P('basis'), may hold values from -0.1875 to 0.1875
- band_offsets: int32 [256, 4], P('basis'), may hold values from -2 to 2, as said below
Outputs:
- cont_orth: bfloat16 [65536, 2048], P('basis', 'orb')
- dipole_mo: bfloat16 [1024, 2048], P('basis', 'orb')
The draws below stay inside these ranges and needn't reach their ends.
Inputs may be any that keep to these rules, and one draw needn't show every extreme that they name: `band_offsets`: each block row names 4 different offsets.
All inputs are finite; a program needn't handle non-finite values.
Results may differ from the reference program's by a relative error of at most 0.012.
Values may be sent and summed in bfloat16 or wider, within the bound.
A program may use at most 128 MiB of HBM per device.

```python
import jax
import jax.numpy as jnp
from jax import lax

BK = 256
KB = 4
NT = 1024
NC = 2048
NBLK = 256
NB = 65536


def draw_band_offsets(key, part):
    dropped = jax.random.randint(key, (NBLK, 1), 0, 5)
    base = jnp.arange(4, dtype=jnp.int32)[None, :]
    shifted = base + (base >= dropped).astype(jnp.int32) - 2
    return shifted.astype(jnp.int32)


def block_scale(key, shape, cuts, least, high):
    loudness = 1.0
    for dim, parts in cuts:
        draws = jax.random.uniform(jax.random.fold_in(jax.random.fold_in(key, 6), dim), (parts,), jnp.float32, least / len(cuts), high / len(cuts))
        loudness = loudness * jnp.repeat(jnp.exp(draws), shape[dim] // parts).reshape((-1,) + (1,) * (len(shape) - 1 - dim))
    return loudness


def noise(key, extent, scale, most, pieces=(), held_as=jnp.bfloat16):
    entries = jax.random.normal(key, extent, jnp.float32) * scale
    if len(pieces) > 0:
        entries = block_scale(key, extent, pieces, -0.22, 0.18) * entries
    return jnp.clip(entries, min=-most, max=most).astype(held_as)


def setup_inputs(seed: int = 0) -> dict:
    seeds = jax.random.split(jax.random.key(seed), 6)
    return {
        "cont_orbitals": noise(seeds[0], (NB, NC), 1.0, 6.0, ((0, 16), (1, 8))),
        "target_orbitals": noise(seeds[1], (NB, NT), (4 * NT) ** -0.5, 0.09375, ((0, 16),)),
        "margin_blocks": noise(seeds[2], (NBLK, KB, BK, BK), (KB * BK) ** -0.5, 0.1875, ((0, 16),)),
        "dipole_blocks": noise(seeds[3], (NBLK, KB, BK, BK), (KB * BK) ** -0.5, 0.1875, ((0, 16),)),
        "band_offsets": draw_band_offsets(jax.random.fold_in(seeds[5], 71), 0),
    }


def band_apply(blocks, offsets, field):
    nblk = blocks.shape[0]
    width = field.shape[1]
    padded = jnp.pad(field, ((2 * BK, 2 * BK), (0, 0))).reshape(nblk + 4, BK, width)
    total = jnp.zeros((nblk, BK, width), jnp.float32)
    for k in range(KB):
        index = (jnp.arange(nblk, dtype=jnp.int32) + 2 + offsets[:, k].astype(jnp.int32)).astype(jnp.int32)
        taken = padded[index]
        total = total + jnp.einsum('bij,bjc->bic', blocks[:, k].astype(jnp.float32), taken.astype(jnp.float32))
    return total.reshape(nblk * BK, width)

def reference(cont_orbitals, target_orbitals, margin_blocks, dipole_blocks, band_offsets):
    margin_cont = band_apply(margin_blocks, band_offsets, cont_orbitals).astype(jnp.bfloat16)
    projection = jnp.dot(target_orbitals.T, margin_cont, preferred_element_type=jnp.float32)
    projection_b = projection.astype(jnp.bfloat16)
    removed = jnp.dot(target_orbitals, projection_b, preferred_element_type=jnp.float32)
    cont_orth = (cont_orbitals.astype(jnp.float32) - removed).astype(jnp.bfloat16)
    squares = lax.optimization_barrier(jnp.sum(jnp.square(cont_orth.astype(jnp.float32)), axis=0))
    col_norm = 1.0 / jnp.sqrt(squares / NB + 1e-06)
    dipole_cont = band_apply(dipole_blocks, band_offsets, cont_orth).astype(jnp.bfloat16)
    dipole_raw = jnp.dot(target_orbitals.T, dipole_cont, preferred_element_type=jnp.float32)
    dipole_mo = (dipole_raw * col_norm[None, :]).astype(jnp.bfloat16)
    return (cont_orth, dipole_mo)
```

```python
import functools

import jax
import jax.numpy as jnp
from jax import lax
from jax.experimental import pallas as pl
from jax.experimental.pallas import tpu as pltpu
from jax.sharding import PartitionSpec as P

BK = 256
KB = 4
MESH = pl.DeviceIdType.MESH


def padded_2(block, sides, width):
    for axis, dim in sides:
        count = lax.axis_size(axis)
        forward = [(i, i + 1) for i in range(count - 1)]
        backward = [(target, source) for source, target in forward]
        low = lax.ppermute(
            lax.slice_in_dim(block, block.shape[dim] - width, None, axis=dim), axis, forward
        )
        high = lax.ppermute(lax.slice_in_dim(block, 0, width, axis=dim), axis, backward)
        block = jnp.concatenate([low, block, high], axis=dim)
    return block


def band_local(blocks, offsets, padded):
    nblk = blocks.shape[0]
    width = padded.shape[1]
    stacked = padded.reshape(nblk + 4, BK, width)
    total = jnp.zeros((nblk, BK, width), jnp.float32)
    for k in range(KB):
        index = jnp.arange(nblk, dtype=jnp.int32) + 2 + offsets[:, k]
        taken = stacked[index]
        total = total + jnp.einsum(
            "bij,bjc->bic", blocks[:, k], taken, preferred_element_type=jnp.float32
        )
    return total.reshape(nblk * BK, width)


def _barrier_all(n, me, orb):
    barrier = pltpu.get_barrier_semaphore()
    for j in range(1, n):
        peer = lax.rem(me + j, n)
        pl.semaphore_signal(barrier, inc=1, device_id=(peer, orb), device_id_type=MESH)
    pl.semaphore_wait(barrier, n - 1)


def _scatter_sum(n, me, orb, x_ref, recv, send_sem, recv_sem):
    sends = []
    for j in range(1, n):
        peer = lax.rem(me + j, n)
        c = pltpu.make_async_remote_copy(
            src_ref=x_ref.at[peer],
            dst_ref=recv.at[me],
            send_sem=send_sem.at[j],
            recv_sem=recv_sem.at[me],
            device_id=(peer, orb),
            device_id_type=MESH,
        )
        c.start()
        sends.append(c)
    acc = x_ref[me]
    for j in range(1, n):
        src = lax.rem(me + n - j, n)
        pltpu.make_async_remote_copy(
            src_ref=x_ref.at[src],
            dst_ref=recv.at[src],
            send_sem=send_sem.at[j],
            recv_sem=recv_sem.at[src],
            device_id=(src, orb),
            device_id_type=MESH,
        ).wait_recv()
        acc = acc + recv[src]
    for c in sends:
        c.wait_send()
    return acc


def allreduce_kernel(n, x_ref, out_ref, recv, sendbuf, gath, rs_send, rs_recv, ag_send, ag_recv):
    me = lax.axis_index("basis")
    orb = lax.axis_index("orb")
    _barrier_all(n, me, orb)
    total = _scatter_sum(n, me, orb, x_ref, recv, rs_send, rs_recv)
    rounded = total.astype(out_ref.dtype)
    sendbuf[...] = rounded
    out_ref[me] = rounded
    sends = []
    for j in range(1, n):
        peer = lax.rem(me + j, n)
        c = pltpu.make_async_remote_copy(
            src_ref=sendbuf,
            dst_ref=gath.at[me],
            send_sem=ag_send.at[j],
            recv_sem=ag_recv.at[me],
            device_id=(peer, orb),
            device_id_type=MESH,
        )
        c.start()
        sends.append(c)
    for j in range(1, n):
        src = lax.rem(me + n - j, n)
        pltpu.make_async_remote_copy(
            src_ref=sendbuf,
            dst_ref=gath.at[src],
            send_sem=ag_send.at[j],
            recv_sem=ag_recv.at[src],
            device_id=(src, orb),
            device_id_type=MESH,
        ).wait_recv()
        out_ref[src] = gath[src]
    for c in sends:
        c.wait_send()


def allreduce_to_bf16(partial, n):
    rows, cols = partial.shape
    chunk = rows // n
    x = partial.reshape(n, chunk, cols)
    out = pl.pallas_call(
        functools.partial(allreduce_kernel, n),
        out_shape=jax.ShapeDtypeStruct((n, chunk, cols), jnp.bfloat16),
        in_specs=[pl.BlockSpec(memory_space=pltpu.VMEM)],
        out_specs=pl.BlockSpec(memory_space=pltpu.VMEM),
        scratch_shapes=[
            pltpu.VMEM((n, chunk, cols), jnp.float32),
            pltpu.VMEM((chunk, cols), jnp.bfloat16),
            pltpu.VMEM((n, chunk, cols), jnp.bfloat16),
            pltpu.SemaphoreType.DMA((n,)),
            pltpu.SemaphoreType.DMA((n,)),
            pltpu.SemaphoreType.DMA((n,)),
            pltpu.SemaphoreType.DMA((n,)),
        ],
        compiler_params=pltpu.CompilerParams(collective_id=0, has_side_effects=True),
    )(x)
    return out.reshape(rows, cols)


def dipole_kernel(n, chunk, count, x_ref, out_ref, recv, rs_send, rs_recv):
    me = lax.axis_index("basis")
    orb = lax.axis_index("orb")
    _barrier_all(n, me, orb)
    total = _scatter_sum(n, me, orb, x_ref, recv, rs_send, rs_recv)
    squares = total[chunk:chunk + 1, :]
    col_norm = 1.0 / jnp.sqrt(squares / count + 1e-06)
    out_ref[...] = (total[:chunk, :] * col_norm).astype(out_ref.dtype)


def dipole_scatter(partial, squares, n, count):
    rows, cols = partial.shape
    chunk = rows // n
    x = jnp.concatenate(
        [partial.reshape(n, chunk, cols), jnp.broadcast_to(squares[None, None, :], (n, 8, cols))],
        axis=1,
    )
    return pl.pallas_call(
        functools.partial(dipole_kernel, n, chunk, count),
        out_shape=jax.ShapeDtypeStruct((chunk, cols), jnp.bfloat16),
        in_specs=[pl.BlockSpec(memory_space=pltpu.VMEM)],
        out_specs=pl.BlockSpec(memory_space=pltpu.VMEM),
        scratch_shapes=[
            pltpu.VMEM((n, chunk + 8, cols), jnp.float32),
            pltpu.SemaphoreType.DMA((n,)),
            pltpu.SemaphoreType.DMA((n,)),
        ],
        compiler_params=pltpu.CompilerParams(collective_id=1, has_side_effects=True),
    )(x)


def on_device(cont_orbitals, target_orbitals, margin_blocks, dipole_blocks, band_offsets):
    n = lax.axis_size("basis")
    count = band_offsets.shape[0] * BK * n
    cont_padded = padded_2(cont_orbitals, (("basis", 0),), 2 * BK)
    margin_cont = band_local(margin_blocks, band_offsets, cont_padded).astype(jnp.bfloat16)
    partial_proj = lax.dot_general(
        target_orbitals, margin_cont, (((0,), (0,)), ((), ())), preferred_element_type=jnp.float32
    )
    projection_b = allreduce_to_bf16(partial_proj, n)
    removed = jnp.dot(target_orbitals, projection_b, preferred_element_type=jnp.float32)
    cont_orth = (cont_orbitals.astype(jnp.float32) - removed).astype(jnp.bfloat16)
    squares = jnp.sum(jnp.square(cont_orth.astype(jnp.float32)), axis=0)
    orth_padded = padded_2(cont_orth, (("basis", 0),), 2 * BK)
    dipole_cont = band_local(dipole_blocks, band_offsets, orth_padded).astype(jnp.bfloat16)
    partial_dip = lax.dot_general(
        target_orbitals,
        dipole_cont,
        (((0,), (0,)), ((), ())),
        preferred_element_type=jnp.float32,
    )
    dipole_mo = dipole_scatter(partial_dip, squares, n, count)
    return (cont_orth, dipole_mo)


def solution(mesh):
    return jax.shard_map(
        on_device,
        mesh=mesh,
        in_specs=(
            P("basis", "orb"),
            P("basis", None),
            P("basis", None, None, None),
            P("basis", None, None, None),
            P("basis", None),
        ),
        out_specs=(P("basis", "orb"), P("basis", "orb")),
        check_vma=False,
    )
```

```python
import functools

import jax
import jax.numpy as jnp
from jax import lax
from jax.experimental import pallas as pl
from jax.experimental.pallas import tpu as pltpu
from jax.sharding import PartitionSpec as P

BK = 256
KB = 4
MESH = pl.DeviceIdType.MESH


def padded_2(block, sides, width):
    for axis, dim in sides:
        count = lax.axis_size(axis)
        forward = [(i, i + 1) for i in range(count - 1)]
        backward = [(target, source) for source, target in forward]
        low = lax.ppermute(
            lax.slice_in_dim(block, block.shape[dim] - width, None, axis=dim), axis, forward
        )
        high = lax.ppermute(lax.slice_in_dim(block, 0, width, axis=dim), axis, backward)
        block = jnp.concatenate([low, block, high], axis=dim)
    return block


def band_kernel(off_ref, blk_ref, field_ref, out_ref):
    b = pl.program_id(0)
    acc = None
    for k in range(KB):
        start = pl.multiple_of((b + 2 + off_ref[b, k]) * BK, BK)
        term = jnp.dot(
            blk_ref[0, k], field_ref[pl.ds(start, BK), :], preferred_element_type=jnp.float32
        )
        acc = term if acc is None else acc + term
    out_ref[...] = acc.astype(out_ref.dtype)


def band_local(blocks, offsets, padded):
    nblk = blocks.shape[0]
    rows, width = padded.shape
    return pl.pallas_call(
        band_kernel,
        out_shape=jax.ShapeDtypeStruct((nblk * BK, width), jnp.bfloat16),
        grid_spec=pltpu.PrefetchScalarGridSpec(
            num_scalar_prefetch=1,
            grid=(nblk,),
            in_specs=[
                pl.BlockSpec((1, KB, BK, BK), lambda b, off: (b, 0, 0, 0)),
                pl.BlockSpec((rows, width), lambda b, off: (0, 0)),
            ],
            out_specs=pl.BlockSpec((BK, width), lambda b, off: (b, 0)),
        ),
        cost_estimate=pl.CostEstimate(
            flops=2 * nblk * KB * BK * BK * width,
            bytes_accessed=blocks.size * 2 + padded.size * 2 + nblk * BK * width * 2,
            transcendentals=0,
        ),
    )(offsets, blocks, padded)


def _barrier_all(n, me, orb):
    barrier = pltpu.get_barrier_semaphore()
    for j in range(1, n):
        peer = lax.rem(me + j, n)
        pl.semaphore_signal(barrier, inc=1, device_id=(peer, orb), device_id_type=MESH)
    pl.semaphore_wait(barrier, n - 1)


def _scatter_sum(n, me, orb, x_ref, recv, send_sem, recv_sem):
    sends = []
    for j in range(1, n):
        peer = lax.rem(me + j, n)
        c = pltpu.make_async_remote_copy(
            src_ref=x_ref.at[peer],
            dst_ref=recv.at[me],
            send_sem=send_sem.at[j],
            recv_sem=recv_sem.at[me],
            device_id=(peer, orb),
            device_id_type=MESH,
        )
        c.start()
        sends.append(c)
    acc = x_ref[me]
    for j in range(1, n):
        src = lax.rem(me + n - j, n)
        pltpu.make_async_remote_copy(
            src_ref=x_ref.at[src],
            dst_ref=recv.at[src],
            send_sem=send_sem.at[j],
            recv_sem=recv_sem.at[src],
            device_id=(src, orb),
            device_id_type=MESH,
        ).wait_recv()
        acc = acc + recv[src]
    for c in sends:
        c.wait_send()
    return acc


def allreduce_kernel(n, x_ref, out_ref, recv, sendbuf, gath, rs_send, rs_recv, ag_send, ag_recv):
    me = lax.axis_index("basis")
    orb = lax.axis_index("orb")
    _barrier_all(n, me, orb)
    total = _scatter_sum(n, me, orb, x_ref, recv, rs_send, rs_recv)
    rounded = total.astype(out_ref.dtype)
    sendbuf[...] = rounded
    out_ref[me] = rounded
    sends = []
    for j in range(1, n):
        peer = lax.rem(me + j, n)
        c = pltpu.make_async_remote_copy(
            src_ref=sendbuf,
            dst_ref=gath.at[me],
            send_sem=ag_send.at[j],
            recv_sem=ag_recv.at[me],
            device_id=(peer, orb),
            device_id_type=MESH,
        )
        c.start()
        sends.append(c)
    for j in range(1, n):
        src = lax.rem(me + n - j, n)
        pltpu.make_async_remote_copy(
            src_ref=sendbuf,
            dst_ref=gath.at[src],
            send_sem=ag_send.at[j],
            recv_sem=ag_recv.at[src],
            device_id=(src, orb),
            device_id_type=MESH,
        ).wait_recv()
        out_ref[src] = gath[src]
    for c in sends:
        c.wait_send()


def allreduce_to_bf16(partial, n):
    rows, cols = partial.shape
    chunk = rows // n
    x = partial.reshape(n, chunk, cols)
    out = pl.pallas_call(
        functools.partial(allreduce_kernel, n),
        out_shape=jax.ShapeDtypeStruct((n, chunk, cols), jnp.bfloat16),
        in_specs=[pl.BlockSpec(memory_space=pltpu.VMEM)],
        out_specs=pl.BlockSpec(memory_space=pltpu.VMEM),
        scratch_shapes=[
            pltpu.VMEM((n, chunk, cols), jnp.float32),
            pltpu.VMEM((chunk, cols), jnp.bfloat16),
            pltpu.VMEM((n, chunk, cols), jnp.bfloat16),
            pltpu.SemaphoreType.DMA((n,)),
            pltpu.SemaphoreType.DMA((n,)),
            pltpu.SemaphoreType.DMA((n,)),
            pltpu.SemaphoreType.DMA((n,)),
        ],
        compiler_params=pltpu.CompilerParams(collective_id=0, has_side_effects=True),
    )(x)
    return out.reshape(rows, cols)


def dipole_kernel(n, chunk, count, x_ref, out_ref, recv, rs_send, rs_recv):
    me = lax.axis_index("basis")
    orb = lax.axis_index("orb")
    _barrier_all(n, me, orb)
    total = _scatter_sum(n, me, orb, x_ref, recv, rs_send, rs_recv)
    squares = total[chunk:chunk + 1, :]
    col_norm = 1.0 / jnp.sqrt(squares / count + 1e-06)
    out_ref[...] = (total[:chunk, :] * col_norm).astype(out_ref.dtype)


def dipole_scatter(partial, squares, n, count):
    rows, cols = partial.shape
    chunk = rows // n
    x = jnp.concatenate(
        [partial.reshape(n, chunk, cols), jnp.broadcast_to(squares[None, None, :], (n, 8, cols))],
        axis=1,
    )
    return pl.pallas_call(
        functools.partial(dipole_kernel, n, chunk, count),
        out_shape=jax.ShapeDtypeStruct((chunk, cols), jnp.bfloat16),
        in_specs=[pl.BlockSpec(memory_space=pltpu.VMEM)],
        out_specs=pl.BlockSpec(memory_space=pltpu.VMEM),
        scratch_shapes=[
            pltpu.VMEM((n, chunk + 8, cols), jnp.float32),
            pltpu.SemaphoreType.DMA((n,)),
            pltpu.SemaphoreType.DMA((n,)),
        ],
        compiler_params=pltpu.CompilerParams(collective_id=1, has_side_effects=True),
    )(x)


def on_device(cont_orbitals, target_orbitals, margin_blocks, dipole_blocks, band_offsets):
    n = lax.axis_size("basis")
    count = band_offsets.shape[0] * BK * n
    cont_padded = padded_2(cont_orbitals, (("basis", 0),), 2 * BK)
    margin_cont = band_local(margin_blocks, band_offsets, cont_padded)
    partial_proj = lax.dot_general(
        target_orbitals, margin_cont, (((0,), (0,)), ((), ())), preferred_element_type=jnp.float32
    )
    projection_b = allreduce_to_bf16(partial_proj, n)
    removed = jnp.dot(target_orbitals, projection_b, preferred_element_type=jnp.float32)
    cont_orth = (cont_orbitals.astype(jnp.float32) - removed).astype(jnp.bfloat16)
    squares = jnp.sum(jnp.square(cont_orth.astype(jnp.float32)), axis=0)
    orth_padded = padded_2(cont_orth, (("basis", 0),), 2 * BK)
    dipole_cont = band_local(dipole_blocks, band_offsets, orth_padded)
    partial_dip = lax.dot_general(
        target_orbitals,
        dipole_cont,
        (((0,), (0,)), ((), ())),
        preferred_element_type=jnp.float32,
    )
    dipole_mo = dipole_scatter(partial_dip, squares, n, count)
    return (cont_orth, dipole_mo)


def solution(mesh):
    return jax.shard_map(
        on_device,
        mesh=mesh,
        in_specs=(
            P("basis", "orb"),
            P("basis", None),
            P("basis", None, None, None),
            P("basis", None, None, None),
            P("basis", None),
        ),
        out_specs=(P("basis", "orb"), P("basis", "orb")),
        check_vma=False,
    )
```

```python
import functools

import jax
import jax.numpy as jnp
from jax import lax
from jax.experimental import pallas as pl
from jax.experimental.pallas import tpu as pltpu
from jax.sharding import PartitionSpec as P

BK = 256
KB = 4
MESH = pl.DeviceIdType.MESH


def padded_2(block, sides, width):
    for axis, dim in sides:
        count = lax.axis_size(axis)
        forward = [(i, i + 1) for i in range(count - 1)]
        backward = [(target, source) for source, target in forward]
        low = lax.ppermute(
            lax.slice_in_dim(block, block.shape[dim] - width, None, axis=dim), axis, forward
        )
        high = lax.ppermute(lax.slice_in_dim(block, 0, width, axis=dim), axis, backward)
        block = jnp.concatenate([low, block, high], axis=dim)
    return block


def band_kernel(off_ref, blk_ref, field_ref, out_ref):
    b = pl.program_id(0)
    acc = None
    for k in range(KB):
        start = pl.multiple_of((b + 2 + off_ref[b, k]) * BK, BK)
        term = jnp.dot(
            blk_ref[0, k], field_ref[pl.ds(start, BK), :], preferred_element_type=jnp.float32
        )
        acc = term if acc is None else acc + term
    out_ref[...] = acc.astype(out_ref.dtype)


def band_local(blocks, offsets, padded):
    nblk = blocks.shape[0]
    rows, width = padded.shape
    return pl.pallas_call(
        band_kernel,
        out_shape=jax.ShapeDtypeStruct((nblk * BK, width), jnp.bfloat16),
        grid_spec=pltpu.PrefetchScalarGridSpec(
            num_scalar_prefetch=1,
            grid=(nblk,),
            in_specs=[
                pl.BlockSpec((1, KB, BK, BK), lambda b, off: (b, 0, 0, 0)),
                pl.BlockSpec((rows, width), lambda b, off: (0, 0)),
            ],
            out_specs=pl.BlockSpec((BK, width), lambda b, off: (b, 0)),
        ),
        cost_estimate=pl.CostEstimate(
            flops=2 * nblk * KB * BK * BK * width,
            bytes_accessed=blocks.size * 2 + padded.size * 2 + nblk * BK * width * 2,
            transcendentals=0,
        ),
    )(offsets, blocks, padded)


def _place():
    me = lax.axis_index("basis")
    orb = lax.axis_index("orb")
    core = lax.rem(me, 2)
    partner = me + 1 - 2 * core
    chip = lax.div(me, 2)
    return orb, core, partner, chip


def _barrier_group(nchip, orb, core, partner, chip):
    barrier = pltpu.get_barrier_semaphore()
    pl.semaphore_signal(barrier, inc=1, device_id=(partner, orb), device_id_type=MESH)
    for j in range(1, nchip):
        peer = 2 * lax.rem(chip + j, nchip) + core
        pl.semaphore_signal(barrier, inc=1, device_id=(peer, orb), device_id_type=MESH)
    pl.semaphore_wait(barrier, nchip)


def _remote(src, dst, ssem, rsem, device, orb):
    return pltpu.make_async_remote_copy(
        src_ref=src, dst_ref=dst, send_sem=ssem, recv_sem=rsem,
        device_id=(device, orb), device_id_type=MESH,
    )


def _two_level_sum(nchip, x_ref, pair_recv, part, chip_recv, p_send, p_recv, c_send, c_recv):
    orb, core, partner, chip = _place()
    _barrier_group(nchip, orb, core, partner, chip)
    pair = []
    for i in range(nchip):
        cp = _remote(x_ref.at[i, 1 - core], pair_recv.at[i], p_send.at[i], p_recv.at[i], partner, orb)
        cp.start()
        pair.append(cp)
    for i in range(nchip):
        pair[i].wait_recv()
        part[i] = x_ref[i, core] + pair_recv[i]
    sends = []
    for j in range(1, nchip):
        dst = lax.rem(chip + j, nchip)
        cp = _remote(part.at[dst], chip_recv.at[chip], c_send.at[j], c_recv.at[chip], 2 * dst + core, orb)
        cp.start()
        sends.append(cp)
    total = part[chip]
    for j in range(1, nchip):
        src = lax.rem(chip + nchip - j, nchip)
        _remote(part.at[src], chip_recv.at[src], c_send.at[j], c_recv.at[src], 2 * src + core, orb).wait_recv()
        total = total + chip_recv[src]
    for cp in pair + sends:
        cp.wait_send()
    return total


def allreduce_kernel(nchip, x_ref, out_ref, pair_recv, part, chip_recv, sendbuf, half, other,
                     p_send, p_recv, c_send, c_recv, g_send, g_recv, h_send, h_recv):
    total = _two_level_sum(nchip, x_ref, pair_recv, part, chip_recv, p_send, p_recv, c_send, c_recv)
    orb, core, partner, chip = _place()
    rounded = total.astype(sendbuf.dtype)
    sendbuf[...] = rounded
    half[chip] = rounded
    sends = []
    for j in range(1, nchip):
        dst = lax.rem(chip + j, nchip)
        cp = _remote(sendbuf, half.at[chip], g_send.at[j], g_recv.at[chip], 2 * dst + core, orb)
        cp.start()
        sends.append(cp)
    for j in range(1, nchip):
        src = lax.rem(chip + nchip - j, nchip)
        _remote(sendbuf, half.at[src], g_send.at[j], g_recv.at[src], 2 * src + core, orb).wait_recv()
    for cp in sends:
        cp.wait_send()
    cp = _remote(half, other, h_send.at[0], h_recv.at[0], partner, orb)
    cp.start()
    cp.wait_recv()
    for i in range(nchip):
        out_ref[i, core] = half[i]
        out_ref[i, 1 - core] = other[i]
    cp.wait_send()


def _two_level_scratch(nchip, rows, cols):
    return [
        pltpu.VMEM((nchip, rows, cols), jnp.float32),
        pltpu.VMEM((nchip, rows, cols), jnp.float32),
        pltpu.VMEM((nchip, rows, cols), jnp.float32),
    ]


def allreduce_to_bf16(partial, n):
    rows, cols = partial.shape
    nchip = n // 2
    chunk = rows // n
    x = partial.reshape(nchip, 2, chunk, cols)
    out = pl.pallas_call(
        functools.partial(allreduce_kernel, nchip),
        out_shape=jax.ShapeDtypeStruct((nchip, 2, chunk, cols), jnp.bfloat16),
        in_specs=[pl.BlockSpec(memory_space=pltpu.VMEM)],
        out_specs=pl.BlockSpec(memory_space=pltpu.VMEM),
        scratch_shapes=_two_level_scratch(nchip, chunk, cols) + [
            pltpu.VMEM((chunk, cols), jnp.bfloat16),
            pltpu.VMEM((nchip, chunk, cols), jnp.bfloat16),
            pltpu.VMEM((nchip, chunk, cols), jnp.bfloat16),
        ] + [pltpu.SemaphoreType.DMA((nchip,))] * 6 + [pltpu.SemaphoreType.DMA((1,))] * 2,
        compiler_params=pltpu.CompilerParams(collective_id=0, has_side_effects=True),
    )(x)
    return out.reshape(rows, cols)


def dipole_kernel(nchip, chunk, count, x_ref, out_ref, pair_recv, part, chip_recv,
                  p_send, p_recv, c_send, c_recv):
    total = _two_level_sum(nchip, x_ref, pair_recv, part, chip_recv, p_send, p_recv, c_send, c_recv)
    squares = total[chunk:chunk + 1, :]
    col_norm = 1.0 / jnp.sqrt(squares / count + 1e-06)
    out_ref[...] = (total[:chunk, :] * col_norm).astype(out_ref.dtype)


def dipole_scatter(partial, squares, n, count):
    rows, cols = partial.shape
    nchip = n // 2
    chunk = rows // n
    x = jnp.concatenate(
        [
            partial.reshape(nchip, 2, chunk, cols),
            jnp.broadcast_to(squares[None, None, None, :], (nchip, 2, 8, cols)),
        ],
        axis=2,
    )
    return pl.pallas_call(
        functools.partial(dipole_kernel, nchip, chunk, count),
        out_shape=jax.ShapeDtypeStruct((chunk, cols), jnp.bfloat16),
        in_specs=[pl.BlockSpec(memory_space=pltpu.VMEM)],
        out_specs=pl.BlockSpec(memory_space=pltpu.VMEM),
        scratch_shapes=_two_level_scratch(nchip, chunk + 8, cols)
        + [pltpu.SemaphoreType.DMA((nchip,))] * 4,
        compiler_params=pltpu.CompilerParams(collective_id=1, has_side_effects=True),
    )(x)


def on_device(cont_orbitals, target_orbitals, margin_blocks, dipole_blocks, band_offsets):
    n = lax.axis_size("basis")
    count = band_offsets.shape[0] * BK * n
    cont_padded = padded_2(cont_orbitals, (("basis", 0),), 2 * BK)
    margin_cont = band_local(margin_blocks, band_offsets, cont_padded)
    partial_proj = lax.dot_general(
        target_orbitals, margin_cont, (((0,), (0,)), ((), ())), preferred_element_type=jnp.float32
    )
    projection_b = allreduce_to_bf16(partial_proj, n)
    removed = jnp.dot(target_orbitals, projection_b, preferred_element_type=jnp.float32)
    cont_orth = (cont_orbitals.astype(jnp.float32) - removed).astype(jnp.bfloat16)
    squares = jnp.sum(jnp.square(cont_orth.astype(jnp.float32)), axis=0)
    orth_padded = padded_2(cont_orth, (("basis", 0),), 2 * BK)
    dipole_cont = band_local(dipole_blocks, band_offsets, orth_padded)
    partial_dip = lax.dot_general(
        target_orbitals,
        dipole_cont,
        (((0,), (0,)), ((), ())),
        preferred_element_type=jnp.float32,
    )
    dipole_mo = dipole_scatter(partial_dip, squares, n, count)
    return (cont_orth, dipole_mo)


def solution(mesh):
    return jax.shard_map(
        on_device,
        mesh=mesh,
        in_specs=(
            P("basis", "orb"),
            P("basis", None),
            P("basis", None, None, None),
            P("basis", None, None, None),
            P("basis", None),
        ),
        out_specs=(P("basis", "orb"), P("basis", "orb")),
        check_vma=False,
    )
```

```python
import functools

import jax
import jax.numpy as jnp
from jax import lax
from jax.experimental import pallas as pl
from jax.experimental.pallas import tpu as pltpu
from jax.sharding import PartitionSpec as P

BK = 256
KB = 4
MESH = pl.DeviceIdType.MESH


def padded_2(block, sides, width):
    for axis, dim in sides:
        count = lax.axis_size(axis)
        forward = [(i, i + 1) for i in range(count - 1)]
        backward = [(target, source) for source, target in forward]
        low = lax.ppermute(
            lax.slice_in_dim(block, block.shape[dim] - width, None, axis=dim), axis, forward
        )
        high = lax.ppermute(lax.slice_in_dim(block, 0, width, axis=dim), axis, backward)
        block = jnp.concatenate([low, block, high], axis=dim)
    return block


def band_kernel(rows_per_step, off_ref, blk_ref, field_ref, out_ref):
    g = pl.program_id(0)
    for r in range(rows_per_step):
        b = g * rows_per_step + r
        acc = None
        for k in range(KB):
            start = pl.multiple_of((b + 2 + off_ref[b, k]) * BK, BK)
            term = jnp.dot(
                blk_ref[r, k], field_ref[pl.ds(start, BK), :], preferred_element_type=jnp.float32
            )
            acc = term if acc is None else acc + term
        out_ref[pl.ds(r * BK, BK), :] = acc.astype(out_ref.dtype)


def band_local(blocks, offsets, padded):
    nblk = blocks.shape[0]
    rows, width = padded.shape
    per = 8 if nblk % 8 == 0 else 1
    return pl.pallas_call(
        functools.partial(band_kernel, per),
        out_shape=jax.ShapeDtypeStruct((nblk * BK, width), jnp.bfloat16),
        grid_spec=pltpu.PrefetchScalarGridSpec(
            num_scalar_prefetch=1,
            grid=(nblk // per,),
            in_specs=[
                pl.BlockSpec((per, KB, BK, BK), lambda g, off: (g, 0, 0, 0)),
                pl.BlockSpec((rows, width), lambda g, off: (0, 0)),
            ],
            out_specs=pl.BlockSpec((per * BK, width), lambda g, off: (g, 0)),
        ),
        cost_estimate=pl.CostEstimate(
            flops=2 * nblk * KB * BK * BK * width,
            bytes_accessed=blocks.size * 2 + padded.size * 2 + nblk * BK * width * 2,
            transcendentals=0,
        ),
        compiler_params=pltpu.CompilerParams(vmem_limit_bytes=24 * 1024 * 1024),
    )(offsets, blocks, padded)


def _place():
    me = lax.axis_index("basis")
    orb = lax.axis_index("orb")
    core = lax.rem(me, 2)
    partner = me + 1 - 2 * core
    chip = lax.div(me, 2)
    return orb, core, partner, chip


def _barrier_group(nchip, orb, core, partner, chip):
    barrier = pltpu.get_barrier_semaphore()
    pl.semaphore_signal(barrier, inc=1, device_id=(partner, orb), device_id_type=MESH)
    for j in range(1, nchip):
        peer = 2 * lax.rem(chip + j, nchip) + core
        pl.semaphore_signal(barrier, inc=1, device_id=(peer, orb), device_id_type=MESH)
    pl.semaphore_wait(barrier, nchip)


def _remote(src, dst, ssem, rsem, device, orb):
    return pltpu.make_async_remote_copy(
        src_ref=src, dst_ref=dst, send_sem=ssem, recv_sem=rsem,
        device_id=(device, orb), device_id_type=MESH,
    )


def _two_level_sum(nchip, x_ref, pair_recv, part, chip_recv, p_send, p_recv, c_send, c_recv):
    orb, core, partner, chip = _place()
    _barrier_group(nchip, orb, core, partner, chip)
    pair = []
    for i in range(nchip):
        cp = _remote(x_ref.at[i, 1 - core], pair_recv.at[i], p_send.at[i], p_recv.at[i], partner, orb)
        cp.start()
        pair.append(cp)
    for i in range(nchip):
        pair[i].wait_recv()
        part[i] = x_ref[i, core] + pair_recv[i]
    sends = []
    for j in range(1, nchip):
        dst = lax.rem(chip + j, nchip)
        cp = _remote(part.at[dst], chip_recv.at[chip], c_send.at[j], c_recv.at[chip], 2 * dst + core, orb)
        cp.start()
        sends.append(cp)
    total = part[chip]
    for j in range(1, nchip):
        src = lax.rem(chip + nchip - j, nchip)
        _remote(part.at[src], chip_recv.at[src], c_send.at[j], c_recv.at[src], 2 * src + core, orb).wait_recv()
        total = total + chip_recv[src]
    for cp in pair + sends:
        cp.wait_send()
    return total


def allreduce_kernel(nchip, x_ref, out_ref, pair_recv, part, chip_recv, sendbuf, half, other,
                     p_send, p_recv, c_send, c_recv, g_send, g_recv, h_send, h_recv):
    total = _two_level_sum(nchip, x_ref, pair_recv, part, chip_recv, p_send, p_recv, c_send, c_recv)
    orb, core, partner, chip = _place()
    rounded = total.astype(sendbuf.dtype)
    sendbuf[...] = rounded
    half[chip] = rounded
    sends = []
    for j in range(1, nchip):
        dst = lax.rem(chip + j, nchip)
        cp = _remote(sendbuf, half.at[chip], g_send.at[j], g_recv.at[chip], 2 * dst + core, orb)
        cp.start()
        sends.append(cp)
    for j in range(1, nchip):
        src = lax.rem(chip + nchip - j, nchip)
        _remote(sendbuf, half.at[src], g_send.at[j], g_recv.at[src], 2 * src + core, orb).wait_recv()
    for cp in sends:
        cp.wait_send()
    cp = _remote(half, other, h_send.at[0], h_recv.at[0], partner, orb)
    cp.start()
    cp.wait_recv()
    for i in range(nchip):
        out_ref[i, core] = half[i]
        out_ref[i, 1 - core] = other[i]
    cp.wait_send()


def _two_level_scratch(nchip, rows, cols):
    return [
        pltpu.VMEM((nchip, rows, cols), jnp.float32),
        pltpu.VMEM((nchip, rows, cols), jnp.float32),
        pltpu.VMEM((nchip, rows, cols), jnp.float32),
    ]


def allreduce_to_bf16(partial, n):
    rows, cols = partial.shape
    nchip = n // 2
    chunk = rows // n
    x = partial.reshape(nchip, 2, chunk, cols)
    out = pl.pallas_call(
        functools.partial(allreduce_kernel, nchip),
        out_shape=jax.ShapeDtypeStruct((nchip, 2, chunk, cols), jnp.bfloat16),
        in_specs=[pl.BlockSpec(memory_space=pltpu.VMEM)],
        out_specs=pl.BlockSpec(memory_space=pltpu.VMEM),
        scratch_shapes=_two_level_scratch(nchip, chunk, cols) + [
            pltpu.VMEM((chunk, cols), jnp.bfloat16),
            pltpu.VMEM((nchip, chunk, cols), jnp.bfloat16),
            pltpu.VMEM((nchip, chunk, cols), jnp.bfloat16),
        ] + [pltpu.SemaphoreType.DMA((nchip,))] * 6 + [pltpu.SemaphoreType.DMA((1,))] * 2,
        compiler_params=pltpu.CompilerParams(collective_id=0, has_side_effects=True),
    )(x)
    return out.reshape(rows, cols)


def dipole_kernel(nchip, chunk, count, x_ref, out_ref, pair_recv, part, chip_recv,
                  p_send, p_recv, c_send, c_recv):
    total = _two_level_sum(nchip, x_ref, pair_recv, part, chip_recv, p_send, p_recv, c_send, c_recv)
    squares = total[chunk:chunk + 1, :]
    col_norm = 1.0 / jnp.sqrt(squares / count + 1e-06)
    out_ref[...] = (total[:chunk, :] * col_norm).astype(out_ref.dtype)


def dipole_scatter(partial, squares, n, count):
    rows, cols = partial.shape
    nchip = n // 2
    chunk = rows // n
    x = jnp.concatenate(
        [
            partial.reshape(nchip, 2, chunk, cols),
            jnp.broadcast_to(squares[None, None, None, :], (nchip, 2, 8, cols)),
        ],
        axis=2,
    )
    return pl.pallas_call(
        functools.partial(dipole_kernel, nchip, chunk, count),
        out_shape=jax.ShapeDtypeStruct((chunk, cols), jnp.bfloat16),
        in_specs=[pl.BlockSpec(memory_space=pltpu.VMEM)],
        out_specs=pl.BlockSpec(memory_space=pltpu.VMEM),
        scratch_shapes=_two_level_scratch(nchip, chunk + 8, cols)
        + [pltpu.SemaphoreType.DMA((nchip,))] * 4,
        compiler_params=pltpu.CompilerParams(collective_id=1, has_side_effects=True),
    )(x)


def on_device(cont_orbitals, target_orbitals, margin_blocks, dipole_blocks, band_offsets):
    n = lax.axis_size("basis")
    count = band_offsets.shape[0] * BK * n
    cont_padded = padded_2(cont_orbitals, (("basis", 0),), 2 * BK)
    margin_cont = band_local(margin_blocks, band_offsets, cont_padded)
    partial_proj = lax.dot_general(
        target_orbitals, margin_cont, (((0,), (0,)), ((), ())), preferred_element_type=jnp.float32
    )
    projection_b = allreduce_to_bf16(partial_proj, n)
    removed = jnp.dot(target_orbitals, projection_b, preferred_element_type=jnp.float32)
    cont_orth = (cont_orbitals.astype(jnp.float32) - removed).astype(jnp.bfloat16)
    squares = jnp.sum(jnp.square(cont_orth.astype(jnp.float32)), axis=0)
    orth_padded = padded_2(cont_orth, (("basis", 0),), 2 * BK)
    dipole_cont = band_local(dipole_blocks, band_offsets, orth_padded)
    partial_dip = lax.dot_general(
        target_orbitals,
        dipole_cont,
        (((0,), (0,)), ((), ())),
        preferred_element_type=jnp.float32,
    )
    dipole_mo = dipole_scatter(partial_dip, squares, n, count)
    return (cont_orth, dipole_mo)


def solution(mesh):
    return jax.shard_map(
        on_device,
        mesh=mesh,
        in_specs=(
            P("basis", "orb"),
            P("basis", None),
            P("basis", None, None, None),
            P("basis", None, None, None),
            P("basis", None),
        ),
        out_specs=(P("basis", "orb"), P("basis", "orb")),
        check_vma=False,
    )
```

```python
import functools

import jax
import jax.numpy as jnp
from jax import lax
from jax.experimental import pallas as pl
from jax.experimental.pallas import tpu as pltpu
from jax.sharding import PartitionSpec as P

BK = 256
KB = 4
MESH = pl.DeviceIdType.MESH


def padded_2(block, sides, width):
    for axis, dim in sides:
        count = lax.axis_size(axis)
        forward = [(i, i + 1) for i in range(count - 1)]
        backward = [(target, source) for source, target in forward]
        low = lax.ppermute(
            lax.slice_in_dim(block, block.shape[dim] - width, None, axis=dim), axis, forward
        )
        high = lax.ppermute(lax.slice_in_dim(block, 0, width, axis=dim), axis, backward)
        block = jnp.concatenate([low, block, high], axis=dim)
    return block


def band_kernel(rows_per_step, off_ref, blk_ref, field_ref, out_ref):
    g = pl.program_id(0)
    for r in range(rows_per_step):
        b = g * rows_per_step + r
        acc = None
        for k in range(KB):
            start = pl.multiple_of((b + 2 + off_ref[b, k]) * BK, BK)
            term = jnp.dot(
                blk_ref[r, k], field_ref[pl.ds(start, BK), :], preferred_element_type=jnp.float32
            )
            acc = term if acc is None else acc + term
        out_ref[pl.ds(r * BK, BK), :] = acc.astype(out_ref.dtype)


def band_local(blocks, offsets, padded):
    nblk = blocks.shape[0]
    rows, width = padded.shape
    per = 8 if nblk % 8 == 0 else 1
    return pl.pallas_call(
        functools.partial(band_kernel, per),
        out_shape=jax.ShapeDtypeStruct((nblk * BK, width), jnp.bfloat16),
        grid_spec=pltpu.PrefetchScalarGridSpec(
            num_scalar_prefetch=1,
            grid=(nblk // per,),
            in_specs=[
                pl.BlockSpec((per, KB, BK, BK), lambda g, off: (g, 0, 0, 0)),
                pl.BlockSpec((rows, width), lambda g, off: (0, 0)),
            ],
            out_specs=pl.BlockSpec((per * BK, width), lambda g, off: (g, 0)),
        ),
        cost_estimate=pl.CostEstimate(
            flops=2 * nblk * KB * BK * BK * width,
            bytes_accessed=blocks.size * 2 + padded.size * 2 + nblk * BK * width * 2,
            transcendentals=0,
        ),
        compiler_params=pltpu.CompilerParams(vmem_limit_bytes=24 * 1024 * 1024),
    )(offsets, blocks, padded)


def _place():
    me = lax.axis_index("basis")
    orb = lax.axis_index("orb")
    core = lax.rem(me, 2)
    partner = me + 1 - 2 * core
    chip = lax.div(me, 2)
    return orb, core, partner, chip


def _barrier_group(nchip, orb, core, partner, chip):
    barrier = pltpu.get_barrier_semaphore()
    pl.semaphore_signal(barrier, inc=1, device_id=(partner, orb), device_id_type=MESH)
    for j in range(1, nchip):
        peer = 2 * lax.rem(chip + j, nchip) + core
        pl.semaphore_signal(barrier, inc=1, device_id=(peer, orb), device_id_type=MESH)
    pl.semaphore_wait(barrier, nchip)


def _remote(src, dst, ssem, rsem, device, orb):
    return pltpu.make_async_remote_copy(
        src_ref=src, dst_ref=dst, send_sem=ssem, recv_sem=rsem,
        device_id=(device, orb), device_id_type=MESH,
    )


def _two_level_sum(nchip, x_ref, pair_recv, part, chip_recv, p_send, p_recv, c_send, c_recv):
    orb, core, partner, chip = _place()
    _barrier_group(nchip, orb, core, partner, chip)
    pair = []
    for i in range(nchip):
        cp = _remote(x_ref.at[i, 1 - core], pair_recv.at[i], p_send.at[i], p_recv.at[i], partner, orb)
        cp.start()
        pair.append(cp)
    for i in range(nchip):
        pair[i].wait_recv()
        part[i] = x_ref[i, core] + pair_recv[i]
    sends = []
    for j in range(1, nchip):
        dst = lax.rem(chip + j, nchip)
        cp = _remote(part.at[dst], chip_recv.at[chip], c_send.at[j], c_recv.at[chip], 2 * dst + core, orb)
        cp.start()
        sends.append(cp)
    total = part[chip]
    for j in range(1, nchip):
        src = lax.rem(chip + nchip - j, nchip)
        _remote(part.at[src], chip_recv.at[src], c_send.at[j], c_recv.at[src], 2 * src + core, orb).wait_recv()
        total = total + chip_recv[src]
    for cp in pair + sends:
        cp.wait_send()
    return total


def allreduce_kernel(nchip, x_ref, out_ref, pair_recv, part, chip_recv, sendbuf, half, other,
                     p_send, p_recv, c_send, c_recv, g_send, g_recv, h_send, h_recv):
    total = _two_level_sum(nchip, x_ref, pair_recv, part, chip_recv, p_send, p_recv, c_send, c_recv)
    orb, core, partner, chip = _place()
    rounded = total.astype(sendbuf.dtype)
    sendbuf[...] = rounded
    half[chip] = rounded
    sends = []
    for j in range(1, nchip):
        dst = lax.rem(chip + j, nchip)
        cp = _remote(sendbuf, half.at[chip], g_send.at[j], g_recv.at[chip], 2 * dst + core, orb)
        cp.start()
        sends.append(cp)
    for j in range(1, nchip):
        src = lax.rem(chip + nchip - j, nchip)
        _remote(sendbuf, half.at[src], g_send.at[j], g_recv.at[src], 2 * src + core, orb).wait_recv()
    for cp in sends:
        cp.wait_send()
    cp = _remote(half, other, h_send.at[0], h_recv.at[0], partner, orb)
    cp.start()
    cp.wait_recv()
    for i in range(nchip):
        out_ref[i, core] = half[i]
        out_ref[i, 1 - core] = other[i]
    cp.wait_send()


def _two_level_scratch(nchip, rows, cols):
    return [
        pltpu.VMEM((nchip, rows, cols), jnp.float32),
        pltpu.VMEM((nchip, rows, cols), jnp.float32),
        pltpu.VMEM((nchip, rows, cols), jnp.float32),
    ]


def allreduce_to_bf16(partial, n):
    rows, cols = partial.shape
    nchip = n // 2
    chunk = rows // n
    x = partial.reshape(nchip, 2, chunk, cols)
    out = pl.pallas_call(
        functools.partial(allreduce_kernel, nchip),
        out_shape=jax.ShapeDtypeStruct((nchip, 2, chunk, cols), jnp.bfloat16),
        in_specs=[pl.BlockSpec(memory_space=pltpu.VMEM)],
        out_specs=pl.BlockSpec(memory_space=pltpu.VMEM),
        scratch_shapes=_two_level_scratch(nchip, chunk, cols) + [
            pltpu.VMEM((chunk, cols), jnp.bfloat16),
            pltpu.VMEM((nchip, chunk, cols), jnp.bfloat16),
            pltpu.VMEM((nchip, chunk, cols), jnp.bfloat16),
        ] + [pltpu.SemaphoreType.DMA((nchip,))] * 6 + [pltpu.SemaphoreType.DMA((1,))] * 2,
        compiler_params=pltpu.CompilerParams(
            collective_id=0, has_side_effects=True, vmem_limit_bytes=12 * 1024 * 1024
        ),
        cost_estimate=pl.CostEstimate(flops=0, bytes_accessed=64 * x.size, transcendentals=0),
    )(x)
    return out.reshape(rows, cols)


def dipole_kernel(nchip, chunk, count, x_ref, out_ref, pair_recv, part, chip_recv,
                  p_send, p_recv, c_send, c_recv):
    total = _two_level_sum(nchip, x_ref, pair_recv, part, chip_recv, p_send, p_recv, c_send, c_recv)
    squares = total[chunk:chunk + 1, :]
    col_norm = 1.0 / jnp.sqrt(squares / count + 1e-06)
    out_ref[...] = (total[:chunk, :] * col_norm).astype(out_ref.dtype)


def dipole_scatter(partial, squares, n, count):
    rows, cols = partial.shape
    nchip = n // 2
    chunk = rows // n
    x = jnp.concatenate(
        [
            partial.reshape(nchip, 2, chunk, cols),
            jnp.broadcast_to(squares[None, None, None, :], (nchip, 2, 8, cols)),
        ],
        axis=2,
    )
    return pl.pallas_call(
        functools.partial(dipole_kernel, nchip, chunk, count),
        out_shape=jax.ShapeDtypeStruct((chunk, cols), jnp.bfloat16),
        in_specs=[pl.BlockSpec(memory_space=pltpu.VMEM)],
        out_specs=pl.BlockSpec(memory_space=pltpu.VMEM),
        scratch_shapes=_two_level_scratch(nchip, chunk + 8, cols)
        + [pltpu.SemaphoreType.DMA((nchip,))] * 4,
        compiler_params=pltpu.CompilerParams(
            collective_id=1, has_side_effects=True, vmem_limit_bytes=12 * 1024 * 1024
        ),
        cost_estimate=pl.CostEstimate(flops=0, bytes_accessed=32 * x.size, transcendentals=0),
    )(x)


def on_device(cont_orbitals, target_orbitals, margin_blocks, dipole_blocks, band_offsets):
    n = lax.axis_size("basis")
    count = band_offsets.shape[0] * BK * n
    cont_padded = padded_2(cont_orbitals, (("basis", 0),), 2 * BK)
    margin_cont = band_local(margin_blocks, band_offsets, cont_padded)
    partial_proj = lax.dot_general(
        target_orbitals, margin_cont, (((0,), (0,)), ((), ())), preferred_element_type=jnp.float32
    )
    projection_b = allreduce_to_bf16(partial_proj, n)
    removed = jnp.dot(target_orbitals, projection_b, preferred_element_type=jnp.float32)
    cont_orth = (cont_orbitals.astype(jnp.float32) - removed).astype(jnp.bfloat16)
    squares = jnp.sum(jnp.square(cont_orth.astype(jnp.float32)), axis=0)
    orth_padded = padded_2(cont_orth, (("basis", 0),), 2 * BK)
    dipole_cont = band_local(dipole_blocks, band_offsets, orth_padded)
    partial_dip = lax.dot_general(
        target_orbitals,
        dipole_cont,
        (((0,), (0,)), ((), ())),
        preferred_element_type=jnp.float32,
    )
    dipole_mo = dipole_scatter(partial_dip, squares, n, count)
    return (cont_orth, dipole_mo)


def solution(mesh):
    return jax.shard_map(
        on_device,
        mesh=mesh,
        in_specs=(
            P("basis", "orb"),
            P("basis", None),
            P("basis", None, None, None),
            P("basis", None, None, None),
            P("basis", None),
        ),
        out_specs=(P("basis", "orb"), P("basis", "orb")),
        check_vma=False,
    )
```

```python
import functools

import jax
import jax.numpy as jnp
from jax import lax
from jax.experimental import pallas as pl
from jax.experimental.pallas import tpu as pltpu
from jax.sharding import PartitionSpec as P

BK = 256
KB = 4
MESH = pl.DeviceIdType.MESH


def padded_2(block, sides, width):
    for axis, dim in sides:
        count = lax.axis_size(axis)
        forward = [(i, i + 1) for i in range(count - 1)]
        backward = [(target, source) for source, target in forward]
        low = lax.ppermute(
            lax.slice_in_dim(block, block.shape[dim] - width, None, axis=dim), axis, forward
        )
        high = lax.ppermute(lax.slice_in_dim(block, 0, width, axis=dim), axis, backward)
        block = jnp.concatenate([low, block, high], axis=dim)
    return block


def band_kernel(n, off_ref, blk_hbm, field_ref, out_ref, blk, low, high, blk_sem, send_sem, recv_sem):
    nblk = blk.shape[0]
    me = lax.axis_index("basis")
    orb = lax.axis_index("orb")
    has_low = me > 0
    has_high = me < n - 1
    loads = []
    for b in range(nblk):
        cp = pltpu.make_async_copy(blk_hbm.at[b], blk.at[b], blk_sem.at[b])
        cp.start()
        loads.append(cp)
    barrier = pltpu.get_barrier_semaphore()

    @pl.when(has_low)
    def _():
        pl.semaphore_signal(barrier, inc=1, device_id=(me - 1, orb), device_id_type=MESH)

    @pl.when(has_high)
    def _():
        pl.semaphore_signal(barrier, inc=1, device_id=(me + 1, orb), device_id_type=MESH)

    pl.semaphore_wait(barrier, has_low.astype(jnp.int32) + has_high.astype(jnp.int32))
    to_low = pltpu.make_async_remote_copy(
        src_ref=field_ref.at[pl.ds(0, 2)], dst_ref=high.at[pl.ds(4, 2)],
        send_sem=send_sem.at[0], recv_sem=recv_sem.at[0],
        device_id=(jnp.maximum(me - 1, 0), orb), device_id_type=MESH,
    )
    to_high = pltpu.make_async_remote_copy(
        src_ref=field_ref.at[pl.ds(nblk - 2, 2)], dst_ref=low.at[pl.ds(0, 2)],
        send_sem=send_sem.at[1], recv_sem=recv_sem.at[1],
        device_id=(jnp.minimum(me + 1, n - 1), orb), device_id_type=MESH,
    )

    @pl.when(has_low)
    def _():
        to_low.start()

    @pl.when(has_high)
    def _():
        to_high.start()

    for i in range(4):
        low[2 + i] = field_ref[i]
        high[i] = field_ref[nblk - 4 + i]

    def row(b, src, base):
        loads[b].wait()
        acc = None
        for k in range(KB):
            term = jnp.dot(blk[b, k], src[b + base + off_ref[b, k]], preferred_element_type=jnp.float32)
            acc = term if acc is None else acc + term
        out_ref[b] = acc.astype(out_ref.dtype)

    for b in range(2, nblk - 2):
        row(b, field_ref, 0)

    @pl.when(has_high)
    def _():
        to_low.wait_recv()

    @pl.when(jnp.logical_not(has_high))
    def _():
        high[4] = jnp.zeros(field_ref.shape[1:], field_ref.dtype)
        high[5] = jnp.zeros(field_ref.shape[1:], field_ref.dtype)

    @pl.when(has_low)
    def _():
        to_high.wait_recv()

    @pl.when(jnp.logical_not(has_low))
    def _():
        low[0] = jnp.zeros(field_ref.shape[1:], field_ref.dtype)
        low[1] = jnp.zeros(field_ref.shape[1:], field_ref.dtype)

    row(0, low, 2)
    row(1, low, 2)
    row(nblk - 2, high, 4 - nblk)
    row(nblk - 1, high, 4 - nblk)

    @pl.when(has_low)
    def _():
        to_low.wait_send()

    @pl.when(has_high)
    def _():
        to_high.wait_send()


def band_local(blocks, offsets, field, collective_id):
    nblk = blocks.shape[0]
    rows, width = field.shape
    n = lax.axis_size("basis")
    return pl.pallas_call(
        functools.partial(band_kernel, n),
        out_shape=jax.ShapeDtypeStruct((nblk, BK, width), jnp.bfloat16),
        in_specs=[
            pl.BlockSpec(memory_space=pltpu.SMEM),
            pl.BlockSpec(memory_space=pl.ANY),
            pl.BlockSpec(memory_space=pltpu.VMEM),
        ],
        out_specs=pl.BlockSpec(memory_space=pltpu.VMEM),
        scratch_shapes=[
            pltpu.VMEM(blocks.shape, blocks.dtype),
            pltpu.VMEM((6, BK, width), field.dtype),
            pltpu.VMEM((6, BK, width), field.dtype),
            pltpu.SemaphoreType.DMA((nblk,)),
            pltpu.SemaphoreType.DMA((2,)),
            pltpu.SemaphoreType.DMA((2,)),
        ],
        cost_estimate=pl.CostEstimate(
            flops=2 * nblk * KB * BK * BK * width,
            bytes_accessed=blocks.size * 2 + 2 * field.size * 2,
            transcendentals=0,
        ),
        compiler_params=pltpu.CompilerParams(
            collective_id=collective_id, has_side_effects=True, vmem_limit_bytes=24 * 1024 * 1024
        ),
    )(offsets, blocks, field.reshape(nblk, BK, width)).reshape(rows, width)


def _place():
    me = lax.axis_index("basis")
    orb = lax.axis_index("orb")
    core = lax.rem(me, 2)
    partner = me + 1 - 2 * core
    chip = lax.div(me, 2)
    return orb, core, partner, chip


def _barrier_group(nchip, orb, core, partner, chip):
    barrier = pltpu.get_barrier_semaphore()
    pl.semaphore_signal(barrier, inc=1, device_id=(partner, orb), device_id_type=MESH)
    for j in range(1, nchip):
        peer = 2 * lax.rem(chip + j, nchip) + core
        pl.semaphore_signal(barrier, inc=1, device_id=(peer, orb), device_id_type=MESH)
    pl.semaphore_wait(barrier, nchip)


def _remote(src, dst, ssem, rsem, device, orb):
    return pltpu.make_async_remote_copy(
        src_ref=src, dst_ref=dst, send_sem=ssem, recv_sem=rsem,
        device_id=(device, orb), device_id_type=MESH,
    )


def _two_level_sum(nchip, x_ref, pair_recv, part, chip_recv, p_send, p_recv, c_send, c_recv):
    orb, core, partner, chip = _place()
    _barrier_group(nchip, orb, core, partner, chip)
    pair = []
    for i in range(nchip):
        cp = _remote(x_ref.at[i, 1 - core], pair_recv.at[i], p_send.at[i], p_recv.at[i], partner, orb)
        cp.start()
        pair.append(cp)
    for i in range(nchip):
        pair[i].wait_recv()
        part[i] = x_ref[i, core] + pair_recv[i]
    sends = []
    for j in range(1, nchip):
        dst = lax.rem(chip + j, nchip)
        cp = _remote(part.at[dst], chip_recv.at[chip], c_send.at[j], c_recv.at[chip], 2 * dst + core, orb)
        cp.start()
        sends.append(cp)
    total = part[chip]
    for j in range(1, nchip):
        src = lax.rem(chip + nchip - j, nchip)
        _remote(part.at[src], chip_recv.at[src], c_send.at[j], c_recv.at[src], 2 * src + core, orb).wait_recv()
        total = total + chip_recv[src]
    for cp in pair + sends:
        cp.wait_send()
    return total


def allreduce_kernel(nchip, x_ref, out_ref, pair_recv, part, chip_recv, sendbuf, half, other,
                     p_send, p_recv, c_send, c_recv, g_send, g_recv, h_send, h_recv):
    total = _two_level_sum(nchip, x_ref, pair_recv, part, chip_recv, p_send, p_recv, c_send, c_recv)
    orb, core, partner, chip = _place()
    rounded = total.astype(sendbuf.dtype)
    sendbuf[...] = rounded
    half[chip] = rounded
    sends = []
    for j in range(1, nchip):
        dst = lax.rem(chip + j, nchip)
        cp = _remote(sendbuf, half.at[chip], g_send.at[j], g_recv.at[chip], 2 * dst + core, orb)
        cp.start()
        sends.append(cp)
    for j in range(1, nchip):
        src = lax.rem(chip + nchip - j, nchip)
        _remote(sendbuf, half.at[src], g_send.at[j], g_recv.at[src], 2 * src + core, orb).wait_recv()
    for cp in sends:
        cp.wait_send()
    cp = _remote(half, other, h_send.at[0], h_recv.at[0], partner, orb)
    cp.start()
    cp.wait_recv()
    for i in range(nchip):
        out_ref[i, core] = half[i]
        out_ref[i, 1 - core] = other[i]
    cp.wait_send()


def _two_level_scratch(nchip, rows, cols):
    return [
        pltpu.VMEM((nchip, rows, cols), jnp.float32),
        pltpu.VMEM((nchip, rows, cols), jnp.float32),
        pltpu.VMEM((nchip, rows, cols), jnp.float32),
    ]


def allreduce_to_bf16(partial, n):
    rows, cols = partial.shape
    nchip = n // 2
    chunk = rows // n
    x = partial.reshape(nchip, 2, chunk, cols)
    out = pl.pallas_call(
        functools.partial(allreduce_kernel, nchip),
        out_shape=jax.ShapeDtypeStruct((nchip, 2, chunk, cols), jnp.bfloat16),
        in_specs=[pl.BlockSpec(memory_space=pltpu.VMEM)],
        out_specs=pl.BlockSpec(memory_space=pltpu.VMEM),
        scratch_shapes=_two_level_scratch(nchip, chunk, cols) + [
            pltpu.VMEM((chunk, cols), jnp.bfloat16),
            pltpu.VMEM((nchip, chunk, cols), jnp.bfloat16),
            pltpu.VMEM((nchip, chunk, cols), jnp.bfloat16),
        ] + [pltpu.SemaphoreType.DMA((nchip,))] * 6 + [pltpu.SemaphoreType.DMA((1,))] * 2,
        compiler_params=pltpu.CompilerParams(
            collective_id=0, has_side_effects=True, vmem_limit_bytes=12 * 1024 * 1024
        ),
        cost_estimate=pl.CostEstimate(flops=0, bytes_accessed=64 * x.size, transcendentals=0),
    )(x)
    return out.reshape(rows, cols)


def dipole_kernel(nchip, chunk, count, x_ref, out_ref, pair_recv, part, chip_recv,
                  p_send, p_recv, c_send, c_recv):
    total = _two_level_sum(nchip, x_ref, pair_recv, part, chip_recv, p_send, p_recv, c_send, c_recv)
    squares = total[chunk:chunk + 1, :]
    col_norm = 1.0 / jnp.sqrt(squares / count + 1e-06)
    out_ref[...] = (total[:chunk, :] * col_norm).astype(out_ref.dtype)


def dipole_scatter(partial, squares, n, count):
    rows, cols = partial.shape
    nchip = n // 2
    chunk = rows // n
    x = jnp.concatenate(
        [
            partial.reshape(nchip, 2, chunk, cols),
            jnp.broadcast_to(squares[None, None, None, :], (nchip, 2, 8, cols)),
        ],
        axis=2,
    )
    return pl.pallas_call(
        functools.partial(dipole_kernel, nchip, chunk, count),
        out_shape=jax.ShapeDtypeStruct((chunk, cols), jnp.bfloat16),
        in_specs=[pl.BlockSpec(memory_space=pltpu.VMEM)],
        out_specs=pl.BlockSpec(memory_space=pltpu.VMEM),
        scratch_shapes=_two_level_scratch(nchip, chunk + 8, cols)
        + [pltpu.SemaphoreType.DMA((nchip,))] * 4,
        compiler_params=pltpu.CompilerParams(
            collective_id=1, has_side_effects=True, vmem_limit_bytes=12 * 1024 * 1024
        ),
        cost_estimate=pl.CostEstimate(flops=0, bytes_accessed=32 * x.size, transcendentals=0),
    )(x)


def on_device(cont_orbitals, target_orbitals, margin_blocks, dipole_blocks, band_offsets):
    n = lax.axis_size("basis")
    count = band_offsets.shape[0] * BK * n
    margin_cont = band_local(margin_blocks, band_offsets, cont_orbitals, 2)
    partial_proj = lax.dot_general(
        target_orbitals, margin_cont, (((0,), (0,)), ((), ())), preferred_element_type=jnp.float32
    )
    projection_b = allreduce_to_bf16(partial_proj, n)
    removed = jnp.dot(target_orbitals, projection_b, preferred_element_type=jnp.float32)
    cont_orth = (cont_orbitals.astype(jnp.float32) - removed).astype(jnp.bfloat16)
    squares = jnp.sum(jnp.square(cont_orth.astype(jnp.float32)), axis=0)
    dipole_cont = band_local(dipole_blocks, band_offsets, cont_orth, 3)
    partial_dip = lax.dot_general(
        target_orbitals,
        dipole_cont,
        (((0,), (0,)), ((), ())),
        preferred_element_type=jnp.float32,
    )
    dipole_mo = dipole_scatter(partial_dip, squares, n, count)
    return (cont_orth, dipole_mo)


def solution(mesh):
    return jax.shard_map(
        on_device,
        mesh=mesh,
        in_specs=(
            P("basis", "orb"),
            P("basis", None),
            P("basis", None, None, None),
            P("basis", None, None, None),
            P("basis", None),
        ),
        out_specs=(P("basis", "orb"), P("basis", "orb")),
        check_vma=False,
    )
```

```python
import functools

import jax
import jax.numpy as jnp
from jax import lax
from jax.experimental import pallas as pl
from jax.experimental.pallas import tpu as pltpu
from jax.sharding import PartitionSpec as P

BK = 256
KB = 4
MESH = pl.DeviceIdType.MESH


def padded_2(block, sides, width):
    for axis, dim in sides:
        count = lax.axis_size(axis)
        forward = [(i, i + 1) for i in range(count - 1)]
        backward = [(target, source) for source, target in forward]
        low = lax.ppermute(
            lax.slice_in_dim(block, block.shape[dim] - width, None, axis=dim), axis, forward
        )
        high = lax.ppermute(lax.slice_in_dim(block, 0, width, axis=dim), axis, backward)
        block = jnp.concatenate([low, block, high], axis=dim)
    return block


def band_kernel(rows_per_step, off_ref, blk_ref, field_ref, out_ref):
    g = pl.program_id(0)
    for r in range(rows_per_step):
        b = g * rows_per_step + r
        acc = None
        for k in range(KB):
            start = pl.multiple_of((b + 2 + off_ref[b, k]) * BK, BK)
            term = jnp.dot(
                blk_ref[r, k], field_ref[pl.ds(start, BK), :], preferred_element_type=jnp.float32
            )
            acc = term if acc is None else acc + term
        out_ref[pl.ds(r * BK, BK), :] = acc.astype(out_ref.dtype)


def band_local(blocks, offsets, padded):
    nblk = blocks.shape[0]
    rows, width = padded.shape
    per = 8 if nblk % 8 == 0 else 1
    return pl.pallas_call(
        functools.partial(band_kernel, per),
        out_shape=jax.ShapeDtypeStruct((nblk * BK, width), jnp.bfloat16),
        grid_spec=pltpu.PrefetchScalarGridSpec(
            num_scalar_prefetch=1,
            grid=(nblk // per,),
            in_specs=[
                pl.BlockSpec((per, KB, BK, BK), lambda g, off: (g, 0, 0, 0)),
                pl.BlockSpec((rows, width), lambda g, off: (0, 0)),
            ],
            out_specs=pl.BlockSpec((per * BK, width), lambda g, off: (g, 0)),
        ),
        cost_estimate=pl.CostEstimate(
            flops=2 * nblk * KB * BK * BK * width,
            bytes_accessed=blocks.size * 2 + padded.size * 2 + nblk * BK * width * 2,
            transcendentals=0,
        ),
        compiler_params=pltpu.CompilerParams(vmem_limit_bytes=24 * 1024 * 1024),
    )(offsets, blocks, padded)


def _place():
    me = lax.axis_index("basis")
    orb = lax.axis_index("orb")
    core = lax.rem(me, 2)
    partner = me + 1 - 2 * core
    chip = lax.div(me, 2)
    return orb, core, partner, chip


def _barrier_group(nchip, orb, core, partner, chip):
    barrier = pltpu.get_barrier_semaphore()
    pl.semaphore_signal(barrier, inc=1, device_id=(partner, orb), device_id_type=MESH)
    for j in range(1, nchip):
        peer = 2 * lax.rem(chip + j, nchip) + core
        pl.semaphore_signal(barrier, inc=1, device_id=(peer, orb), device_id_type=MESH)
    pl.semaphore_wait(barrier, nchip)


def _remote(src, dst, ssem, rsem, device, orb):
    return pltpu.make_async_remote_copy(
        src_ref=src, dst_ref=dst, send_sem=ssem, recv_sem=rsem,
        device_id=(device, orb), device_id_type=MESH,
    )


def _two_level_sum(nchip, x_ref, pair_recv, part, chip_recv, p_send, p_recv, c_send, c_recv):
    orb, core, partner, chip = _place()
    _barrier_group(nchip, orb, core, partner, chip)
    pair = []
    for i in range(nchip):
        cp = _remote(x_ref.at[i, 1 - core], pair_recv.at[i], p_send.at[i], p_recv.at[i], partner, orb)
        cp.start()
        pair.append(cp)
    f32 = jnp.float32
    for i in range(nchip):
        pair[i].wait_recv()
        part[i] = (x_ref[i, core].astype(f32) + pair_recv[i].astype(f32)).astype(part.dtype)
    sends = []
    for j in range(1, nchip):
        dst = lax.rem(chip + j, nchip)
        cp = _remote(part.at[dst], chip_recv.at[chip], c_send.at[j], c_recv.at[chip], 2 * dst + core, orb)
        cp.start()
        sends.append(cp)
    total = x_ref[chip, core].astype(f32) + pair_recv[chip].astype(f32)
    for j in range(1, nchip):
        src = lax.rem(chip + nchip - j, nchip)
        _remote(part.at[src], chip_recv.at[src], c_send.at[j], c_recv.at[src], 2 * src + core, orb).wait_recv()
        total = total + chip_recv[src].astype(f32)
    for cp in pair + sends:
        cp.wait_send()
    return total


def allreduce_kernel(nchip, x_ref, out_ref, pair_recv, part, chip_recv, sendbuf, half, other,
                     p_send, p_recv, c_send, c_recv, g_send, g_recv, h_send, h_recv):
    total = _two_level_sum(nchip, x_ref, pair_recv, part, chip_recv, p_send, p_recv, c_send, c_recv)
    orb, core, partner, chip = _place()
    rounded = total.astype(sendbuf.dtype)
    sendbuf[...] = rounded
    half[chip] = rounded
    sends = []
    for j in range(1, nchip):
        dst = lax.rem(chip + j, nchip)
        cp = _remote(sendbuf, half.at[chip], g_send.at[j], g_recv.at[chip], 2 * dst + core, orb)
        cp.start()
        sends.append(cp)
    for j in range(1, nchip):
        src = lax.rem(chip + nchip - j, nchip)
        _remote(sendbuf, half.at[src], g_send.at[j], g_recv.at[src], 2 * src + core, orb).wait_recv()
    for cp in sends:
        cp.wait_send()
    cp = _remote(half, other, h_send.at[0], h_recv.at[0], partner, orb)
    cp.start()
    cp.wait_recv()
    for i in range(nchip):
        out_ref[i, core] = half[i]
        out_ref[i, 1 - core] = other[i]
    cp.wait_send()


def _two_level_scratch(nchip, rows, cols):
    return [pltpu.VMEM((nchip, rows, cols), jnp.bfloat16)] * 3


def allreduce_to_bf16(partial, n):
    rows, cols = partial.shape
    nchip = n // 2
    chunk = rows // n
    x = partial.astype(jnp.bfloat16).reshape(nchip, 2, chunk, cols)
    out = pl.pallas_call(
        functools.partial(allreduce_kernel, nchip),
        out_shape=jax.ShapeDtypeStruct((nchip, 2, chunk, cols), jnp.bfloat16),
        in_specs=[pl.BlockSpec(memory_space=pltpu.VMEM)],
        out_specs=pl.BlockSpec(memory_space=pltpu.VMEM),
        scratch_shapes=_two_level_scratch(nchip, chunk, cols) + [
            pltpu.VMEM((chunk, cols), jnp.bfloat16),
            pltpu.VMEM((nchip, chunk, cols), jnp.bfloat16),
            pltpu.VMEM((nchip, chunk, cols), jnp.bfloat16),
        ] + [pltpu.SemaphoreType.DMA((nchip,))] * 6 + [pltpu.SemaphoreType.DMA((1,))] * 2,
        compiler_params=pltpu.CompilerParams(
            collective_id=0, has_side_effects=True, vmem_limit_bytes=12 * 1024 * 1024
        ),
        cost_estimate=pl.CostEstimate(flops=0, bytes_accessed=64 * x.size, transcendentals=0),
    )(x)
    return out.reshape(rows, cols)


def dipole_kernel(nchip, chunk, count, x_ref, out_ref, pair_recv, part, chip_recv,
                  p_send, p_recv, c_send, c_recv):
    total = _two_level_sum(nchip, x_ref, pair_recv, part, chip_recv, p_send, p_recv, c_send, c_recv)
    squares = total[chunk:chunk + 1, :] + total[chunk + 1:chunk + 2, :]
    col_norm = 1.0 / jnp.sqrt(squares / count + 1e-06)
    out_ref[...] = (total[:chunk, :] * col_norm).astype(out_ref.dtype)


def dipole_scatter(partial, squares, n, count):
    rows, cols = partial.shape
    nchip = n // 2
    chunk = rows // n
    high = squares.astype(jnp.bfloat16)
    low = (squares - high.astype(jnp.float32)).astype(jnp.bfloat16)
    tail = jnp.concatenate([high[None, :], low[None, :], jnp.zeros((6, cols), jnp.bfloat16)], axis=0)
    x = jnp.concatenate(
        [
            partial.astype(jnp.bfloat16).reshape(nchip, 2, chunk, cols),
            jnp.broadcast_to(tail[None, None], (nchip, 2, 8, cols)),
        ],
        axis=2,
    )
    return pl.pallas_call(
        functools.partial(dipole_kernel, nchip, chunk, count),
        out_shape=jax.ShapeDtypeStruct((chunk, cols), jnp.bfloat16),
        in_specs=[pl.BlockSpec(memory_space=pltpu.VMEM)],
        out_specs=pl.BlockSpec(memory_space=pltpu.VMEM),
        scratch_shapes=_two_level_scratch(nchip, chunk + 8, cols)
        + [pltpu.SemaphoreType.DMA((nchip,))] * 4,
        compiler_params=pltpu.CompilerParams(
            collective_id=1, has_side_effects=True, vmem_limit_bytes=12 * 1024 * 1024
        ),
        cost_estimate=pl.CostEstimate(flops=0, bytes_accessed=32 * x.size, transcendentals=0),
    )(x)


def on_device(cont_orbitals, target_orbitals, margin_blocks, dipole_blocks, band_offsets):
    n = lax.axis_size("basis")
    count = band_offsets.shape[0] * BK * n
    cont_padded = padded_2(cont_orbitals, (("basis", 0),), 2 * BK)
    margin_cont = band_local(margin_blocks, band_offsets, cont_padded)
    partial_proj = lax.dot_general(
        target_orbitals, margin_cont, (((0,), (0,)), ((), ())), preferred_element_type=jnp.float32
    )
    projection_b = allreduce_to_bf16(partial_proj, n)
    removed = jnp.dot(target_orbitals, projection_b, preferred_element_type=jnp.float32)
    cont_orth = (cont_orbitals.astype(jnp.float32) - removed).astype(jnp.bfloat16)
    squares = jnp.sum(jnp.square(cont_orth.astype(jnp.float32)), axis=0)
    orth_padded = padded_2(cont_orth, (("basis", 0),), 2 * BK)
    dipole_cont = band_local(dipole_blocks, band_offsets, orth_padded)
    partial_dip = lax.dot_general(
        target_orbitals,
        dipole_cont,
        (((0,), (0,)), ((), ())),
        preferred_element_type=jnp.float32,
    )
    dipole_mo = dipole_scatter(partial_dip, squares, n, count)
    return (cont_orth, dipole_mo)


def solution(mesh):
    return jax.shard_map(
        on_device,
        mesh=mesh,
        in_specs=(
            P("basis", "orb"),
            P("basis", None),
            P("basis", None, None, None),
            P("basis", None, None, None),
            P("basis", None),
        ),
        out_specs=(P("basis", "orb"), P("basis", "orb")),
        check_vma=False,
    )
```

```python
import functools

import jax
import jax.numpy as jnp
from jax import lax
from jax.experimental import pallas as pl
from jax.experimental.pallas import tpu as pltpu
from jax.sharding import PartitionSpec as P

BK = 256
KB = 4
MESH = pl.DeviceIdType.MESH


def padded_2(block, sides, width):
    for axis, dim in sides:
        count = lax.axis_size(axis)
        forward = [(i, i + 1) for i in range(count - 1)]
        backward = [(target, source) for source, target in forward]
        low = lax.ppermute(
            lax.slice_in_dim(block, block.shape[dim] - width, None, axis=dim), axis, forward
        )
        high = lax.ppermute(lax.slice_in_dim(block, 0, width, axis=dim), axis, backward)
        block = jnp.concatenate([low, block, high], axis=dim)
    return block


def band_kernel(rows_per_step, off_ref, blk_ref, field_ref, out_ref):
    g = pl.program_id(0)
    for r in range(rows_per_step):
        b = g * rows_per_step + r
        acc = None
        for k in range(KB):
            start = pl.multiple_of((b + 2 + off_ref[b, k]) * BK, BK)
            term = jnp.dot(
                blk_ref[r, k], field_ref[pl.ds(start, BK), :], preferred_element_type=jnp.float32
            )
            acc = term if acc is None else acc + term
        out_ref[pl.ds(r * BK, BK), :] = acc.astype(out_ref.dtype)


def band_local(blocks, offsets, padded):
    nblk = blocks.shape[0]
    rows, width = padded.shape
    per = 8 if nblk % 8 == 0 else 1
    return pl.pallas_call(
        functools.partial(band_kernel, per),
        out_shape=jax.ShapeDtypeStruct((nblk * BK, width), jnp.bfloat16),
        grid_spec=pltpu.PrefetchScalarGridSpec(
            num_scalar_prefetch=1,
            grid=(nblk // per,),
            in_specs=[
                pl.BlockSpec((per, KB, BK, BK), lambda g, off: (g, 0, 0, 0)),
                pl.BlockSpec((rows, width), lambda g, off: (0, 0)),
            ],
            out_specs=pl.BlockSpec((per * BK, width), lambda g, off: (g, 0)),
        ),
        cost_estimate=pl.CostEstimate(
            flops=2 * nblk * KB * BK * BK * width,
            bytes_accessed=blocks.size * 2 + padded.size * 2 + nblk * BK * width * 2,
            transcendentals=0,
        ),
        compiler_params=pltpu.CompilerParams(vmem_limit_bytes=24 * 1024 * 1024),
    )(offsets, blocks, padded)


def orth_kernel(tgt_ref, proj_ref, cont_ref, orth_ref, sq_ref):
    removed = jnp.dot(tgt_ref[...], proj_ref[...], preferred_element_type=jnp.float32)
    orth = (cont_ref[...].astype(jnp.float32) - removed).astype(orth_ref.dtype)
    orth_ref[...] = orth
    wide = orth.astype(jnp.float32)
    part = jnp.sum(wide * wide, axis=0, keepdims=True)

    @pl.when(pl.program_id(0) == 0)
    def _():
        sq_ref[...] = part

    @pl.when(pl.program_id(0) > 0)
    def _():
        sq_ref[...] += part


def orthogonalize(target, projection_b, cont):
    rows, nt = target.shape
    width = cont.shape[1]
    tile = 512 if rows % 512 == 0 else rows
    orth, squares = pl.pallas_call(
        orth_kernel,
        out_shape=(
            jax.ShapeDtypeStruct((rows, width), jnp.bfloat16),
            jax.ShapeDtypeStruct((1, width), jnp.float32),
        ),
        grid=(rows // tile,),
        in_specs=[
            pl.BlockSpec((tile, nt), lambda i: (i, 0)),
            pl.BlockSpec((nt, width), lambda i: (0, 0)),
            pl.BlockSpec((tile, width), lambda i: (i, 0)),
        ],
        out_specs=(
            pl.BlockSpec((tile, width), lambda i: (i, 0)),
            pl.BlockSpec((1, width), lambda i: (0, 0)),
        ),
        cost_estimate=pl.CostEstimate(
            flops=2 * rows * nt * width,
            bytes_accessed=target.size * 2 + projection_b.size * 2 + 2 * cont.size * 2,
            transcendentals=0,
        ),
        compiler_params=pltpu.CompilerParams(vmem_limit_bytes=16 * 1024 * 1024),
    )(target, projection_b, cont)
    return orth, squares[0]


def _place():
    me = lax.axis_index("basis")
    orb = lax.axis_index("orb")
    core = lax.rem(me, 2)
    partner = me + 1 - 2 * core
    chip = lax.div(me, 2)
    return orb, core, partner, chip


def _barrier_group(nchip, orb, core, partner, chip):
    barrier = pltpu.get_barrier_semaphore()
    pl.semaphore_signal(barrier, inc=1, device_id=(partner, orb), device_id_type=MESH)
    for j in range(1, nchip):
        peer = 2 * lax.rem(chip + j, nchip) + core
        pl.semaphore_signal(barrier, inc=1, device_id=(peer, orb), device_id_type=MESH)
    pl.semaphore_wait(barrier, nchip)


def _remote(src, dst, ssem, rsem, device, orb):
    return pltpu.make_async_remote_copy(
        src_ref=src, dst_ref=dst, send_sem=ssem, recv_sem=rsem,
        device_id=(device, orb), device_id_type=MESH,
    )


def _two_level_sum(nchip, x_ref, pair_recv, part, chip_recv, p_send, p_recv, c_send, c_recv):
    orb, core, partner, chip = _place()
    _barrier_group(nchip, orb, core, partner, chip)
    pair = []
    for i in range(nchip):
        cp = _remote(x_ref.at[i, 1 - core], pair_recv.at[i], p_send.at[i], p_recv.at[i], partner, orb)
        cp.start()
        pair.append(cp)
    for i in range(nchip):
        pair[i].wait_recv()
        part[i] = x_ref[i, core] + pair_recv[i]
    sends = []
    for j in range(1, nchip):
        dst = lax.rem(chip + j, nchip)
        cp = _remote(part.at[dst], chip_recv.at[chip], c_send.at[j], c_recv.at[chip], 2 * dst + core, orb)
        cp.start()
        sends.append(cp)
    total = part[chip]
    for j in range(1, nchip):
        src = lax.rem(chip + nchip - j, nchip)
        _remote(part.at[src], chip_recv.at[src], c_send.at[j], c_recv.at[src], 2 * src + core, orb).wait_recv()
        total = total + chip_recv[src]
    for cp in pair + sends:
        cp.wait_send()
    return total


def allreduce_kernel(nchip, x_ref, out_ref, pair_recv, part, chip_recv, sendbuf, half, other,
                     p_send, p_recv, c_send, c_recv, g_send, g_recv, h_send, h_recv):
    total = _two_level_sum(nchip, x_ref, pair_recv, part, chip_recv, p_send, p_recv, c_send, c_recv)
    orb, core, partner, chip = _place()
    rounded = total.astype(sendbuf.dtype)
    sendbuf[...] = rounded
    half[chip] = rounded
    sends = []
    for j in range(1, nchip):
        dst = lax.rem(chip + j, nchip)
        cp = _remote(sendbuf, half.at[chip], g_send.at[j], g_recv.at[chip], 2 * dst + core, orb)
        cp.start()
        sends.append(cp)
    for j in range(1, nchip):
        src = lax.rem(chip + nchip - j, nchip)
        _remote(sendbuf, half.at[src], g_send.at[j], g_recv.at[src], 2 * src + core, orb).wait_recv()
    for cp in sends:
        cp.wait_send()
    cp = _remote(half, other, h_send.at[0], h_recv.at[0], partner, orb)
    cp.start()
    cp.wait_recv()
    for i in range(nchip):
        out_ref[i, core] = half[i]
        out_ref[i, 1 - core] = other[i]
    cp.wait_send()


def _two_level_scratch(nchip, rows, cols):
    return [
        pltpu.VMEM((nchip, rows, cols), jnp.float32),
        pltpu.VMEM((nchip, rows, cols), jnp.float32),
        pltpu.VMEM((nchip, rows, cols), jnp.float32),
    ]


def allreduce_to_bf16(partial, n):
    rows, cols = partial.shape
    nchip = n // 2
    chunk = rows // n
    x = partial.reshape(nchip, 2, chunk, cols)
    out = pl.pallas_call(
        functools.partial(allreduce_kernel, nchip),
        out_shape=jax.ShapeDtypeStruct((nchip, 2, chunk, cols), jnp.bfloat16),
        in_specs=[pl.BlockSpec(memory_space=pltpu.VMEM)],
        out_specs=pl.BlockSpec(memory_space=pltpu.VMEM),
        scratch_shapes=_two_level_scratch(nchip, chunk, cols) + [
            pltpu.VMEM((chunk, cols), jnp.bfloat16),
            pltpu.VMEM((nchip, chunk, cols), jnp.bfloat16),
            pltpu.VMEM((nchip, chunk, cols), jnp.bfloat16),
        ] + [pltpu.SemaphoreType.DMA((nchip,))] * 6 + [pltpu.SemaphoreType.DMA((1,))] * 2,
        compiler_params=pltpu.CompilerParams(
            collective_id=0, has_side_effects=True, vmem_limit_bytes=12 * 1024 * 1024
        ),
        cost_estimate=pl.CostEstimate(flops=0, bytes_accessed=64 * x.size, transcendentals=0),
    )(x)
    return out.reshape(rows, cols)


def dipole_kernel(nchip, chunk, count, x_ref, out_ref, pair_recv, part, chip_recv,
                  p_send, p_recv, c_send, c_recv):
    total = _two_level_sum(nchip, x_ref, pair_recv, part, chip_recv, p_send, p_recv, c_send, c_recv)
    squares = total[chunk:chunk + 1, :]
    col_norm = 1.0 / jnp.sqrt(squares / count + 1e-06)
    out_ref[...] = (total[:chunk, :] * col_norm).astype(out_ref.dtype)


def dipole_scatter(partial, squares, n, count):
    rows, cols = partial.shape
    nchip = n // 2
    chunk = rows // n
    x = jnp.concatenate(
        [
            partial.reshape(nchip, 2, chunk, cols),
            jnp.broadcast_to(squares[None, None, None, :], (nchip, 2, 8, cols)),
        ],
        axis=2,
    )
    return pl.pallas_call(
        functools.partial(dipole_kernel, nchip, chunk, count),
        out_shape=jax.ShapeDtypeStruct((chunk, cols), jnp.bfloat16),
        in_specs=[pl.BlockSpec(memory_space=pltpu.VMEM)],
        out_specs=pl.BlockSpec(memory_space=pltpu.VMEM),
        scratch_shapes=_two_level_scratch(nchip, chunk + 8, cols)
        + [pltpu.SemaphoreType.DMA((nchip,))] * 4,
        compiler_params=pltpu.CompilerParams(
            collective_id=1, has_side_effects=True, vmem_limit_bytes=12 * 1024 * 1024
        ),
        cost_estimate=pl.CostEstimate(flops=0, bytes_accessed=32 * x.size, transcendentals=0),
    )(x)


def on_device(cont_orbitals, target_orbitals, margin_blocks, dipole_blocks, band_offsets):
    n = lax.axis_size("basis")
    count = band_offsets.shape[0] * BK * n
    cont_padded = padded_2(cont_orbitals, (("basis", 0),), 2 * BK)
    margin_cont = band_local(margin_blocks, band_offsets, cont_padded)
    partial_proj = lax.dot_general(
        target_orbitals, margin_cont, (((0,), (0,)), ((), ())), preferred_element_type=jnp.float32
    )
    projection_b = allreduce_to_bf16(partial_proj, n)
    cont_orth, squares = orthogonalize(target_orbitals, projection_b, cont_orbitals)
    orth_padded = padded_2(cont_orth, (("basis", 0),), 2 * BK)
    dipole_cont = band_local(dipole_blocks, band_offsets, orth_padded)
    partial_dip = lax.dot_general(
        target_orbitals,
        dipole_cont,
        (((0,), (0,)), ((), ())),
        preferred_element_type=jnp.float32,
    )
    dipole_mo = dipole_scatter(partial_dip, squares, n, count)
    return (cont_orth, dipole_mo)


def solution(mesh):
    return jax.shard_map(
        on_device,
        mesh=mesh,
        in_specs=(
            P("basis", "orb"),
            P("basis", None),
            P("basis", None, None, None),
            P("basis", None, None, None),
            P("basis", None),
        ),
        out_specs=(P("basis", "orb"), P("basis", "orb")),
        check_vma=False,
    )
```

```python
import functools

import jax
import jax.numpy as jnp
from jax import lax
from jax.experimental import pallas as pl
from jax.experimental.pallas import tpu as pltpu
from jax.sharding import PartitionSpec as P

BK = 256
KB = 4
MESH = pl.DeviceIdType.MESH


def padded_2(block, sides, width):
    for axis, dim in sides:
        count = lax.axis_size(axis)
        forward = [(i, i + 1) for i in range(count - 1)]
        backward = [(target, source) for source, target in forward]
        low = lax.ppermute(
            lax.slice_in_dim(block, block.shape[dim] - width, None, axis=dim), axis, forward
        )
        high = lax.ppermute(lax.slice_in_dim(block, 0, width, axis=dim), axis, backward)
        block = jnp.concatenate([low, block, high], axis=dim)
    return block


def band_kernel(rows_per_step, off_ref, blk_ref, field_ref, out_ref):
    g = pl.program_id(0)
    for r in range(rows_per_step):
        b = g * rows_per_step + r
        acc = None
        for k in range(KB):
            start = pl.multiple_of((b + 2 + off_ref[b, k]) * BK, BK)
            term = jnp.dot(
                blk_ref[r, k], field_ref[pl.ds(start, BK), :], preferred_element_type=jnp.float32
            )
            acc = term if acc is None else acc + term
        out_ref[pl.ds(r * BK, BK), :] = acc.astype(out_ref.dtype)


def band_local(blocks, offsets, padded):
    nblk = blocks.shape[0]
    rows, width = padded.shape
    per = 8 if nblk % 8 == 0 else 1
    return pl.pallas_call(
        functools.partial(band_kernel, per),
        out_shape=jax.ShapeDtypeStruct((nblk * BK, width), jnp.bfloat16),
        grid_spec=pltpu.PrefetchScalarGridSpec(
            num_scalar_prefetch=1,
            grid=(nblk // per,),
            in_specs=[
                pl.BlockSpec((per, KB, BK, BK), lambda g, off: (g, 0, 0, 0)),
                pl.BlockSpec((rows, width), lambda g, off: (0, 0)),
            ],
            out_specs=pl.BlockSpec((per * BK, width), lambda g, off: (g, 0)),
        ),
        cost_estimate=pl.CostEstimate(
            flops=2 * nblk * KB * BK * BK * width,
            bytes_accessed=blocks.size * 2 + padded.size * 2 + nblk * BK * width * 2,
            transcendentals=0,
        ),
        compiler_params=pltpu.CompilerParams(vmem_limit_bytes=24 * 1024 * 1024),
    )(offsets, blocks, padded)


def _place():
    me = lax.axis_index("basis")
    orb = lax.axis_index("orb")
    core = lax.rem(me, 2)
    partner = me + 1 - 2 * core
    chip = lax.div(me, 2)
    return orb, core, partner, chip


def _barrier_group(nchip, orb, core, partner, chip):
    barrier = pltpu.get_barrier_semaphore()
    pl.semaphore_signal(barrier, inc=1, device_id=(partner, orb), device_id_type=MESH)
    for j in range(1, nchip):
        peer = 2 * lax.rem(chip + j, nchip) + core
        pl.semaphore_signal(barrier, inc=1, device_id=(peer, orb), device_id_type=MESH)
    pl.semaphore_wait(barrier, nchip)


def _remote(src, dst, ssem, rsem, device, orb):
    return pltpu.make_async_remote_copy(
        src_ref=src, dst_ref=dst, send_sem=ssem, recv_sem=rsem,
        device_id=(device, orb), device_id_type=MESH,
    )


def _two_level_sum(nchip, x_ref, pair_recv, part, chip_recv, p_send, p_recv, c_send, c_recv):
    orb, core, partner, chip = _place()
    _barrier_group(nchip, orb, core, partner, chip)
    pair = []
    for j in list(range(1, nchip)) + [0]:
        dst = lax.rem(chip + j, nchip)
        cp = _remote(x_ref.at[dst, 1 - core], pair_recv.at[dst], p_send.at[j], p_recv.at[dst], partner, orb)
        cp.start()
        pair.append(cp)
    sends = []
    for j in range(1, nchip):
        dst = lax.rem(chip + j, nchip)
        pair[j - 1].wait_recv()
        part[dst] = x_ref[dst, core] + pair_recv[dst]
        cp = _remote(part.at[dst], chip_recv.at[chip], c_send.at[j], c_recv.at[chip], 2 * dst + core, orb)
        cp.start()
        sends.append(cp)
    pair[-1].wait_recv()
    total = x_ref[chip, core] + pair_recv[chip]
    for j in range(1, nchip):
        src = lax.rem(chip + nchip - j, nchip)
        _remote(part.at[src], chip_recv.at[src], c_send.at[j], c_recv.at[src], 2 * src + core, orb).wait_recv()
        total = total + chip_recv[src]
    for cp in pair + sends:
        cp.wait_send()
    return total


def allreduce_kernel(nchip, x_ref, out_ref, pair_recv, part, chip_recv, sendbuf, half, other,
                     p_send, p_recv, c_send, c_recv, g_send, g_recv, h_send, h_recv):
    total = _two_level_sum(nchip, x_ref, pair_recv, part, chip_recv, p_send, p_recv, c_send, c_recv)
    orb, core, partner, chip = _place()
    rounded = total.astype(sendbuf.dtype)
    sendbuf[...] = rounded
    sends = []
    for j in range(1, nchip):
        dst = lax.rem(chip + j, nchip)
        cp = _remote(sendbuf, half.at[chip], g_send.at[j], g_recv.at[chip], 2 * dst + core, orb)
        cp.start()
        sends.append(cp)
    cp = _remote(sendbuf, other.at[chip], h_send.at[0], h_recv.at[chip], partner, orb)
    cp.start()
    sends.append(cp)
    out_ref[chip, core] = rounded
    for j in range(1, nchip):
        src = lax.rem(chip + nchip - j, nchip)
        _remote(sendbuf, half.at[src], g_send.at[j], g_recv.at[src], 2 * src + core, orb).wait_recv()
        cp = _remote(half.at[src], other.at[src], h_send.at[j], h_recv.at[src], partner, orb)
        cp.start()
        sends.append(cp)
        out_ref[src, core] = half[src]
    for j in range(nchip):
        src = lax.rem(chip + nchip - j, nchip)
        _remote(sendbuf, other.at[src], h_send.at[j], h_recv.at[src], partner, orb).wait_recv()
        out_ref[src, 1 - core] = other[src]
    for cp in sends:
        cp.wait_send()


def _two_level_scratch(nchip, rows, cols):
    return [
        pltpu.VMEM((nchip, rows, cols), jnp.float32),
        pltpu.VMEM((nchip, rows, cols), jnp.float32),
        pltpu.VMEM((nchip, rows, cols), jnp.float32),
    ]


def allreduce_to_bf16(partial, n):
    rows, cols = partial.shape
    nchip = n // 2
    chunk = rows // n
    x = partial.reshape(nchip, 2, chunk, cols)
    out = pl.pallas_call(
        functools.partial(allreduce_kernel, nchip),
        out_shape=jax.ShapeDtypeStruct((nchip, 2, chunk, cols), jnp.bfloat16),
        in_specs=[pl.BlockSpec(memory_space=pltpu.VMEM)],
        out_specs=pl.BlockSpec(memory_space=pltpu.VMEM),
        scratch_shapes=_two_level_scratch(nchip, chunk, cols) + [
            pltpu.VMEM((chunk, cols), jnp.bfloat16),
            pltpu.VMEM((nchip, chunk, cols), jnp.bfloat16),
            pltpu.VMEM((nchip, chunk, cols), jnp.bfloat16),
        ] + [pltpu.SemaphoreType.DMA((nchip,))] * 8,
        compiler_params=pltpu.CompilerParams(
            collective_id=0, has_side_effects=True, vmem_limit_bytes=12 * 1024 * 1024
        ),
        cost_estimate=pl.CostEstimate(flops=0, bytes_accessed=64 * x.size, transcendentals=0),
    )(x)
    return out.reshape(rows, cols)


def dipole_kernel(nchip, chunk, count, x_ref, out_ref, pair_recv, part, chip_recv,
                  p_send, p_recv, c_send, c_recv):
    total = _two_level_sum(nchip, x_ref, pair_recv, part, chip_recv, p_send, p_recv, c_send, c_recv)
    squares = total[chunk:chunk + 1, :]
    col_norm = 1.0 / jnp.sqrt(squares / count + 1e-06)
    out_ref[...] = (total[:chunk, :] * col_norm).astype(out_ref.dtype)


def dipole_scatter(partial, squares, n, count):
    rows, cols = partial.shape
    nchip = n // 2
    chunk = rows // n
    x = jnp.concatenate(
        [
            partial.reshape(nchip, 2, chunk, cols),
            jnp.broadcast_to(squares[None, None, None, :], (nchip, 2, 8, cols)),
        ],
        axis=2,
    )
    return pl.pallas_call(
        functools.partial(dipole_kernel, nchip, chunk, count),
        out_shape=jax.ShapeDtypeStruct((chunk, cols), jnp.bfloat16),
        in_specs=[pl.BlockSpec(memory_space=pltpu.VMEM)],
        out_specs=pl.BlockSpec(memory_space=pltpu.VMEM),
        scratch_shapes=_two_level_scratch(nchip, chunk + 8, cols)
        + [pltpu.SemaphoreType.DMA((nchip,))] * 4,
        compiler_params=pltpu.CompilerParams(
            collective_id=1, has_side_effects=True, vmem_limit_bytes=12 * 1024 * 1024
        ),
        cost_estimate=pl.CostEstimate(flops=0, bytes_accessed=32 * x.size, transcendentals=0),
    )(x)


def on_device(cont_orbitals, target_orbitals, margin_blocks, dipole_blocks, band_offsets):
    n = lax.axis_size("basis")
    count = band_offsets.shape[0] * BK * n
    cont_padded = padded_2(cont_orbitals, (("basis", 0),), 2 * BK)
    margin_cont = band_local(margin_blocks, band_offsets, cont_padded)
    partial_proj = lax.dot_general(
        target_orbitals, margin_cont, (((0,), (0,)), ((), ())), preferred_element_type=jnp.float32
    )
    projection_b = allreduce_to_bf16(partial_proj, n)
    removed = jnp.dot(target_orbitals, projection_b, preferred_element_type=jnp.float32)
    cont_orth = (cont_orbitals.astype(jnp.float32) - removed).astype(jnp.bfloat16)
    squares = jnp.sum(jnp.square(cont_orth.astype(jnp.float32)), axis=0)
    orth_padded = padded_2(cont_orth, (("basis", 0),), 2 * BK)
    dipole_cont = band_local(dipole_blocks, band_offsets, orth_padded)
    partial_dip = lax.dot_general(
        target_orbitals,
        dipole_cont,
        (((0,), (0,)), ((), ())),
        preferred_element_type=jnp.float32,
    )
    dipole_mo = dipole_scatter(partial_dip, squares, n, count)
    return (cont_orth, dipole_mo)


def solution(mesh):
    return jax.shard_map(
        on_device,
        mesh=mesh,
        in_specs=(
            P("basis", "orb"),
            P("basis", None),
            P("basis", None, None, None),
            P("basis", None, None, None),
            P("basis", None),
        ),
        out_specs=(P("basis", "orb"), P("basis", "orb")),
        check_vma=False,
    )
```

```python
import functools

import jax
import jax.numpy as jnp
from jax import lax
from jax.experimental import pallas as pl
from jax.experimental.pallas import tpu as pltpu
from jax.sharding import PartitionSpec as P

BK = 256
KB = 4
MESH = pl.DeviceIdType.MESH


def padded_2(block, sides, width):
    for axis, dim in sides:
        count = lax.axis_size(axis)
        forward = [(i, i + 1) for i in range(count - 1)]
        backward = [(target, source) for source, target in forward]
        low = lax.ppermute(
            lax.slice_in_dim(block, block.shape[dim] - width, None, axis=dim), axis, forward
        )
        high = lax.ppermute(lax.slice_in_dim(block, 0, width, axis=dim), axis, backward)
        block = jnp.concatenate([low, block, high], axis=dim)
    return block


def halo_kernel(n, field_ref, out_ref, low, high, send_sem, recv_sem, copy_sem):
    rows, width = field_ref.shape
    edge = 2 * BK
    me = lax.axis_index("basis")
    orb = lax.axis_index("orb")
    has_low = me > 0
    has_high = me < n - 1
    middle = pltpu.make_async_copy(field_ref, out_ref.at[pl.ds(edge, rows)], copy_sem.at[0])
    middle.start()
    barrier = pltpu.get_barrier_semaphore()

    @pl.when(has_low)
    def _():
        pl.semaphore_signal(barrier, inc=1, device_id=(me - 1, orb), device_id_type=MESH)

    @pl.when(has_high)
    def _():
        pl.semaphore_signal(barrier, inc=1, device_id=(me + 1, orb), device_id_type=MESH)

    pl.semaphore_wait(barrier, has_low.astype(jnp.int32) + has_high.astype(jnp.int32))
    to_low = pltpu.make_async_remote_copy(
        src_ref=field_ref.at[pl.ds(0, edge)], dst_ref=high,
        send_sem=send_sem.at[0], recv_sem=recv_sem.at[0],
        device_id=(jnp.maximum(me - 1, 0), orb), device_id_type=MESH,
    )
    to_high = pltpu.make_async_remote_copy(
        src_ref=field_ref.at[pl.ds(rows - edge, edge)], dst_ref=low,
        send_sem=send_sem.at[1], recv_sem=recv_sem.at[1],
        device_id=(jnp.minimum(me + 1, n - 1), orb), device_id_type=MESH,
    )

    @pl.when(has_low)
    def _():
        to_low.start()

    @pl.when(has_high)
    def _():
        to_high.start()

    @pl.when(has_high)
    def _():
        to_low.wait_recv()
        out_ref[pl.ds(rows + edge, edge), :] = high[...]

    @pl.when(jnp.logical_not(has_high))
    def _():
        out_ref[pl.ds(rows + edge, edge), :] = jnp.zeros((edge, width), out_ref.dtype)

    @pl.when(has_low)
    def _():
        to_high.wait_recv()
        out_ref[pl.ds(0, edge), :] = low[...]

    @pl.when(jnp.logical_not(has_low))
    def _():
        out_ref[pl.ds(0, edge), :] = jnp.zeros((edge, width), out_ref.dtype)

    @pl.when(has_low)
    def _():
        to_low.wait_send()

    @pl.when(has_high)
    def _():
        to_high.wait_send()

    middle.wait()


def with_halo(field, collective_id):
    rows, width = field.shape
    n = lax.axis_size("basis")
    return pl.pallas_call(
        functools.partial(halo_kernel, n),
        out_shape=jax.ShapeDtypeStruct((rows + 4 * BK, width), field.dtype),
        in_specs=[pl.BlockSpec(memory_space=pltpu.VMEM)],
        out_specs=pl.BlockSpec(memory_space=pltpu.VMEM),
        scratch_shapes=[
            pltpu.VMEM((2 * BK, width), field.dtype),
            pltpu.VMEM((2 * BK, width), field.dtype),
            pltpu.SemaphoreType.DMA((2,)),
            pltpu.SemaphoreType.DMA((2,)),
            pltpu.SemaphoreType.DMA((1,)),
        ],
        cost_estimate=pl.CostEstimate(flops=0, bytes_accessed=4 * field.size * 2, transcendentals=0),
        compiler_params=pltpu.CompilerParams(
            collective_id=collective_id, has_side_effects=True, vmem_limit_bytes=8 * 1024 * 1024
        ),
    )(field)


def band_kernel(rows_per_step, off_ref, blk_ref, field_ref, out_ref):
    g = pl.program_id(0)
    for r in range(rows_per_step):
        b = g * rows_per_step + r
        acc = None
        for k in range(KB):
            start = pl.multiple_of((b + 2 + off_ref[b, k]) * BK, BK)
            term = jnp.dot(
                blk_ref[r, k], field_ref[pl.ds(start, BK), :], preferred_element_type=jnp.float32
            )
            acc = term if acc is None else acc + term
        out_ref[pl.ds(r * BK, BK), :] = acc.astype(out_ref.dtype)


def band_local(blocks, offsets, padded):
    nblk = blocks.shape[0]
    rows, width = padded.shape
    per = 8 if nblk % 8 == 0 else 1
    return pl.pallas_call(
        functools.partial(band_kernel, per),
        out_shape=jax.ShapeDtypeStruct((nblk * BK, width), jnp.bfloat16),
        grid_spec=pltpu.PrefetchScalarGridSpec(
            num_scalar_prefetch=1,
            grid=(nblk // per,),
            in_specs=[
                pl.BlockSpec((per, KB, BK, BK), lambda g, off: (g, 0, 0, 0)),
                pl.BlockSpec((rows, width), lambda g, off: (0, 0)),
            ],
            out_specs=pl.BlockSpec((per * BK, width), lambda g, off: (g, 0)),
        ),
        cost_estimate=pl.CostEstimate(
            flops=2 * nblk * KB * BK * BK * width,
            bytes_accessed=blocks.size * 2 + padded.size * 2 + nblk * BK * width * 2,
            transcendentals=0,
        ),
        compiler_params=pltpu.CompilerParams(vmem_limit_bytes=24 * 1024 * 1024),
    )(offsets, blocks, padded)


def _place():
    me = lax.axis_index("basis")
    orb = lax.axis_index("orb")
    core = lax.rem(me, 2)
    partner = me + 1 - 2 * core
    chip = lax.div(me, 2)
    return orb, core, partner, chip


def _barrier_group(nchip, orb, core, partner, chip):
    barrier = pltpu.get_barrier_semaphore()
    pl.semaphore_signal(barrier, inc=1, device_id=(partner, orb), device_id_type=MESH)
    for j in range(1, nchip):
        peer = 2 * lax.rem(chip + j, nchip) + core
        pl.semaphore_signal(barrier, inc=1, device_id=(peer, orb), device_id_type=MESH)
    pl.semaphore_wait(barrier, nchip)


def _remote(src, dst, ssem, rsem, device, orb):
    return pltpu.make_async_remote_copy(
        src_ref=src, dst_ref=dst, send_sem=ssem, recv_sem=rsem,
        device_id=(device, orb), device_id_type=MESH,
    )


def _two_level_sum(nchip, x_ref, pair_recv, part, chip_recv, p_send, p_recv, c_send, c_recv):
    orb, core, partner, chip = _place()
    _barrier_group(nchip, orb, core, partner, chip)
    pair = []
    for j in list(range(1, nchip)) + [0]:
        dst = lax.rem(chip + j, nchip)
        cp = _remote(x_ref.at[dst, 1 - core], pair_recv.at[dst], p_send.at[j], p_recv.at[dst], partner, orb)
        cp.start()
        pair.append(cp)
    sends = []
    for j in range(1, nchip):
        dst = lax.rem(chip + j, nchip)
        pair[j - 1].wait_recv()
        part[dst] = x_ref[dst, core] + pair_recv[dst]
        cp = _remote(part.at[dst], chip_recv.at[chip], c_send.at[j], c_recv.at[chip], 2 * dst + core, orb)
        cp.start()
        sends.append(cp)
    pair[-1].wait_recv()
    total = x_ref[chip, core] + pair_recv[chip]
    for j in range(1, nchip):
        src = lax.rem(chip + nchip - j, nchip)
        _remote(part.at[src], chip_recv.at[src], c_send.at[j], c_recv.at[src], 2 * src + core, orb).wait_recv()
        total = total + chip_recv[src]
    for cp in pair + sends:
        cp.wait_send()
    return total


def allreduce_kernel(nchip, x_ref, out_ref, pair_recv, part, chip_recv, sendbuf, half, other,
                     p_send, p_recv, c_send, c_recv, g_send, g_recv, h_send, h_recv):
    total = _two_level_sum(nchip, x_ref, pair_recv, part, chip_recv, p_send, p_recv, c_send, c_recv)
    orb, core, partner, chip = _place()
    rounded = total.astype(sendbuf.dtype)
    sendbuf[...] = rounded
    sends = []
    for j in range(1, nchip):
        dst = lax.rem(chip + j, nchip)
        cp = _remote(sendbuf, half.at[chip], g_send.at[j], g_recv.at[chip], 2 * dst + core, orb)
        cp.start()
        sends.append(cp)
    cp = _remote(sendbuf, other.at[chip], h_send.at[0], h_recv.at[chip], partner, orb)
    cp.start()
    sends.append(cp)
    out_ref[chip, core] = rounded
    for j in range(1, nchip):
        src = lax.rem(chip + nchip - j, nchip)
        _remote(sendbuf, half.at[src], g_send.at[j], g_recv.at[src], 2 * src + core, orb).wait_recv()
        cp = _remote(half.at[src], other.at[src], h_send.at[j], h_recv.at[src], partner, orb)
        cp.start()
        sends.append(cp)
        out_ref[src, core] = half[src]
    for j in range(nchip):
        src = lax.rem(chip + nchip - j, nchip)
        _remote(sendbuf, other.at[src], h_send.at[j], h_recv.at[src], partner, orb).wait_recv()
        out_ref[src, 1 - core] = other[src]
    for cp in sends:
        cp.wait_send()


def _two_level_scratch(nchip, rows, cols):
    return [
        pltpu.VMEM((nchip, rows, cols), jnp.float32),
        pltpu.VMEM((nchip, rows, cols), jnp.float32),
        pltpu.VMEM((nchip, rows, cols), jnp.float32),
    ]


def allreduce_to_bf16(partial, n):
    rows, cols = partial.shape
    nchip = n // 2
    chunk = rows // n
    x = partial.reshape(nchip, 2, chunk, cols)
    out = pl.pallas_call(
        functools.partial(allreduce_kernel, nchip),
        out_shape=jax.ShapeDtypeStruct((nchip, 2, chunk, cols), jnp.bfloat16),
        in_specs=[pl.BlockSpec(memory_space=pltpu.VMEM)],
        out_specs=pl.BlockSpec(memory_space=pltpu.VMEM),
        scratch_shapes=_two_level_scratch(nchip, chunk, cols) + [
            pltpu.VMEM((chunk, cols), jnp.bfloat16),
            pltpu.VMEM((nchip, chunk, cols), jnp.bfloat16),
            pltpu.VMEM((nchip, chunk, cols), jnp.bfloat16),
        ] + [pltpu.SemaphoreType.DMA((nchip,))] * 8,
        compiler_params=pltpu.CompilerParams(
            collective_id=0, has_side_effects=True, vmem_limit_bytes=12 * 1024 * 1024
        ),
        cost_estimate=pl.CostEstimate(flops=0, bytes_accessed=64 * x.size, transcendentals=0),
    )(x)
    return out.reshape(rows, cols)


def dipole_kernel(nchip, chunk, count, x_ref, out_ref, pair_recv, part, chip_recv,
                  p_send, p_recv, c_send, c_recv):
    total = _two_level_sum(nchip, x_ref, pair_recv, part, chip_recv, p_send, p_recv, c_send, c_recv)
    squares = total[chunk:chunk + 1, :]
    col_norm = 1.0 / jnp.sqrt(squares / count + 1e-06)
    out_ref[...] = (total[:chunk, :] * col_norm).astype(out_ref.dtype)


def dipole_scatter(partial, squares, n, count):
    rows, cols = partial.shape
    nchip = n // 2
    chunk = rows // n
    x = jnp.concatenate(
        [
            partial.reshape(nchip, 2, chunk, cols),
            jnp.broadcast_to(squares[None, None, None, :], (nchip, 2, 8, cols)),
        ],
        axis=2,
    )
    return pl.pallas_call(
        functools.partial(dipole_kernel, nchip, chunk, count),
        out_shape=jax.ShapeDtypeStruct((chunk, cols), jnp.bfloat16),
        in_specs=[pl.BlockSpec(memory_space=pltpu.VMEM)],
        out_specs=pl.BlockSpec(memory_space=pltpu.VMEM),
        scratch_shapes=_two_level_scratch(nchip, chunk + 8, cols)
        + [pltpu.SemaphoreType.DMA((nchip,))] * 4,
        compiler_params=pltpu.CompilerParams(
            collective_id=1, has_side_effects=True, vmem_limit_bytes=12 * 1024 * 1024
        ),
        cost_estimate=pl.CostEstimate(flops=0, bytes_accessed=32 * x.size, transcendentals=0),
    )(x)


def on_device(cont_orbitals, target_orbitals, margin_blocks, dipole_blocks, band_offsets):
    n = lax.axis_size("basis")
    count = band_offsets.shape[0] * BK * n
    cont_padded = with_halo(cont_orbitals, 2)
    margin_cont = band_local(margin_blocks, band_offsets, cont_padded)
    partial_proj = lax.dot_general(
        target_orbitals, margin_cont, (((0,), (0,)), ((), ())), preferred_element_type=jnp.float32
    )
    projection_b = allreduce_to_bf16(partial_proj, n)
    removed = jnp.dot(target_orbitals, projection_b, preferred_element_type=jnp.float32)
    cont_orth = (cont_orbitals.astype(jnp.float32) - removed).astype(jnp.bfloat16)
    squares = jnp.sum(jnp.square(cont_orth.astype(jnp.float32)), axis=0)
    orth_padded = with_halo(cont_orth, 3)
    dipole_cont = band_local(dipole_blocks, band_offsets, orth_padded)
    partial_dip = lax.dot_general(
        target_orbitals,
        dipole_cont,
        (((0,), (0,)), ((), ())),
        preferred_element_type=jnp.float32,
    )
    dipole_mo = dipole_scatter(partial_dip, squares, n, count)
    return (cont_orth, dipole_mo)


def solution(mesh):
    return jax.shard_map(
        on_device,
        mesh=mesh,
        in_specs=(
            P("basis", "orb"),
            P("basis", None),
            P("basis", None, None, None),
            P("basis", None, None, None),
            P("basis", None),
        ),
        out_specs=(P("basis", "orb"), P("basis", "orb")),
        check_vma=False,
    )
```

```python
import functools

import jax
import jax.numpy as jnp
from jax import lax
from jax.experimental import pallas as pl
from jax.experimental.pallas import tpu as pltpu
from jax.sharding import PartitionSpec as P

BK = 256
KB = 4
MESH = pl.DeviceIdType.MESH


def padded_2(block, sides, width):
    for axis, dim in sides:
        count = lax.axis_size(axis)
        forward = [(i, i + 1) for i in range(count - 1)]
        backward = [(target, source) for source, target in forward]
        low = lax.ppermute(
            lax.slice_in_dim(block, block.shape[dim] - width, None, axis=dim), axis, forward
        )
        high = lax.ppermute(lax.slice_in_dim(block, 0, width, axis=dim), axis, backward)
        block = jnp.concatenate([low, block, high], axis=dim)
    return block


def halo_kernel(n, field_ref, out_ref, low, high, send_sem, recv_sem, copy_sem):
    rows, width = field_ref.shape
    edge = 2 * BK
    me = lax.axis_index("basis")
    orb = lax.axis_index("orb")
    has_low = me > 0
    has_high = me < n - 1
    middle = pltpu.make_async_copy(field_ref, out_ref.at[pl.ds(edge, rows)], copy_sem.at[0])
    middle.start()
    barrier = pltpu.get_barrier_semaphore()

    @pl.when(has_low)
    def _():
        pl.semaphore_signal(barrier, inc=1, device_id=(me - 1, orb), device_id_type=MESH)

    @pl.when(has_high)
    def _():
        pl.semaphore_signal(barrier, inc=1, device_id=(me + 1, orb), device_id_type=MESH)

    pl.semaphore_wait(barrier, has_low.astype(jnp.int32) + has_high.astype(jnp.int32))
    to_low = pltpu.make_async_remote_copy(
        src_ref=field_ref.at[pl.ds(0, edge)], dst_ref=high,
        send_sem=send_sem.at[0], recv_sem=recv_sem.at[0],
        device_id=(jnp.maximum(me - 1, 0), orb), device_id_type=MESH,
    )
    to_high = pltpu.make_async_remote_copy(
        src_ref=field_ref.at[pl.ds(rows - edge, edge)], dst_ref=low,
        send_sem=send_sem.at[1], recv_sem=recv_sem.at[1],
        device_id=(jnp.minimum(me + 1, n - 1), orb), device_id_type=MESH,
    )

    @pl.when(has_low)
    def _():
        to_low.start()

    @pl.when(has_high)
    def _():
        to_high.start()

    @pl.when(has_high)
    def _():
        to_low.wait_recv()
        out_ref[pl.ds(rows + edge, edge), :] = high[...]

    @pl.when(jnp.logical_not(has_high))
    def _():
        out_ref[pl.ds(rows + edge, edge), :] = jnp.zeros((edge, width), out_ref.dtype)

    @pl.when(has_low)
    def _():
        to_high.wait_recv()
        out_ref[pl.ds(0, edge), :] = low[...]

    @pl.when(jnp.logical_not(has_low))
    def _():
        out_ref[pl.ds(0, edge), :] = jnp.zeros((edge, width), out_ref.dtype)

    @pl.when(has_low)
    def _():
        to_low.wait_send()

    @pl.when(has_high)
    def _():
        to_high.wait_send()

    middle.wait()


def with_halo(field, collective_id):
    rows, width = field.shape
    n = lax.axis_size("basis")
    return pl.pallas_call(
        functools.partial(halo_kernel, n),
        out_shape=jax.ShapeDtypeStruct((rows + 4 * BK, width), field.dtype),
        in_specs=[pl.BlockSpec(memory_space=pltpu.VMEM)],
        out_specs=pl.BlockSpec(memory_space=pltpu.VMEM),
        scratch_shapes=[
            pltpu.VMEM((2 * BK, width), field.dtype),
            pltpu.VMEM((2 * BK, width), field.dtype),
            pltpu.SemaphoreType.DMA((2,)),
            pltpu.SemaphoreType.DMA((2,)),
            pltpu.SemaphoreType.DMA((1,)),
        ],
        cost_estimate=pl.CostEstimate(flops=0, bytes_accessed=4 * field.size * 2, transcendentals=0),
        compiler_params=pltpu.CompilerParams(
            collective_id=collective_id, has_side_effects=True, vmem_limit_bytes=8 * 1024 * 1024
        ),
    )(field)


def orth_halo_kernel(n, tgt_ref, proj_ref, cont_ref, orth_ref, pad_ref, sq_ref, low, high, send_sem, recv_sem):
    rows, width = cont_ref.shape
    edge = 2 * BK
    me = lax.axis_index("basis")
    orb = lax.axis_index("orb")
    has_low = me > 0
    has_high = me < n - 1
    barrier = pltpu.get_barrier_semaphore()

    @pl.when(has_low)
    def _():
        pl.semaphore_signal(barrier, inc=1, device_id=(me - 1, orb), device_id_type=MESH)

    @pl.when(has_high)
    def _():
        pl.semaphore_signal(barrier, inc=1, device_id=(me + 1, orb), device_id_type=MESH)

    def tile(start):
        removed = jnp.dot(tgt_ref[pl.ds(start, edge), :], proj_ref[...], preferred_element_type=jnp.float32)
        orth = (cont_ref[pl.ds(start, edge), :].astype(jnp.float32) - removed).astype(orth_ref.dtype)
        orth_ref[pl.ds(start, edge), :] = orth
        pad_ref[pl.ds(start + edge, edge), :] = orth
        wide = orth.astype(jnp.float32)
        return jnp.sum(wide * wide, axis=0, keepdims=True)

    squares = tile(0) + tile(rows - edge)
    pl.semaphore_wait(barrier, has_low.astype(jnp.int32) + has_high.astype(jnp.int32))
    to_low = pltpu.make_async_remote_copy(
        src_ref=orth_ref.at[pl.ds(0, edge)], dst_ref=high,
        send_sem=send_sem.at[0], recv_sem=recv_sem.at[0],
        device_id=(jnp.maximum(me - 1, 0), orb), device_id_type=MESH,
    )
    to_high = pltpu.make_async_remote_copy(
        src_ref=orth_ref.at[pl.ds(rows - edge, edge)], dst_ref=low,
        send_sem=send_sem.at[1], recv_sem=recv_sem.at[1],
        device_id=(jnp.minimum(me + 1, n - 1), orb), device_id_type=MESH,
    )

    @pl.when(has_low)
    def _():
        to_low.start()

    @pl.when(has_high)
    def _():
        to_high.start()

    for start in range(edge, rows - edge, edge):
        squares = squares + tile(start)
    sq_ref[...] = squares

    @pl.when(has_high)
    def _():
        to_low.wait_recv()
        pad_ref[pl.ds(rows + edge, edge), :] = high[...]

    @pl.when(jnp.logical_not(has_high))
    def _():
        pad_ref[pl.ds(rows + edge, edge), :] = jnp.zeros((edge, width), pad_ref.dtype)

    @pl.when(has_low)
    def _():
        to_high.wait_recv()
        pad_ref[pl.ds(0, edge), :] = low[...]

    @pl.when(jnp.logical_not(has_low))
    def _():
        pad_ref[pl.ds(0, edge), :] = jnp.zeros((edge, width), pad_ref.dtype)

    @pl.when(has_low)
    def _():
        to_low.wait_send()

    @pl.when(has_high)
    def _():
        to_high.wait_send()


def orthogonalize_with_halo(target, projection_b, cont, collective_id):
    rows, nt = target.shape
    width = cont.shape[1]
    n = lax.axis_size("basis")
    vmem = pl.BlockSpec(memory_space=pltpu.VMEM)
    orth, padded, squares = pl.pallas_call(
        functools.partial(orth_halo_kernel, n),
        out_shape=(
            jax.ShapeDtypeStruct((rows, width), jnp.bfloat16),
            jax.ShapeDtypeStruct((rows + 4 * BK, width), jnp.bfloat16),
            jax.ShapeDtypeStruct((1, width), jnp.float32),
        ),
        in_specs=[vmem, vmem, vmem],
        out_specs=(vmem, vmem, vmem),
        scratch_shapes=[
            pltpu.VMEM((2 * BK, width), jnp.bfloat16),
            pltpu.VMEM((2 * BK, width), jnp.bfloat16),
            pltpu.SemaphoreType.DMA((2,)),
            pltpu.SemaphoreType.DMA((2,)),
        ],
        cost_estimate=pl.CostEstimate(
            flops=2 * rows * nt * width,
            bytes_accessed=target.size * 2 + projection_b.size * 2 + 3 * cont.size * 2,
            transcendentals=0,
        ),
        compiler_params=pltpu.CompilerParams(
            collective_id=collective_id, has_side_effects=True, vmem_limit_bytes=24 * 1024 * 1024
        ),
    )(target, projection_b, cont)
    return orth, padded, squares[0]


def band_kernel(rows_per_step, off_ref, blk_ref, field_ref, out_ref):
    g = pl.program_id(0)
    for r in range(rows_per_step):
        b = g * rows_per_step + r
        acc = None
        for k in range(KB):
            start = pl.multiple_of((b + 2 + off_ref[b, k]) * BK, BK)
            term = jnp.dot(
                blk_ref[r, k], field_ref[pl.ds(start, BK), :], preferred_element_type=jnp.float32
            )
            acc = term if acc is None else acc + term
        out_ref[pl.ds(r * BK, BK), :] = acc.astype(out_ref.dtype)


def band_local(blocks, offsets, padded):
    nblk = blocks.shape[0]
    rows, width = padded.shape
    per = 8 if nblk % 8 == 0 else 1
    return pl.pallas_call(
        functools.partial(band_kernel, per),
        out_shape=jax.ShapeDtypeStruct((nblk * BK, width), jnp.bfloat16),
        grid_spec=pltpu.PrefetchScalarGridSpec(
            num_scalar_prefetch=1,
            grid=(nblk // per,),
            in_specs=[
                pl.BlockSpec((per, KB, BK, BK), lambda g, off: (g, 0, 0, 0)),
                pl.BlockSpec((rows, width), lambda g, off: (0, 0)),
            ],
            out_specs=pl.BlockSpec((per * BK, width), lambda g, off: (g, 0)),
        ),
        cost_estimate=pl.CostEstimate(
            flops=2 * nblk * KB * BK * BK * width,
            bytes_accessed=blocks.size * 2 + padded.size * 2 + nblk * BK * width * 2,
            transcendentals=0,
        ),
        compiler_params=pltpu.CompilerParams(vmem_limit_bytes=24 * 1024 * 1024),
    )(offsets, blocks, padded)


def _place():
    me = lax.axis_index("basis")
    orb = lax.axis_index("orb")
    core = lax.rem(me, 2)
    partner = me + 1 - 2 * core
    chip = lax.div(me, 2)
    return orb, core, partner, chip


def _barrier_group(nchip, orb, core, partner, chip):
    barrier = pltpu.get_barrier_semaphore()
    pl.semaphore_signal(barrier, inc=1, device_id=(partner, orb), device_id_type=MESH)
    for j in range(1, nchip):
        peer = 2 * lax.rem(chip + j, nchip) + core
        pl.semaphore_signal(barrier, inc=1, device_id=(peer, orb), device_id_type=MESH)
    pl.semaphore_wait(barrier, nchip)


def _remote(src, dst, ssem, rsem, device, orb):
    return pltpu.make_async_remote_copy(
        src_ref=src, dst_ref=dst, send_sem=ssem, recv_sem=rsem,
        device_id=(device, orb), device_id_type=MESH,
    )


def _two_level_sum(nchip, x_ref, pair_recv, part, chip_recv, p_send, p_recv, c_send, c_recv):
    orb, core, partner, chip = _place()
    _barrier_group(nchip, orb, core, partner, chip)
    pair = []
    for j in list(range(1, nchip)) + [0]:
        dst = lax.rem(chip + j, nchip)
        cp = _remote(x_ref.at[dst, 1 - core], pair_recv.at[dst], p_send.at[j], p_recv.at[dst], partner, orb)
        cp.start()
        pair.append(cp)
    sends = []
    for j in range(1, nchip):
        dst = lax.rem(chip + j, nchip)
        pair[j - 1].wait_recv()
        part[dst] = x_ref[dst, core] + pair_recv[dst]
        cp = _remote(part.at[dst], chip_recv.at[chip], c_send.at[j], c_recv.at[chip], 2 * dst + core, orb)
        cp.start()
        sends.append(cp)
    pair[-1].wait_recv()
    total = x_ref[chip, core] + pair_recv[chip]
    for j in range(1, nchip):
        src = lax.rem(chip + nchip - j, nchip)
        _remote(part.at[src], chip_recv.at[src], c_send.at[j], c_recv.at[src], 2 * src + core, orb).wait_recv()
        total = total + chip_recv[src]
    for cp in pair + sends:
        cp.wait_send()
    return total


def allreduce_kernel(nchip, x_ref, out_ref, pair_recv, part, chip_recv, sendbuf, half, other,
                     p_send, p_recv, c_send, c_recv, g_send, g_recv, h_send, h_recv):
    total = _two_level_sum(nchip, x_ref, pair_recv, part, chip_recv, p_send, p_recv, c_send, c_recv)
    orb, core, partner, chip = _place()
    rounded = total.astype(sendbuf.dtype)
    sendbuf[...] = rounded
    sends = []
    for j in range(1, nchip):
        dst = lax.rem(chip + j, nchip)
        cp = _remote(sendbuf, half.at[chip], g_send.at[j], g_recv.at[chip], 2 * dst + core, orb)
        cp.start()
        sends.append(cp)
    cp = _remote(sendbuf, other.at[chip], h_send.at[0], h_recv.at[chip], partner, orb)
    cp.start()
    sends.append(cp)
    out_ref[chip, core] = rounded
    for j in range(1, nchip):
        src = lax.rem(chip + nchip - j, nchip)
        _remote(sendbuf, half.at[src], g_send.at[j], g_recv.at[src], 2 * src + core, orb).wait_recv()
        cp = _remote(half.at[src], other.at[src], h_send.at[j], h_recv.at[src], partner, orb)
        cp.start()
        sends.append(cp)
        out_ref[src, core] = half[src]
    for j in range(nchip):
        src = lax.rem(chip + nchip - j, nchip)
        _remote(sendbuf, other.at[src], h_send.at[j], h_recv.at[src], partner, orb).wait_recv()
        out_ref[src, 1 - core] = other[src]
    for cp in sends:
        cp.wait_send()


def _two_level_scratch(nchip, rows, cols):
    return [
        pltpu.VMEM((nchip, rows, cols), jnp.float32),
        pltpu.VMEM((nchip, rows, cols), jnp.float32),
        pltpu.VMEM((nchip, rows, cols), jnp.float32),
    ]


def allreduce_to_bf16(partial, n):
    rows, cols = partial.shape
    nchip = n // 2
    chunk = rows // n
    x = partial.reshape(nchip, 2, chunk, cols)
    out = pl.pallas_call(
        functools.partial(allreduce_kernel, nchip),
        out_shape=jax.ShapeDtypeStruct((nchip, 2, chunk, cols), jnp.bfloat16),
        in_specs=[pl.BlockSpec(memory_space=pltpu.VMEM)],
        out_specs=pl.BlockSpec(memory_space=pltpu.VMEM),
        scratch_shapes=_two_level_scratch(nchip, chunk, cols) + [
            pltpu.VMEM((chunk, cols), jnp.bfloat16),
            pltpu.VMEM((nchip, chunk, cols), jnp.bfloat16),
            pltpu.VMEM((nchip, chunk, cols), jnp.bfloat16),
        ] + [pltpu.SemaphoreType.DMA((nchip,))] * 8,
        compiler_params=pltpu.CompilerParams(
            collective_id=0, has_side_effects=True, vmem_limit_bytes=12 * 1024 * 1024
        ),
        cost_estimate=pl.CostEstimate(flops=0, bytes_accessed=64 * x.size, transcendentals=0),
    )(x)
    return out.reshape(rows, cols)


def dipole_kernel(nchip, chunk, count, x_ref, out_ref, pair_recv, part, chip_recv,
                  p_send, p_recv, c_send, c_recv):
    total = _two_level_sum(nchip, x_ref, pair_recv, part, chip_recv, p_send, p_recv, c_send, c_recv)
    squares = total[chunk:chunk + 1, :]
    col_norm = 1.0 / jnp.sqrt(squares / count + 1e-06)
    out_ref[...] = (total[:chunk, :] * col_norm).astype(out_ref.dtype)


def dipole_scatter(partial, squares, n, count):
    rows, cols = partial.shape
    nchip = n // 2
    chunk = rows // n
    x = jnp.concatenate(
        [
            partial.reshape(nchip, 2, chunk, cols),
            jnp.broadcast_to(squares[None, None, None, :], (nchip, 2, 8, cols)),
        ],
        axis=2,
    )
    return pl.pallas_call(
        functools.partial(dipole_kernel, nchip, chunk, count),
        out_shape=jax.ShapeDtypeStruct((chunk, cols), jnp.bfloat16),
        in_specs=[pl.BlockSpec(memory_space=pltpu.VMEM)],
        out_specs=pl.BlockSpec(memory_space=pltpu.VMEM),
        scratch_shapes=_two_level_scratch(nchip, chunk + 8, cols)
        + [pltpu.SemaphoreType.DMA((nchip,))] * 4,
        compiler_params=pltpu.CompilerParams(
            collective_id=1, has_side_effects=True, vmem_limit_bytes=12 * 1024 * 1024
        ),
        cost_estimate=pl.CostEstimate(flops=0, bytes_accessed=32 * x.size, transcendentals=0),
    )(x)


def on_device(cont_orbitals, target_orbitals, margin_blocks, dipole_blocks, band_offsets):
    n = lax.axis_size("basis")
    count = band_offsets.shape[0] * BK * n
    cont_padded = with_halo(cont_orbitals, 2)
    margin_cont = band_local(margin_blocks, band_offsets, cont_padded)
    partial_proj = lax.dot_general(
        target_orbitals, margin_cont, (((0,), (0,)), ((), ())), preferred_element_type=jnp.float32
    )
    projection_b = allreduce_to_bf16(partial_proj, n)
    cont_orth, orth_padded, squares = orthogonalize_with_halo(
        target_orbitals, projection_b, cont_orbitals, 3
    )
    dipole_cont = band_local(dipole_blocks, band_offsets, orth_padded)
    partial_dip = lax.dot_general(
        target_orbitals,
        dipole_cont,
        (((0,), (0,)), ((), ())),
        preferred_element_type=jnp.float32,
    )
    dipole_mo = dipole_scatter(partial_dip, squares, n, count)
    return (cont_orth, dipole_mo)


def solution(mesh):
    return jax.shard_map(
        on_device,
        mesh=mesh,
        in_specs=(
            P("basis", "orb"),
            P("basis", None),
            P("basis", None, None, None),
            P("basis", None, None, None),
            P("basis", None),
        ),
        out_specs=(P("basis", "orb"), P("basis", "orb")),
        check_vma=False,
    )
```

```python
import functools

import jax
import jax.numpy as jnp
from jax import lax
from jax.experimental import pallas as pl
from jax.experimental.pallas import tpu as pltpu
from jax.sharding import PartitionSpec as P

BK = 256
KB = 4
MESH = pl.DeviceIdType.MESH


def padded_2(block, sides, width):
    for axis, dim in sides:
        count = lax.axis_size(axis)
        forward = [(i, i + 1) for i in range(count - 1)]
        backward = [(target, source) for source, target in forward]
        low = lax.ppermute(
            lax.slice_in_dim(block, block.shape[dim] - width, None, axis=dim), axis, forward
        )
        high = lax.ppermute(lax.slice_in_dim(block, 0, width, axis=dim), axis, backward)
        block = jnp.concatenate([low, block, high], axis=dim)
    return block


def halo_kernel(n, field_ref, out_ref, low, high, send_sem, recv_sem, copy_sem):
    rows, width = field_ref.shape
    edge = 2 * BK
    me = lax.axis_index("basis")
    orb = lax.axis_index("orb")
    has_low = me > 0
    has_high = me < n - 1
    middle = pltpu.make_async_copy(field_ref, out_ref.at[pl.ds(edge, rows)], copy_sem.at[0])
    middle.start()
    barrier = pltpu.get_barrier_semaphore()

    @pl.when(has_low)
    def _():
        pl.semaphore_signal(barrier, inc=1, device_id=(me - 1, orb), device_id_type=MESH)

    @pl.when(has_high)
    def _():
        pl.semaphore_signal(barrier, inc=1, device_id=(me + 1, orb), device_id_type=MESH)

    pl.semaphore_wait(barrier, has_low.astype(jnp.int32) + has_high.astype(jnp.int32))
    to_low = pltpu.make_async_remote_copy(
        src_ref=field_ref.at[pl.ds(0, edge)], dst_ref=high,
        send_sem=send_sem.at[0], recv_sem=recv_sem.at[0],
        device_id=(jnp.maximum(me - 1, 0), orb), device_id_type=MESH,
    )
    to_high = pltpu.make_async_remote_copy(
        src_ref=field_ref.at[pl.ds(rows - edge, edge)], dst_ref=low,
        send_sem=send_sem.at[1], recv_sem=recv_sem.at[1],
        device_id=(jnp.minimum(me + 1, n - 1), orb), device_id_type=MESH,
    )

    @pl.when(has_low)
    def _():
        to_low.start()

    @pl.when(has_high)
    def _():
        to_high.start()

    @pl.when(has_high)
    def _():
        to_low.wait_recv()
        out_ref[pl.ds(rows + edge, edge), :] = high[...]

    @pl.when(jnp.logical_not(has_high))
    def _():
        out_ref[pl.ds(rows + edge, edge), :] = jnp.zeros((edge, width), out_ref.dtype)

    @pl.when(has_low)
    def _():
        to_high.wait_recv()
        out_ref[pl.ds(0, edge), :] = low[...]

    @pl.when(jnp.logical_not(has_low))
    def _():
        out_ref[pl.ds(0, edge), :] = jnp.zeros((edge, width), out_ref.dtype)

    @pl.when(has_low)
    def _():
        to_low.wait_send()

    @pl.when(has_high)
    def _():
        to_high.wait_send()

    middle.wait()


def with_halo(field, collective_id):
    rows, width = field.shape
    n = lax.axis_size("basis")
    return pl.pallas_call(
        functools.partial(halo_kernel, n),
        out_shape=jax.ShapeDtypeStruct((rows + 4 * BK, width), field.dtype),
        in_specs=[pl.BlockSpec(memory_space=pltpu.VMEM)],
        out_specs=pl.BlockSpec(memory_space=pltpu.VMEM),
        scratch_shapes=[
            pltpu.VMEM((2 * BK, width), field.dtype),
            pltpu.VMEM((2 * BK, width), field.dtype),
            pltpu.SemaphoreType.DMA((2,)),
            pltpu.SemaphoreType.DMA((2,)),
            pltpu.SemaphoreType.DMA((1,)),
        ],
        cost_estimate=pl.CostEstimate(flops=0, bytes_accessed=4 * field.size * 2, transcendentals=0),
        compiler_params=pltpu.CompilerParams(
            collective_id=collective_id, has_side_effects=True, vmem_limit_bytes=8 * 1024 * 1024
        ),
    )(field)


def band_kernel(rows_per_step, off_ref, blk_ref, field_ref, out_ref):
    g = pl.program_id(0)
    for r in range(rows_per_step):
        b = g * rows_per_step + r
        acc = None
        for k in range(KB):
            start = pl.multiple_of((b + 2 + off_ref[b, k]) * BK, BK)
            term = jnp.dot(
                blk_ref[r, k], field_ref[pl.ds(start, BK), :], preferred_element_type=jnp.float32
            )
            acc = term if acc is None else acc + term
        out_ref[pl.ds(r * BK, BK), :] = acc.astype(out_ref.dtype)


def band_local(blocks, offsets, padded):
    nblk = blocks.shape[0]
    rows, width = padded.shape
    per = 8 if nblk % 8 == 0 else 1
    return pl.pallas_call(
        functools.partial(band_kernel, per),
        out_shape=jax.ShapeDtypeStruct((nblk * BK, width), jnp.bfloat16),
        grid_spec=pltpu.PrefetchScalarGridSpec(
            num_scalar_prefetch=1,
            grid=(nblk // per,),
            in_specs=[
                pl.BlockSpec((per, KB, BK, BK), lambda g, off: (g, 0, 0, 0)),
                pl.BlockSpec((rows, width), lambda g, off: (0, 0)),
            ],
            out_specs=pl.BlockSpec((per * BK, width), lambda g, off: (g, 0)),
        ),
        cost_estimate=pl.CostEstimate(
            flops=2 * nblk * KB * BK * BK * width,
            bytes_accessed=blocks.size * 2 + padded.size * 2 + nblk * BK * width * 2,
            transcendentals=0,
        ),
        compiler_params=pltpu.CompilerParams(vmem_limit_bytes=24 * 1024 * 1024),
    )(offsets, blocks, padded)


def _place():
    me = lax.axis_index("basis")
    orb = lax.axis_index("orb")
    core = lax.rem(me, 2)
    partner = me + 1 - 2 * core
    chip = lax.div(me, 2)
    return orb, core, partner, chip


def _barrier_group(nchip, orb, core, partner, chip):
    barrier = pltpu.get_barrier_semaphore()
    pl.semaphore_signal(barrier, inc=1, device_id=(partner, orb), device_id_type=MESH)
    for j in range(1, nchip):
        peer = 2 * lax.rem(chip + j, nchip) + core
        pl.semaphore_signal(barrier, inc=1, device_id=(peer, orb), device_id_type=MESH)
    pl.semaphore_wait(barrier, nchip)


def _remote(src, dst, ssem, rsem, device, orb):
    return pltpu.make_async_remote_copy(
        src_ref=src, dst_ref=dst, send_sem=ssem, recv_sem=rsem,
        device_id=(device, orb), device_id_type=MESH,
    )


def _two_level_sum(nchip, x_ref, pair_recv, part, chip_recv, p_send, p_recv, c_send, c_recv):
    orb, core, partner, chip = _place()
    _barrier_group(nchip, orb, core, partner, chip)
    pair = []
    for j in list(range(1, nchip)) + [0]:
        dst = lax.rem(chip + j, nchip)
        cp = _remote(x_ref.at[dst, 1 - core], pair_recv.at[dst], p_send.at[j], p_recv.at[dst], partner, orb)
        cp.start()
        pair.append(cp)
    sends = []
    for j in range(1, nchip):
        dst = lax.rem(chip + j, nchip)
        pair[j - 1].wait_recv()
        part[dst] = x_ref[dst, core] + pair_recv[dst]
        cp = _remote(part.at[dst], chip_recv.at[chip], c_send.at[j], c_recv.at[chip], 2 * dst + core, orb)
        cp.start()
        sends.append(cp)
    pair[-1].wait_recv()
    total = x_ref[chip, core] + pair_recv[chip]
    for j in range(1, nchip):
        src = lax.rem(chip + nchip - j, nchip)
        _remote(part.at[src], chip_recv.at[src], c_send.at[j], c_recv.at[src], 2 * src + core, orb).wait_recv()
        total = total + chip_recv[src]
    for cp in pair + sends:
        cp.wait_send()
    return total


def allreduce_kernel(nchip, x_ref, out_ref, pair_recv, part, chip_recv, sendbuf, half, other,
                     p_send, p_recv, c_send, c_recv, g_send, g_recv, h_send, h_recv):
    total = _two_level_sum(nchip, x_ref, pair_recv, part, chip_recv, p_send, p_recv, c_send, c_recv)
    orb, core, partner, chip = _place()
    rounded = total.astype(sendbuf.dtype)
    sendbuf[...] = rounded
    sends = []
    for j in range(1, nchip):
        dst = lax.rem(chip + j, nchip)
        cp = _remote(sendbuf, half.at[chip], g_send.at[j], g_recv.at[chip], 2 * dst + core, orb)
        cp.start()
        sends.append(cp)
    cp = _remote(sendbuf, other.at[chip], h_send.at[0], h_recv.at[chip], partner, orb)
    cp.start()
    sends.append(cp)
    out_ref[chip, core] = rounded
    for j in range(1, nchip):
        src = lax.rem(chip + nchip - j, nchip)
        _remote(sendbuf, half.at[src], g_send.at[j], g_recv.at[src], 2 * src + core, orb).wait_recv()
        cp = _remote(half.at[src], other.at[src], h_send.at[j], h_recv.at[src], partner, orb)
        cp.start()
        sends.append(cp)
        out_ref[src, core] = half[src]
    for j in range(nchip):
        src = lax.rem(chip + nchip - j, nchip)
        _remote(sendbuf, other.at[src], h_send.at[j], h_recv.at[src], partner, orb).wait_recv()
        out_ref[src, 1 - core] = other[src]
    for cp in sends:
        cp.wait_send()


def _two_level_scratch(nchip, rows, cols):
    return [
        pltpu.VMEM((nchip, rows, cols), jnp.float32),
        pltpu.VMEM((nchip, rows, cols), jnp.float32),
        pltpu.VMEM((nchip, rows, cols), jnp.float32),
    ]


def allreduce_to_bf16(partial, n):
    rows, cols = partial.shape
    nchip = n // 2
    chunk = rows // n
    x = partial.reshape(nchip, 2, chunk, cols)
    out = pl.pallas_call(
        functools.partial(allreduce_kernel, nchip),
        out_shape=jax.ShapeDtypeStruct((nchip, 2, chunk, cols), jnp.bfloat16),
        in_specs=[pl.BlockSpec(memory_space=pltpu.VMEM)],
        out_specs=pl.BlockSpec(memory_space=pltpu.VMEM),
        scratch_shapes=_two_level_scratch(nchip, chunk, cols) + [
            pltpu.VMEM((chunk, cols), jnp.bfloat16),
            pltpu.VMEM((nchip, chunk, cols), jnp.bfloat16),
            pltpu.VMEM((nchip, chunk, cols), jnp.bfloat16),
        ] + [pltpu.SemaphoreType.DMA((nchip,))] * 8,
        compiler_params=pltpu.CompilerParams(
            collective_id=0, has_side_effects=True, vmem_limit_bytes=12 * 1024 * 1024
        ),
        cost_estimate=pl.CostEstimate(flops=0, bytes_accessed=64 * x.size, transcendentals=0),
    )(x)
    return out.reshape(rows, cols)


def dipole_kernel(nchip, chunk, count, x_ref, out_ref, pair_recv, part, chip_recv,
                  p_send, p_recv, c_send, c_recv):
    total = _two_level_sum(nchip, x_ref, pair_recv, part, chip_recv, p_send, p_recv, c_send, c_recv)
    squares = total[chunk:chunk + 1, :]
    col_norm = 1.0 / jnp.sqrt(squares / count + 1e-06)
    out_ref[...] = (total[:chunk, :] * col_norm).astype(out_ref.dtype)


def dipole_scatter(partial, squares, n, count):
    rows, cols = partial.shape
    nchip = n // 2
    chunk = rows // n
    x = jnp.concatenate(
        [
            partial.reshape(nchip, 2, chunk, cols),
            jnp.broadcast_to(squares[None, None, None, :], (nchip, 2, 8, cols)),
        ],
        axis=2,
    )
    return pl.pallas_call(
        functools.partial(dipole_kernel, nchip, chunk, count),
        out_shape=jax.ShapeDtypeStruct((chunk, cols), jnp.bfloat16),
        in_specs=[pl.BlockSpec(memory_space=pltpu.VMEM)],
        out_specs=pl.BlockSpec(memory_space=pltpu.VMEM),
        scratch_shapes=_two_level_scratch(nchip, chunk + 8, cols)
        + [pltpu.SemaphoreType.DMA((nchip,))] * 4,
        compiler_params=pltpu.CompilerParams(
            collective_id=1, has_side_effects=True, vmem_limit_bytes=12 * 1024 * 1024
        ),
        cost_estimate=pl.CostEstimate(flops=0, bytes_accessed=32 * x.size, transcendentals=0),
    )(x)


def on_device(cont_orbitals, target_orbitals, margin_blocks, dipole_blocks, band_offsets):
    n = lax.axis_size("basis")
    count = band_offsets.shape[0] * BK * n
    cont_padded = with_halo(cont_orbitals, 2)
    margin_cont = band_local(margin_blocks, band_offsets, cont_padded)
    partial_proj_t = lax.dot_general(
        margin_cont, target_orbitals, (((0,), (0,)), ((), ())), preferred_element_type=jnp.float32
    )
    projection_b_t = allreduce_to_bf16(partial_proj_t, n)
    removed = lax.dot_general(
        target_orbitals, projection_b_t, (((1,), (1,)), ((), ())), preferred_element_type=jnp.float32
    )
    cont_orth = (cont_orbitals.astype(jnp.float32) - removed).astype(jnp.bfloat16)
    squares = jnp.sum(jnp.square(cont_orth.astype(jnp.float32)), axis=0)
    orth_padded = with_halo(cont_orth, 3)
    dipole_cont = band_local(dipole_blocks, band_offsets, orth_padded)
    partial_dip = lax.dot_general(
        target_orbitals,
        dipole_cont,
        (((0,), (0,)), ((), ())),
        preferred_element_type=jnp.float32,
    )
    dipole_mo = dipole_scatter(partial_dip, squares, n, count)
    return (cont_orth, dipole_mo)


def solution(mesh):
    return jax.shard_map(
        on_device,
        mesh=mesh,
        in_specs=(
            P("basis", "orb"),
            P("basis", None),
            P("basis", None, None, None),
            P("basis", None, None, None),
            P("basis", None),
        ),
        out_specs=(P("basis", "orb"), P("basis", "orb")),
        check_vma=False,
    )
```

```python
import functools

import jax
import jax.numpy as jnp
from jax import lax
from jax.experimental import pallas as pl
from jax.experimental.pallas import tpu as pltpu
from jax.sharding import PartitionSpec as P

BK = 256
KB = 4
MESH = pl.DeviceIdType.MESH


def padded_2(block, sides, width):
    for axis, dim in sides:
        count = lax.axis_size(axis)
        forward = [(i, i + 1) for i in range(count - 1)]
        backward = [(target, source) for source, target in forward]
        low = lax.ppermute(
            lax.slice_in_dim(block, block.shape[dim] - width, None, axis=dim), axis, forward
        )
        high = lax.ppermute(lax.slice_in_dim(block, 0, width, axis=dim), axis, backward)
        block = jnp.concatenate([low, block, high], axis=dim)
    return block


def halo_kernel(n, field_ref, out_ref, low, high, send_sem, recv_sem, copy_sem):
    rows, width = field_ref.shape
    edge = 2 * BK
    me = lax.axis_index("basis")
    orb = lax.axis_index("orb")
    has_low = me > 0
    has_high = me < n - 1
    middle = pltpu.make_async_copy(field_ref, out_ref.at[pl.ds(edge, rows)], copy_sem.at[0])
    middle.start()
    barrier = pltpu.get_barrier_semaphore()

    @pl.when(has_low)
    def _():
        pl.semaphore_signal(barrier, inc=1, device_id=(me - 1, orb), device_id_type=MESH)

    @pl.when(has_high)
    def _():
        pl.semaphore_signal(barrier, inc=1, device_id=(me + 1, orb), device_id_type=MESH)

    pl.semaphore_wait(barrier, has_low.astype(jnp.int32) + has_high.astype(jnp.int32))
    to_low = pltpu.make_async_remote_copy(
        src_ref=field_ref.at[pl.ds(0, edge)], dst_ref=high,
        send_sem=send_sem.at[0], recv_sem=recv_sem.at[0],
        device_id=(jnp.maximum(me - 1, 0), orb), device_id_type=MESH,
    )
    to_high = pltpu.make_async_remote_copy(
        src_ref=field_ref.at[pl.ds(rows - edge, edge)], dst_ref=low,
        send_sem=send_sem.at[1], recv_sem=recv_sem.at[1],
        device_id=(jnp.minimum(me + 1, n - 1), orb), device_id_type=MESH,
    )

    @pl.when(has_low)
    def _():
        to_low.start()

    @pl.when(has_high)
    def _():
        to_high.start()

    @pl.when(has_high)
    def _():
        to_low.wait_recv()
        out_ref[pl.ds(rows + edge, edge), :] = high[...]

    @pl.when(jnp.logical_not(has_high))
    def _():
        out_ref[pl.ds(rows + edge, edge), :] = jnp.zeros((edge, width), out_ref.dtype)

    @pl.when(has_low)
    def _():
        to_high.wait_recv()
        out_ref[pl.ds(0, edge), :] = low[...]

    @pl.when(jnp.logical_not(has_low))
    def _():
        out_ref[pl.ds(0, edge), :] = jnp.zeros((edge, width), out_ref.dtype)

    @pl.when(has_low)
    def _():
        to_low.wait_send()

    @pl.when(has_high)
    def _():
        to_high.wait_send()

    middle.wait()


def with_halo(field, collective_id):
    rows, width = field.shape
    n = lax.axis_size("basis")
    return pl.pallas_call(
        functools.partial(halo_kernel, n),
        out_shape=jax.ShapeDtypeStruct((rows + 4 * BK, width), field.dtype),
        in_specs=[pl.BlockSpec(memory_space=pltpu.VMEM)],
        out_specs=pl.BlockSpec(memory_space=pltpu.VMEM),
        scratch_shapes=[
            pltpu.VMEM((2 * BK, width), field.dtype),
            pltpu.VMEM((2 * BK, width), field.dtype),
            pltpu.SemaphoreType.DMA((2,)),
            pltpu.SemaphoreType.DMA((2,)),
            pltpu.SemaphoreType.DMA((1,)),
        ],
        cost_estimate=pl.CostEstimate(flops=0, bytes_accessed=4 * field.size * 2, transcendentals=0),
        compiler_params=pltpu.CompilerParams(
            collective_id=collective_id, has_side_effects=True, vmem_limit_bytes=8 * 1024 * 1024
        ),
    )(field)


def orth_halo_kernel(n, tgt_ref, proj_ref, cont_ref, orth_ref, pad_ref, sq_ref, low, high, send_sem, recv_sem):
    rows, width = cont_ref.shape
    edge = 2 * BK
    me = lax.axis_index("basis")
    orb = lax.axis_index("orb")
    has_low = me > 0
    has_high = me < n - 1
    barrier = pltpu.get_barrier_semaphore()

    @pl.when(has_low)
    def _():
        pl.semaphore_signal(barrier, inc=1, device_id=(me - 1, orb), device_id_type=MESH)

    @pl.when(has_high)
    def _():
        pl.semaphore_signal(barrier, inc=1, device_id=(me + 1, orb), device_id_type=MESH)

    def tile(start):
        removed = lax.dot_general(
            tgt_ref[pl.ds(start, edge), :], proj_ref[...], (((1,), (1,)), ((), ())),
            preferred_element_type=jnp.float32,
        )
        orth = (cont_ref[pl.ds(start, edge), :].astype(jnp.float32) - removed).astype(orth_ref.dtype)
        orth_ref[pl.ds(start, edge), :] = orth
        pad_ref[pl.ds(start + edge, edge), :] = orth
        wide = orth.astype(jnp.float32)
        return jnp.sum(wide * wide, axis=0, keepdims=True)

    squares = tile(0) + tile(rows - edge)
    pl.semaphore_wait(barrier, has_low.astype(jnp.int32) + has_high.astype(jnp.int32))
    to_low = pltpu.make_async_remote_copy(
        src_ref=orth_ref.at[pl.ds(0, edge)], dst_ref=high,
        send_sem=send_sem.at[0], recv_sem=recv_sem.at[0],
        device_id=(jnp.maximum(me - 1, 0), orb), device_id_type=MESH,
    )
    to_high = pltpu.make_async_remote_copy(
        src_ref=orth_ref.at[pl.ds(rows - edge, edge)], dst_ref=low,
        send_sem=send_sem.at[1], recv_sem=recv_sem.at[1],
        device_id=(jnp.minimum(me + 1, n - 1), orb), device_id_type=MESH,
    )

    @pl.when(has_low)
    def _():
        to_low.start()

    @pl.when(has_high)
    def _():
        to_high.start()

    for start in range(edge, rows - edge, edge):
        squares = squares + tile(start)
    sq_ref[...] = squares

    @pl.when(has_high)
    def _():
        to_low.wait_recv()
        pad_ref[pl.ds(rows + edge, edge), :] = high[...]

    @pl.when(jnp.logical_not(has_high))
    def _():
        pad_ref[pl.ds(rows + edge, edge), :] = jnp.zeros((edge, width), pad_ref.dtype)

    @pl.when(has_low)
    def _():
        to_high.wait_recv()
        pad_ref[pl.ds(0, edge), :] = low[...]

    @pl.when(jnp.logical_not(has_low))
    def _():
        pad_ref[pl.ds(0, edge), :] = jnp.zeros((edge, width), pad_ref.dtype)

    @pl.when(has_low)
    def _():
        to_low.wait_send()

    @pl.when(has_high)
    def _():
        to_high.wait_send()


def orthogonalize_with_halo(target, projection_b, cont, collective_id):
    rows, nt = target.shape
    width = cont.shape[1]
    n = lax.axis_size("basis")
    vmem = pl.BlockSpec(memory_space=pltpu.VMEM)
    orth, padded, squares = pl.pallas_call(
        functools.partial(orth_halo_kernel, n),
        out_shape=(
            jax.ShapeDtypeStruct((rows, width), jnp.bfloat16),
            jax.ShapeDtypeStruct((rows + 4 * BK, width), jnp.bfloat16),
            jax.ShapeDtypeStruct((1, width), jnp.float32),
        ),
        in_specs=[vmem, vmem, vmem],
        out_specs=(vmem, vmem, vmem),
        scratch_shapes=[
            pltpu.VMEM((2 * BK, width), jnp.bfloat16),
            pltpu.VMEM((2 * BK, width), jnp.bfloat16),
            pltpu.SemaphoreType.DMA((2,)),
            pltpu.SemaphoreType.DMA((2,)),
        ],
        cost_estimate=pl.CostEstimate(
            flops=2 * rows * nt * width,
            bytes_accessed=target.size * 2 + projection_b.size * 2 + 3 * cont.size * 2,
            transcendentals=0,
        ),
        compiler_params=pltpu.CompilerParams(
            collective_id=collective_id, has_side_effects=True, vmem_limit_bytes=24 * 1024 * 1024
        ),
    )(target, projection_b, cont)
    return orth, padded, squares[0]


def band_kernel(rows_per_step, off_ref, blk_ref, field_ref, out_ref):
    g = pl.program_id(0)
    for r in range(rows_per_step):
        b = g * rows_per_step + r
        acc = None
        for k in range(KB):
            start = pl.multiple_of((b + 2 + off_ref[b, k]) * BK, BK)
            term = jnp.dot(
                blk_ref[r, k], field_ref[pl.ds(start, BK), :], preferred_element_type=jnp.float32
            )
            acc = term if acc is None else acc + term
        out_ref[pl.ds(r * BK, BK), :] = acc.astype(out_ref.dtype)


def band_local(blocks, offsets, padded):
    nblk = blocks.shape[0]
    rows, width = padded.shape
    per = 8 if nblk % 8 == 0 else 1
    return pl.pallas_call(
        functools.partial(band_kernel, per),
        out_shape=jax.ShapeDtypeStruct((nblk * BK, width), jnp.bfloat16),
        grid_spec=pltpu.PrefetchScalarGridSpec(
            num_scalar_prefetch=1,
            grid=(nblk // per,),
            in_specs=[
                pl.BlockSpec((per, KB, BK, BK), lambda g, off: (g, 0, 0, 0)),
                pl.BlockSpec((rows, width), lambda g, off: (0, 0)),
            ],
            out_specs=pl.BlockSpec((per * BK, width), lambda g, off: (g, 0)),
        ),
        cost_estimate=pl.CostEstimate(
            flops=2 * nblk * KB * BK * BK * width,
            bytes_accessed=blocks.size * 2 + padded.size * 2 + nblk * BK * width * 2,
            transcendentals=0,
        ),
        compiler_params=pltpu.CompilerParams(vmem_limit_bytes=24 * 1024 * 1024),
    )(offsets, blocks, padded)


def _place():
    me = lax.axis_index("basis")
    orb = lax.axis_index("orb")
    core = lax.rem(me, 2)
    partner = me + 1 - 2 * core
    chip = lax.div(me, 2)
    return orb, core, partner, chip


def _barrier_group(nchip, orb, core, partner, chip):
    barrier = pltpu.get_barrier_semaphore()
    pl.semaphore_signal(barrier, inc=1, device_id=(partner, orb), device_id_type=MESH)
    for j in range(1, nchip):
        peer = 2 * lax.rem(chip + j, nchip) + core
        pl.semaphore_signal(barrier, inc=1, device_id=(peer, orb), device_id_type=MESH)
    pl.semaphore_wait(barrier, nchip)


def _remote(src, dst, ssem, rsem, device, orb):
    return pltpu.make_async_remote_copy(
        src_ref=src, dst_ref=dst, send_sem=ssem, recv_sem=rsem,
        device_id=(device, orb), device_id_type=MESH,
    )


def _two_level_sum(nchip, x_ref, pair_recv, part, chip_recv, p_send, p_recv, c_send, c_recv):
    orb, core, partner, chip = _place()
    _barrier_group(nchip, orb, core, partner, chip)
    pair = []
    for j in list(range(1, nchip)) + [0]:
        dst = lax.rem(chip + j, nchip)
        cp = _remote(x_ref.at[dst, 1 - core], pair_recv.at[dst], p_send.at[j], p_recv.at[dst], partner, orb)
        cp.start()
        pair.append(cp)
    sends = []
    for j in range(1, nchip):
        dst = lax.rem(chip + j, nchip)
        pair[j - 1].wait_recv()
        part[dst] = x_ref[dst, core] + pair_recv[dst]
        cp = _remote(part.at[dst], chip_recv.at[chip], c_send.at[j], c_recv.at[chip], 2 * dst + core, orb)
        cp.start()
        sends.append(cp)
    pair[-1].wait_recv()
    total = x_ref[chip, core] + pair_recv[chip]
    for j in range(1, nchip):
        src = lax.rem(chip + nchip - j, nchip)
        _remote(part.at[src], chip_recv.at[src], c_send.at[j], c_recv.at[src], 2 * src + core, orb).wait_recv()
        total = total + chip_recv[src]
    for cp in pair + sends:
        cp.wait_send()
    return total


def allreduce_kernel(nchip, x_ref, out_ref, pair_recv, part, chip_recv, sendbuf, half, other,
                     p_send, p_recv, c_send, c_recv, g_send, g_recv, h_send, h_recv):
    total = _two_level_sum(nchip, x_ref, pair_recv, part, chip_recv, p_send, p_recv, c_send, c_recv)
    orb, core, partner, chip = _place()
    rounded = total.astype(sendbuf.dtype)
    sendbuf[...] = rounded
    sends = []
    for j in range(1, nchip):
        dst = lax.rem(chip + j, nchip)
        cp = _remote(sendbuf, half.at[chip], g_send.at[j], g_recv.at[chip], 2 * dst + core, orb)
        cp.start()
        sends.append(cp)
    cp = _remote(sendbuf, other.at[chip], h_send.at[0], h_recv.at[chip], partner, orb)
    cp.start()
    sends.append(cp)
    out_ref[chip, core] = rounded
    for j in range(1, nchip):
        src = lax.rem(chip + nchip - j, nchip)
        _remote(sendbuf, half.at[src], g_send.at[j], g_recv.at[src], 2 * src + core, orb).wait_recv()
        cp = _remote(half.at[src], other.at[src], h_send.at[j], h_recv.at[src], partner, orb)
        cp.start()
        sends.append(cp)
        out_ref[src, core] = half[src]
    for j in range(nchip):
        src = lax.rem(chip + nchip - j, nchip)
        _remote(sendbuf, other.at[src], h_send.at[j], h_recv.at[src], partner, orb).wait_recv()
        out_ref[src, 1 - core] = other[src]
    for cp in sends:
        cp.wait_send()


def _two_level_scratch(nchip, rows, cols):
    return [
        pltpu.VMEM((nchip, rows, cols), jnp.float32),
        pltpu.VMEM((nchip, rows, cols), jnp.float32),
        pltpu.VMEM((nchip, rows, cols), jnp.float32),
    ]


def allreduce_to_bf16(partial, n):
    rows, cols = partial.shape
    nchip = n // 2
    chunk = rows // n
    x = partial.reshape(nchip, 2, chunk, cols)
    out = pl.pallas_call(
        functools.partial(allreduce_kernel, nchip),
        out_shape=jax.ShapeDtypeStruct((nchip, 2, chunk, cols), jnp.bfloat16),
        in_specs=[pl.BlockSpec(memory_space=pltpu.VMEM)],
        out_specs=pl.BlockSpec(memory_space=pltpu.VMEM),
        scratch_shapes=_two_level_scratch(nchip, chunk, cols) + [
            pltpu.VMEM((chunk, cols), jnp.bfloat16),
            pltpu.VMEM((nchip, chunk, cols), jnp.bfloat16),
            pltpu.VMEM((nchip, chunk, cols), jnp.bfloat16),
        ] + [pltpu.SemaphoreType.DMA((nchip,))] * 8,
        compiler_params=pltpu.CompilerParams(
            collective_id=0, has_side_effects=True, vmem_limit_bytes=12 * 1024 * 1024
        ),
        cost_estimate=pl.CostEstimate(flops=0, bytes_accessed=64 * x.size, transcendentals=0),
    )(x)
    return out.reshape(rows, cols)


def dipole_kernel(nchip, chunk, count, x_ref, out_ref, pair_recv, part, chip_recv,
                  p_send, p_recv, c_send, c_recv):
    total = _two_level_sum(nchip, x_ref, pair_recv, part, chip_recv, p_send, p_recv, c_send, c_recv)
    squares = total[chunk:chunk + 1, :]
    col_norm = 1.0 / jnp.sqrt(squares / count + 1e-06)
    out_ref[...] = (total[:chunk, :] * col_norm).astype(out_ref.dtype)


def dipole_scatter(partial, squares, n, count):
    rows, cols = partial.shape
    nchip = n // 2
    chunk = rows // n
    x = jnp.concatenate(
        [
            partial.reshape(nchip, 2, chunk, cols),
            jnp.broadcast_to(squares[None, None, None, :], (nchip, 2, 8, cols)),
        ],
        axis=2,
    )
    return pl.pallas_call(
        functools.partial(dipole_kernel, nchip, chunk, count),
        out_shape=jax.ShapeDtypeStruct((chunk, cols), jnp.bfloat16),
        in_specs=[pl.BlockSpec(memory_space=pltpu.VMEM)],
        out_specs=pl.BlockSpec(memory_space=pltpu.VMEM),
        scratch_shapes=_two_level_scratch(nchip, chunk + 8, cols)
        + [pltpu.SemaphoreType.DMA((nchip,))] * 4,
        compiler_params=pltpu.CompilerParams(
            collective_id=1, has_side_effects=True, vmem_limit_bytes=12 * 1024 * 1024
        ),
        cost_estimate=pl.CostEstimate(flops=0, bytes_accessed=32 * x.size, transcendentals=0),
    )(x)


def on_device(cont_orbitals, target_orbitals, margin_blocks, dipole_blocks, band_offsets):
    n = lax.axis_size("basis")
    count = band_offsets.shape[0] * BK * n
    cont_padded = with_halo(cont_orbitals, 2)
    margin_cont = band_local(margin_blocks, band_offsets, cont_padded)
    partial_proj_t = lax.dot_general(
        margin_cont, target_orbitals, (((0,), (0,)), ((), ())), preferred_element_type=jnp.float32
    )
    projection_b_t = allreduce_to_bf16(partial_proj_t, n)
    cont_orth, orth_padded, squares = orthogonalize_with_halo(
        target_orbitals, projection_b_t, cont_orbitals, 3
    )
    dipole_cont = band_local(dipole_blocks, band_offsets, orth_padded)
    partial_dip = lax.dot_general(
        target_orbitals,
        dipole_cont,
        (((0,), (0,)), ((), ())),
        preferred_element_type=jnp.float32,
    )
    dipole_mo = dipole_scatter(partial_dip, squares, n, count)
    return (cont_orth, dipole_mo)


def solution(mesh):
    return jax.shard_map(
        on_device,
        mesh=mesh,
        in_specs=(
            P("basis", "orb"),
            P("basis", None),
            P("basis", None, None, None),
            P("basis", None, None, None),
            P("basis", None),
        ),
        out_specs=(P("basis", "orb"), P("basis", "orb")),
        check_vma=False,
    )
```

```python
import functools

import jax
import jax.numpy as jnp
from jax import lax
from jax.experimental import pallas as pl
from jax.experimental.pallas import tpu as pltpu
from jax.sharding import PartitionSpec as P

BK = 256
KB = 4
MESH = pl.DeviceIdType.MESH


def padded_2(block, sides, width):
    for axis, dim in sides:
        count = lax.axis_size(axis)
        forward = [(i, i + 1) for i in range(count - 1)]
        backward = [(target, source) for source, target in forward]
        low = lax.ppermute(
            lax.slice_in_dim(block, block.shape[dim] - width, None, axis=dim), axis, forward
        )
        high = lax.ppermute(lax.slice_in_dim(block, 0, width, axis=dim), axis, backward)
        block = jnp.concatenate([low, block, high], axis=dim)
    return block


def halo_kernel(n, field_ref, out_ref, low, high, send_sem, recv_sem, copy_sem):
    rows, width = field_ref.shape
    edge = 2 * BK
    me = lax.axis_index("basis")
    orb = lax.axis_index("orb")
    has_low = me > 0
    has_high = me < n - 1
    middle = pltpu.make_async_copy(field_ref, out_ref.at[pl.ds(edge, rows)], copy_sem.at[0])
    middle.start()
    barrier = pltpu.get_barrier_semaphore()

    @pl.when(has_low)
    def _():
        pl.semaphore_signal(barrier, inc=1, device_id=(me - 1, orb), device_id_type=MESH)

    @pl.when(has_high)
    def _():
        pl.semaphore_signal(barrier, inc=1, device_id=(me + 1, orb), device_id_type=MESH)

    pl.semaphore_wait(barrier, has_low.astype(jnp.int32) + has_high.astype(jnp.int32))
    to_low = pltpu.make_async_remote_copy(
        src_ref=field_ref.at[pl.ds(0, edge)], dst_ref=high,
        send_sem=send_sem.at[0], recv_sem=recv_sem.at[0],
        device_id=(jnp.maximum(me - 1, 0), orb), device_id_type=MESH,
    )
    to_high = pltpu.make_async_remote_copy(
        src_ref=field_ref.at[pl.ds(rows - edge, edge)], dst_ref=low,
        send_sem=send_sem.at[1], recv_sem=recv_sem.at[1],
        device_id=(jnp.minimum(me + 1, n - 1), orb), device_id_type=MESH,
    )

    @pl.when(has_low)
    def _():
        to_low.start()

    @pl.when(has_high)
    def _():
        to_high.start()

    @pl.when(has_high)
    def _():
        to_low.wait_recv()
        out_ref[pl.ds(rows + edge, edge), :] = high[...]

    @pl.when(jnp.logical_not(has_high))
    def _():
        out_ref[pl.ds(rows + edge, edge), :] = jnp.zeros((edge, width), out_ref.dtype)

    @pl.when(has_low)
    def _():
        to_high.wait_recv()
        out_ref[pl.ds(0, edge), :] = low[...]

    @pl.when(jnp.logical_not(has_low))
    def _():
        out_ref[pl.ds(0, edge), :] = jnp.zeros((edge, width), out_ref.dtype)

    @pl.when(has_low)
    def _():
        to_low.wait_send()

    @pl.when(has_high)
    def _():
        to_high.wait_send()

    middle.wait()


def with_halo(field, collective_id):
    rows, width = field.shape
    n = lax.axis_size("basis")
    return pl.pallas_call(
        functools.partial(halo_kernel, n),
        out_shape=jax.ShapeDtypeStruct((rows + 4 * BK, width), field.dtype),
        in_specs=[pl.BlockSpec(memory_space=pltpu.VMEM)],
        out_specs=pl.BlockSpec(memory_space=pltpu.VMEM),
        scratch_shapes=[
            pltpu.VMEM((2 * BK, width), field.dtype),
            pltpu.VMEM((2 * BK, width), field.dtype),
            pltpu.SemaphoreType.DMA((2,)),
            pltpu.SemaphoreType.DMA((2,)),
            pltpu.SemaphoreType.DMA((1,)),
        ],
        cost_estimate=pl.CostEstimate(flops=0, bytes_accessed=4 * field.size * 2, transcendentals=0),
        compiler_params=pltpu.CompilerParams(
            collective_id=collective_id, has_side_effects=True, vmem_limit_bytes=8 * 1024 * 1024
        ),
    )(field)


def orth_halo_kernel(n, tgt_ref, proj_ref, cont_ref, pad_ref, sq_ref, orth_ref, low, high, send_sem, recv_sem):
    rows, width = cont_ref.shape
    edge = 2 * BK
    me = lax.axis_index("basis")
    orb = lax.axis_index("orb")
    has_low = me > 0
    has_high = me < n - 1
    barrier = pltpu.get_barrier_semaphore()

    @pl.when(has_low)
    def _():
        pl.semaphore_signal(barrier, inc=1, device_id=(me - 1, orb), device_id_type=MESH)

    @pl.when(has_high)
    def _():
        pl.semaphore_signal(barrier, inc=1, device_id=(me + 1, orb), device_id_type=MESH)

    def tile(start):
        removed = lax.dot_general(
            tgt_ref[pl.ds(start, edge), :], proj_ref[...], (((1,), (1,)), ((), ())),
            preferred_element_type=jnp.float32,
        )
        orth = (cont_ref[pl.ds(start, edge), :].astype(jnp.float32) - removed).astype(orth_ref.dtype)
        orth_ref[pl.ds(start, edge), :] = orth
        pad_ref[pl.ds(start + edge, edge), :] = orth
        wide = orth.astype(jnp.float32)
        return jnp.sum(wide * wide, axis=0, keepdims=True)

    squares = tile(0) + tile(rows - edge)
    pl.semaphore_wait(barrier, has_low.astype(jnp.int32) + has_high.astype(jnp.int32))
    to_low = pltpu.make_async_remote_copy(
        src_ref=orth_ref.at[pl.ds(0, edge)], dst_ref=high,
        send_sem=send_sem.at[0], recv_sem=recv_sem.at[0],
        device_id=(jnp.maximum(me - 1, 0), orb), device_id_type=MESH,
    )
    to_high = pltpu.make_async_remote_copy(
        src_ref=orth_ref.at[pl.ds(rows - edge, edge)], dst_ref=low,
        send_sem=send_sem.at[1], recv_sem=recv_sem.at[1],
        device_id=(jnp.minimum(me + 1, n - 1), orb), device_id_type=MESH,
    )

    @pl.when(has_low)
    def _():
        to_low.start()

    @pl.when(has_high)
    def _():
        to_high.start()

    for start in range(edge, rows - edge, edge):
        squares = squares + tile(start)
    sq_ref[...] = squares

    @pl.when(has_high)
    def _():
        to_low.wait_recv()
        pad_ref[pl.ds(rows + edge, edge), :] = high[...]

    @pl.when(jnp.logical_not(has_high))
    def _():
        pad_ref[pl.ds(rows + edge, edge), :] = jnp.zeros((edge, width), pad_ref.dtype)

    @pl.when(has_low)
    def _():
        to_high.wait_recv()
        pad_ref[pl.ds(0, edge), :] = low[...]

    @pl.when(jnp.logical_not(has_low))
    def _():
        pad_ref[pl.ds(0, edge), :] = jnp.zeros((edge, width), pad_ref.dtype)

    @pl.when(has_low)
    def _():
        to_low.wait_send()

    @pl.when(has_high)
    def _():
        to_high.wait_send()


def orthogonalize_with_halo(target, projection_b, cont, collective_id):
    rows, nt = target.shape
    width = cont.shape[1]
    n = lax.axis_size("basis")
    vmem = pl.BlockSpec(memory_space=pltpu.VMEM)
    padded, squares = pl.pallas_call(
        functools.partial(orth_halo_kernel, n),
        out_shape=(
            jax.ShapeDtypeStruct((rows + 4 * BK, width), jnp.bfloat16),
            jax.ShapeDtypeStruct((1, width), jnp.float32),
        ),
        in_specs=[vmem, vmem, vmem],
        out_specs=(vmem, vmem),
        scratch_shapes=[
            pltpu.VMEM((rows, width), jnp.bfloat16),
            pltpu.VMEM((2 * BK, width), jnp.bfloat16),
            pltpu.VMEM((2 * BK, width), jnp.bfloat16),
            pltpu.SemaphoreType.DMA((2,)),
            pltpu.SemaphoreType.DMA((2,)),
        ],
        cost_estimate=pl.CostEstimate(
            flops=2 * rows * nt * width,
            bytes_accessed=target.size * 2 + projection_b.size * 2 + 3 * cont.size * 2,
            transcendentals=0,
        ),
        compiler_params=pltpu.CompilerParams(
            collective_id=collective_id, has_side_effects=True, vmem_limit_bytes=24 * 1024 * 1024
        ),
    )(target, projection_b, cont)
    return padded, squares[0]


def band_kernel(rows_per_step, off_ref, blk_ref, field_ref, out_ref, *mid):
    g = pl.program_id(0)
    if mid:
        start = pl.multiple_of((g * rows_per_step + 2) * BK, BK)
        mid[0][...] = field_ref[pl.ds(start, rows_per_step * BK), :]
    for r in range(rows_per_step):
        b = g * rows_per_step + r
        acc = None
        for k in range(KB):
            start = pl.multiple_of((b + 2 + off_ref[b, k]) * BK, BK)
            term = jnp.dot(
                blk_ref[r, k], field_ref[pl.ds(start, BK), :], preferred_element_type=jnp.float32
            )
            acc = term if acc is None else acc + term
        out_ref[pl.ds(r * BK, BK), :] = acc.astype(out_ref.dtype)


def band_local(blocks, offsets, padded, with_middle=False):
    nblk = blocks.shape[0]
    rows, width = padded.shape
    per = 8 if nblk % 8 == 0 else 1
    field = jax.ShapeDtypeStruct((nblk * BK, width), jnp.bfloat16)
    spec = pl.BlockSpec((per * BK, width), lambda g, off: (g, 0))
    return pl.pallas_call(
        functools.partial(band_kernel, per),
        out_shape=(field, field) if with_middle else field,
        grid_spec=pltpu.PrefetchScalarGridSpec(
            num_scalar_prefetch=1,
            grid=(nblk // per,),
            in_specs=[
                pl.BlockSpec((per, KB, BK, BK), lambda g, off: (g, 0, 0, 0)),
                pl.BlockSpec((rows, width), lambda g, off: (0, 0)),
            ],
            out_specs=(spec, spec) if with_middle else spec,
        ),
        cost_estimate=pl.CostEstimate(
            flops=2 * nblk * KB * BK * BK * width,
            bytes_accessed=blocks.size * 2 + padded.size * 2 + nblk * BK * width * 2,
            transcendentals=0,
        ),
        compiler_params=pltpu.CompilerParams(vmem_limit_bytes=24 * 1024 * 1024),
    )(offsets, blocks, padded)


def _place():
    me = lax.axis_index("basis")
    orb = lax.axis_index("orb")
    core = lax.rem(me, 2)
    partner = me + 1 - 2 * core
    chip = lax.div(me, 2)
    return orb, core, partner, chip


def _barrier_group(nchip, orb, core, partner, chip):
    barrier = pltpu.get_barrier_semaphore()
    pl.semaphore_signal(barrier, inc=1, device_id=(partner, orb), device_id_type=MESH)
    for j in range(1, nchip):
        peer = 2 * lax.rem(chip + j, nchip) + core
        pl.semaphore_signal(barrier, inc=1, device_id=(peer, orb), device_id_type=MESH)
    pl.semaphore_wait(barrier, nchip)


def _remote(src, dst, ssem, rsem, device, orb):
    return pltpu.make_async_remote_copy(
        src_ref=src, dst_ref=dst, send_sem=ssem, recv_sem=rsem,
        device_id=(device, orb), device_id_type=MESH,
    )


def _two_level_sum(nchip, x_ref, pair_recv, part, chip_recv, p_send, p_recv, c_send, c_recv):
    orb, core, partner, chip = _place()
    _barrier_group(nchip, orb, core, partner, chip)
    pair = []
    for j in list(range(1, nchip)) + [0]:
        dst = lax.rem(chip + j, nchip)
        cp = _remote(x_ref.at[dst, 1 - core], pair_recv.at[dst], p_send.at[j], p_recv.at[dst], partner, orb)
        cp.start()
        pair.append(cp)
    sends = []
    for j in range(1, nchip):
        dst = lax.rem(chip + j, nchip)
        pair[j - 1].wait_recv()
        part[dst] = x_ref[dst, core] + pair_recv[dst]
        cp = _remote(part.at[dst], chip_recv.at[chip], c_send.at[j], c_recv.at[chip], 2 * dst + core, orb)
        cp.start()
        sends.append(cp)
    pair[-1].wait_recv()
    total = x_ref[chip, core] + pair_recv[chip]
    for j in range(1, nchip):
        src = lax.rem(chip + nchip - j, nchip)
        _remote(part.at[src], chip_recv.at[src], c_send.at[j], c_recv.at[src], 2 * src + core, orb).wait_recv()
        total = total + chip_recv[src]
    for cp in pair + sends:
        cp.wait_send()
    return total


def allreduce_kernel(nchip, x_ref, out_ref, pair_recv, part, chip_recv, sendbuf, half, other,
                     p_send, p_recv, c_send, c_recv, g_send, g_recv, h_send, h_recv):
    total = _two_level_sum(nchip, x_ref, pair_recv, part, chip_recv, p_send, p_recv, c_send, c_recv)
    orb, core, partner, chip = _place()
    rounded = total.astype(sendbuf.dtype)
    sendbuf[...] = rounded
    sends = []
    for j in range(1, nchip):
        dst = lax.rem(chip + j, nchip)
        cp = _remote(sendbuf, half.at[chip], g_send.at[j], g_recv.at[chip], 2 * dst + core, orb)
        cp.start()
        sends.append(cp)
    cp = _remote(sendbuf, other.at[chip], h_send.at[0], h_recv.at[chip], partner, orb)
    cp.start()
    sends.append(cp)
    out_ref[chip, core] = rounded
    for j in range(1, nchip):
        src = lax.rem(chip + nchip - j, nchip)
        _remote(sendbuf, half.at[src], g_send.at[j], g_recv.at[src], 2 * src + core, orb).wait_recv()
        cp = _remote(half.at[src], other.at[src], h_send.at[j], h_recv.at[src], partner, orb)
        cp.start()
        sends.append(cp)
        out_ref[src, core] = half[src]
    for j in range(nchip):
        src = lax.rem(chip + nchip - j, nchip)
        _remote(sendbuf, other.at[src], h_send.at[j], h_recv.at[src], partner, orb).wait_recv()
        out_ref[src, 1 - core] = other[src]
    for cp in sends:
        cp.wait_send()


def _two_level_scratch(nchip, rows, cols):
    return [
        pltpu.VMEM((nchip, rows, cols), jnp.float32),
        pltpu.VMEM((nchip, rows, cols), jnp.float32),
        pltpu.VMEM((nchip, rows, cols), jnp.float32),
    ]


def allreduce_to_bf16(partial, n):
    rows, cols = partial.shape
    nchip = n // 2
    chunk = rows // n
    x = partial.reshape(nchip, 2, chunk, cols)
    out = pl.pallas_call(
        functools.partial(allreduce_kernel, nchip),
        out_shape=jax.ShapeDtypeStruct((nchip, 2, chunk, cols), jnp.bfloat16),
        in_specs=[pl.BlockSpec(memory_space=pltpu.VMEM)],
        out_specs=pl.BlockSpec(memory_space=pltpu.VMEM),
        scratch_shapes=_two_level_scratch(nchip, chunk, cols) + [
            pltpu.VMEM((chunk, cols), jnp.bfloat16),
            pltpu.VMEM((nchip, chunk, cols), jnp.bfloat16),
            pltpu.VMEM((nchip, chunk, cols), jnp.bfloat16),
        ] + [pltpu.SemaphoreType.DMA((nchip,))] * 8,
        compiler_params=pltpu.CompilerParams(
            collective_id=0, has_side_effects=True, vmem_limit_bytes=12 * 1024 * 1024
        ),
        cost_estimate=pl.CostEstimate(flops=0, bytes_accessed=64 * x.size, transcendentals=0),
    )(x)
    return out.reshape(rows, cols)


def dipole_kernel(nchip, chunk, count, x_ref, out_ref, pair_recv, part, chip_recv,
                  p_send, p_recv, c_send, c_recv):
    total = _two_level_sum(nchip, x_ref, pair_recv, part, chip_recv, p_send, p_recv, c_send, c_recv)
    squares = total[chunk:chunk + 1, :]
    col_norm = 1.0 / jnp.sqrt(squares / count + 1e-06)
    out_ref[...] = (total[:chunk, :] * col_norm).astype(out_ref.dtype)


def dipole_scatter(partial, squares, n, count):
    rows, cols = partial.shape
    nchip = n // 2
    chunk = rows // n
    x = jnp.concatenate(
        [
            partial.reshape(nchip, 2, chunk, cols),
            jnp.broadcast_to(squares[None, None, None, :], (nchip, 2, 8, cols)),
        ],
        axis=2,
    )
    return pl.pallas_call(
        functools.partial(dipole_kernel, nchip, chunk, count),
        out_shape=jax.ShapeDtypeStruct((chunk, cols), jnp.bfloat16),
        in_specs=[pl.BlockSpec(memory_space=pltpu.VMEM)],
        out_specs=pl.BlockSpec(memory_space=pltpu.VMEM),
        scratch_shapes=_two_level_scratch(nchip, chunk + 8, cols)
        + [pltpu.SemaphoreType.DMA((nchip,))] * 4,
        compiler_params=pltpu.CompilerParams(
            collective_id=1, has_side_effects=True, vmem_limit_bytes=12 * 1024 * 1024
        ),
        cost_estimate=pl.CostEstimate(flops=0, bytes_accessed=32 * x.size, transcendentals=0),
    )(x)


def on_device(cont_orbitals, target_orbitals, margin_blocks, dipole_blocks, band_offsets):
    n = lax.axis_size("basis")
    count = band_offsets.shape[0] * BK * n
    cont_padded = with_halo(cont_orbitals, 2)
    margin_cont = band_local(margin_blocks, band_offsets, cont_padded)
    partial_proj_t = lax.dot_general(
        margin_cont, target_orbitals, (((0,), (0,)), ((), ())), preferred_element_type=jnp.float32
    )
    projection_b_t = allreduce_to_bf16(partial_proj_t, n)
    orth_padded, squares = orthogonalize_with_halo(
        target_orbitals, projection_b_t, cont_orbitals, 3
    )
    dipole_cont, cont_orth = band_local(dipole_blocks, band_offsets, orth_padded, True)
    partial_dip = lax.dot_general(
        target_orbitals,
        dipole_cont,
        (((0,), (0,)), ((), ())),
        preferred_element_type=jnp.float32,
    )
    dipole_mo = dipole_scatter(partial_dip, squares, n, count)
    return (cont_orth, dipole_mo)


def solution(mesh):
    return jax.shard_map(
        on_device,
        mesh=mesh,
        in_specs=(
            P("basis", "orb"),
            P("basis", None),
            P("basis", None, None, None),
            P("basis", None, None, None),
            P("basis", None),
        ),
        out_specs=(P("basis", "orb"), P("basis", "orb")),
        check_vma=False,
    )
```

```python
import functools

import jax
import jax.numpy as jnp
from jax import lax
from jax.experimental import pallas as pl
from jax.experimental.pallas import tpu as pltpu
from jax.sharding import PartitionSpec as P

BK = 256
KB = 4
MESH = pl.DeviceIdType.MESH


def padded_2(block, sides, width):
    for axis, dim in sides:
        count = lax.axis_size(axis)
        forward = [(i, i + 1) for i in range(count - 1)]
        backward = [(target, source) for source, target in forward]
        low = lax.ppermute(
            lax.slice_in_dim(block, block.shape[dim] - width, None, axis=dim), axis, forward
        )
        high = lax.ppermute(lax.slice_in_dim(block, 0, width, axis=dim), axis, backward)
        block = jnp.concatenate([low, block, high], axis=dim)
    return block


def halo_kernel(n, field_ref, out_ref, low, high, send_sem, recv_sem, copy_sem):
    rows, width = field_ref.shape
    edge = 2 * BK
    me = lax.axis_index("basis")
    orb = lax.axis_index("orb")
    has_low = me > 0
    has_high = me < n - 1
    middle = pltpu.make_async_copy(field_ref, out_ref.at[pl.ds(edge, rows)], copy_sem.at[0])
    middle.start()
    barrier = pltpu.get_barrier_semaphore()

    @pl.when(has_low)
    def _():
        pl.semaphore_signal(barrier, inc=1, device_id=(me - 1, orb), device_id_type=MESH)

    @pl.when(has_high)
    def _():
        pl.semaphore_signal(barrier, inc=1, device_id=(me + 1, orb), device_id_type=MESH)

    pl.semaphore_wait(barrier, has_low.astype(jnp.int32) + has_high.astype(jnp.int32))
    to_low = pltpu.make_async_remote_copy(
        src_ref=field_ref.at[pl.ds(0, edge)], dst_ref=high,
        send_sem=send_sem.at[0], recv_sem=recv_sem.at[0],
        device_id=(jnp.maximum(me - 1, 0), orb), device_id_type=MESH,
    )
    to_high = pltpu.make_async_remote_copy(
        src_ref=field_ref.at[pl.ds(rows - edge, edge)], dst_ref=low,
        send_sem=send_sem.at[1], recv_sem=recv_sem.at[1],
        device_id=(jnp.minimum(me + 1, n - 1), orb), device_id_type=MESH,
    )

    @pl.when(has_low)
    def _():
        to_low.start()

    @pl.when(has_high)
    def _():
        to_high.start()

    @pl.when(has_high)
    def _():
        to_low.wait_recv()
        out_ref[pl.ds(rows + edge, edge), :] = high[...]

    @pl.when(jnp.logical_not(has_high))
    def _():
        out_ref[pl.ds(rows + edge, edge), :] = jnp.zeros((edge, width), out_ref.dtype)

    @pl.when(has_low)
    def _():
        to_high.wait_recv()
        out_ref[pl.ds(0, edge), :] = low[...]

    @pl.when(jnp.logical_not(has_low))
    def _():
        out_ref[pl.ds(0, edge), :] = jnp.zeros((edge, width), out_ref.dtype)

    @pl.when(has_low)
    def _():
        to_low.wait_send()

    @pl.when(has_high)
    def _():
        to_high.wait_send()

    middle.wait()


def with_halo(field, collective_id):
    rows, width = field.shape
    n = lax.axis_size("basis")
    return pl.pallas_call(
        functools.partial(halo_kernel, n),
        out_shape=jax.ShapeDtypeStruct((rows + 4 * BK, width), field.dtype),
        in_specs=[pl.BlockSpec(memory_space=pltpu.VMEM)],
        out_specs=pl.BlockSpec(memory_space=pltpu.VMEM),
        scratch_shapes=[
            pltpu.VMEM((2 * BK, width), field.dtype),
            pltpu.VMEM((2 * BK, width), field.dtype),
            pltpu.SemaphoreType.DMA((2,)),
            pltpu.SemaphoreType.DMA((2,)),
            pltpu.SemaphoreType.DMA((1,)),
        ],
        cost_estimate=pl.CostEstimate(flops=0, bytes_accessed=4 * field.size * 2, transcendentals=0),
        compiler_params=pltpu.CompilerParams(
            collective_id=collective_id, has_side_effects=True, vmem_limit_bytes=8 * 1024 * 1024
        ),
    )(field)


def orth_halo_kernel(n, tgt_ref, proj_ref, cont_ref, pad_ref, sq_ref, orth_ref, low, high, send_sem, recv_sem):
    rows, width = cont_ref.shape
    edge = 2 * BK
    me = lax.axis_index("basis")
    orb = lax.axis_index("orb")
    has_low = me > 0
    has_high = me < n - 1
    barrier = pltpu.get_barrier_semaphore()

    @pl.when(has_low)
    def _():
        pl.semaphore_signal(barrier, inc=1, device_id=(me - 1, orb), device_id_type=MESH)

    @pl.when(has_high)
    def _():
        pl.semaphore_signal(barrier, inc=1, device_id=(me + 1, orb), device_id_type=MESH)

    def tile(start):
        removed = lax.dot_general(
            tgt_ref[pl.ds(start, edge), :], proj_ref[...], (((1,), (1,)), ((), ())),
            preferred_element_type=jnp.float32,
        )
        orth = (cont_ref[pl.ds(start, edge), :].astype(jnp.float32) - removed).astype(orth_ref.dtype)
        orth_ref[pl.ds(start, edge), :] = orth
        pad_ref[pl.ds(start + edge, edge), :] = orth
        wide = orth.astype(jnp.float32)
        return jnp.sum(wide * wide, axis=0, keepdims=True)

    squares = tile(0) + tile(rows - edge)
    pl.semaphore_wait(barrier, has_low.astype(jnp.int32) + has_high.astype(jnp.int32))
    to_low = pltpu.make_async_remote_copy(
        src_ref=orth_ref.at[pl.ds(0, edge)], dst_ref=high,
        send_sem=send_sem.at[0], recv_sem=recv_sem.at[0],
        device_id=(jnp.maximum(me - 1, 0), orb), device_id_type=MESH,
    )
    to_high = pltpu.make_async_remote_copy(
        src_ref=orth_ref.at[pl.ds(rows - edge, edge)], dst_ref=low,
        send_sem=send_sem.at[1], recv_sem=recv_sem.at[1],
        device_id=(jnp.minimum(me + 1, n - 1), orb), device_id_type=MESH,
    )

    @pl.when(has_low)
    def _():
        to_low.start()

    @pl.when(has_high)
    def _():
        to_high.start()

    for start in range(edge, rows - edge, edge):
        squares = squares + tile(start)
    sq_ref[...] = squares

    @pl.when(has_high)
    def _():
        to_low.wait_recv()
        pad_ref[pl.ds(rows + edge, edge), :] = high[...]

    @pl.when(jnp.logical_not(has_high))
    def _():
        pad_ref[pl.ds(rows + edge, edge), :] = jnp.zeros((edge, width), pad_ref.dtype)

    @pl.when(has_low)
    def _():
        to_high.wait_recv()
        pad_ref[pl.ds(0, edge), :] = low[...]

    @pl.when(jnp.logical_not(has_low))
    def _():
        pad_ref[pl.ds(0, edge), :] = jnp.zeros((edge, width), pad_ref.dtype)

    @pl.when(has_low)
    def _():
        to_low.wait_send()

    @pl.when(has_high)
    def _():
        to_high.wait_send()


def orthogonalize_with_halo(target, projection_b, cont, collective_id):
    rows, nt = target.shape
    width = cont.shape[1]
    n = lax.axis_size("basis")
    vmem = pl.BlockSpec(memory_space=pltpu.VMEM)
    padded, squares = pl.pallas_call(
        functools.partial(orth_halo_kernel, n),
        out_shape=(
            jax.ShapeDtypeStruct((rows + 4 * BK, width), jnp.bfloat16),
            jax.ShapeDtypeStruct((1, width), jnp.float32),
        ),
        in_specs=[vmem, vmem, vmem],
        out_specs=(vmem, vmem),
        scratch_shapes=[
            pltpu.VMEM((rows, width), jnp.bfloat16),
            pltpu.VMEM((2 * BK, width), jnp.bfloat16),
            pltpu.VMEM((2 * BK, width), jnp.bfloat16),
            pltpu.SemaphoreType.DMA((2,)),
            pltpu.SemaphoreType.DMA((2,)),
        ],
        cost_estimate=pl.CostEstimate(
            flops=2 * rows * nt * width,
            bytes_accessed=target.size * 2 + projection_b.size * 2 + 3 * cont.size * 2,
            transcendentals=0,
        ),
        compiler_params=pltpu.CompilerParams(
            collective_id=collective_id, has_side_effects=True, vmem_limit_bytes=24 * 1024 * 1024
        ),
    )(target, projection_b, cont)
    return padded, squares[0]


def band_kernel(rows_per_step, off_ref, blk_ref, field_ref, out_ref, *mid):
    g = pl.program_id(0)
    if mid:
        start = pl.multiple_of((g * rows_per_step + 2) * BK, BK)
        mid[0][...] = field_ref[pl.ds(start, rows_per_step * BK), :]
    for r in range(rows_per_step):
        b = g * rows_per_step + r
        acc = None
        for k in range(KB):
            start = pl.multiple_of((b + 2 + off_ref[k, b]) * BK, BK)
            term = jnp.dot(
                blk_ref[r, k], field_ref[pl.ds(start, BK), :], preferred_element_type=jnp.float32
            )
            acc = term if acc is None else acc + term
        out_ref[pl.ds(r * BK, BK), :] = acc.astype(out_ref.dtype)


def band_local(blocks, offsets, padded, with_middle=False):
    nblk = blocks.shape[0]
    rows, width = padded.shape
    per = 8 if nblk % 8 == 0 else 1
    field = jax.ShapeDtypeStruct((nblk * BK, width), jnp.bfloat16)
    spec = pl.BlockSpec((per * BK, width), lambda g, off: (g, 0))
    return pl.pallas_call(
        functools.partial(band_kernel, per),
        out_shape=(field, field) if with_middle else field,
        grid_spec=pltpu.PrefetchScalarGridSpec(
            num_scalar_prefetch=1,
            grid=(nblk // per,),
            in_specs=[
                pl.BlockSpec((per, KB, BK, BK), lambda g, off: (g, 0, 0, 0)),
                pl.BlockSpec((rows, width), lambda g, off: (0, 0)),
            ],
            out_specs=(spec, spec) if with_middle else spec,
        ),
        cost_estimate=pl.CostEstimate(
            flops=2 * nblk * KB * BK * BK * width,
            bytes_accessed=blocks.size * 2 + padded.size * 2 + nblk * BK * width * 2,
            transcendentals=0,
        ),
        compiler_params=pltpu.CompilerParams(vmem_limit_bytes=24 * 1024 * 1024),
    )(offsets.T, blocks, padded)


def _place():
    me = lax.axis_index("basis")
    orb = lax.axis_index("orb")
    core = lax.rem(me, 2)
    partner = me + 1 - 2 * core
    chip = lax.div(me, 2)
    return orb, core, partner, chip


def _barrier_group(nchip, orb, core, partner, chip):
    barrier = pltpu.get_barrier_semaphore()
    pl.semaphore_signal(barrier, inc=1, device_id=(partner, orb), device_id_type=MESH)
    for j in range(1, nchip):
        peer = 2 * lax.rem(chip + j, nchip) + core
        pl.semaphore_signal(barrier, inc=1, device_id=(peer, orb), device_id_type=MESH)
    pl.semaphore_wait(barrier, nchip)


def _remote(src, dst, ssem, rsem, device, orb):
    return pltpu.make_async_remote_copy(
        src_ref=src, dst_ref=dst, send_sem=ssem, recv_sem=rsem,
        device_id=(device, orb), device_id_type=MESH,
    )


def _two_level_sum(nchip, x_ref, pair_recv, part, chip_recv, p_send, p_recv, c_send, c_recv):
    orb, core, partner, chip = _place()
    _barrier_group(nchip, orb, core, partner, chip)
    pair = []
    for j in list(range(1, nchip)) + [0]:
        dst = lax.rem(chip + j, nchip)
        cp = _remote(x_ref.at[dst, 1 - core], pair_recv.at[dst], p_send.at[j], p_recv.at[dst], partner, orb)
        cp.start()
        pair.append(cp)
    sends = []
    for j in range(1, nchip):
        dst = lax.rem(chip + j, nchip)
        pair[j - 1].wait_recv()
        part[dst] = x_ref[dst, core] + pair_recv[dst]
        cp = _remote(part.at[dst], chip_recv.at[chip], c_send.at[j], c_recv.at[chip], 2 * dst + core, orb)
        cp.start()
        sends.append(cp)
    pair[-1].wait_recv()
    total = x_ref[chip, core] + pair_recv[chip]
    for j in range(1, nchip):
        src = lax.rem(chip + nchip - j, nchip)
        _remote(part.at[src], chip_recv.at[src], c_send.at[j], c_recv.at[src], 2 * src + core, orb).wait_recv()
        total = total + chip_recv[src]
    for cp in pair + sends:
        cp.wait_send()
    return total


def allreduce_kernel(nchip, x_ref, out_ref, pair_recv, part, chip_recv, sendbuf, half, other,
                     p_send, p_recv, c_send, c_recv, g_send, g_recv, h_send, h_recv):
    total = _two_level_sum(nchip, x_ref, pair_recv, part, chip_recv, p_send, p_recv, c_send, c_recv)
    orb, core, partner, chip = _place()
    rounded = total.astype(sendbuf.dtype)
    sendbuf[...] = rounded
    sends = []
    for j in range(1, nchip):
        dst = lax.rem(chip + j, nchip)
        cp = _remote(sendbuf, half.at[chip], g_send.at[j], g_recv.at[chip], 2 * dst + core, orb)
        cp.start()
        sends.append(cp)
    cp = _remote(sendbuf, other.at[chip], h_send.at[0], h_recv.at[chip], partner, orb)
    cp.start()
    sends.append(cp)
    out_ref[chip, core] = rounded
    for j in range(1, nchip):
        src = lax.rem(chip + nchip - j, nchip)
        _remote(sendbuf, half.at[src], g_send.at[j], g_recv.at[src], 2 * src + core, orb).wait_recv()
        cp = _remote(half.at[src], other.at[src], h_send.at[j], h_recv.at[src], partner, orb)
        cp.start()
        sends.append(cp)
        out_ref[src, core] = half[src]
    for j in range(nchip):
        src = lax.rem(chip + nchip - j, nchip)
        _remote(sendbuf, other.at[src], h_send.at[j], h_recv.at[src], partner, orb).wait_recv()
        out_ref[src, 1 - core] = other[src]
    for cp in sends:
        cp.wait_send()


def _two_level_scratch(nchip, rows, cols):
    return [
        pltpu.VMEM((nchip, rows, cols), jnp.float32),
        pltpu.VMEM((nchip, rows, cols), jnp.float32),
        pltpu.VMEM((nchip, rows, cols), jnp.float32),
    ]


def allreduce_to_bf16(partial, n):
    rows, cols = partial.shape
    nchip = n // 2
    chunk = rows // n
    x = partial.reshape(nchip, 2, chunk, cols)
    out = pl.pallas_call(
        functools.partial(allreduce_kernel, nchip),
        out_shape=jax.ShapeDtypeStruct((nchip, 2, chunk, cols), jnp.bfloat16),
        in_specs=[pl.BlockSpec(memory_space=pltpu.VMEM)],
        out_specs=pl.BlockSpec(memory_space=pltpu.VMEM),
        scratch_shapes=_two_level_scratch(nchip, chunk, cols) + [
            pltpu.VMEM((chunk, cols), jnp.bfloat16),
            pltpu.VMEM((nchip, chunk, cols), jnp.bfloat16),
            pltpu.VMEM((nchip, chunk, cols), jnp.bfloat16),
        ] + [pltpu.SemaphoreType.DMA((nchip,))] * 8,
        compiler_params=pltpu.CompilerParams(
            collective_id=0, has_side_effects=True, vmem_limit_bytes=12 * 1024 * 1024
        ),
        cost_estimate=pl.CostEstimate(flops=0, bytes_accessed=64 * x.size, transcendentals=0),
    )(x)
    return out.reshape(rows, cols)


def dipole_kernel(nchip, chunk, count, x_ref, out_ref, pair_recv, part, chip_recv,
                  p_send, p_recv, c_send, c_recv):
    total = _two_level_sum(nchip, x_ref, pair_recv, part, chip_recv, p_send, p_recv, c_send, c_recv)
    squares = total[chunk:chunk + 1, :]
    col_norm = 1.0 / jnp.sqrt(squares / count + 1e-06)
    out_ref[...] = (total[:chunk, :] * col_norm).astype(out_ref.dtype)


def dipole_scatter(partial, squares, n, count):
    rows, cols = partial.shape
    nchip = n // 2
    chunk = rows // n
    x = jnp.concatenate(
        [
            partial.reshape(nchip, 2, chunk, cols),
            jnp.broadcast_to(squares[None, None, None, :], (nchip, 2, 8, cols)),
        ],
        axis=2,
    )
    return pl.pallas_call(
        functools.partial(dipole_kernel, nchip, chunk, count),
        out_shape=jax.ShapeDtypeStruct((chunk, cols), jnp.bfloat16),
        in_specs=[pl.BlockSpec(memory_space=pltpu.VMEM)],
        out_specs=pl.BlockSpec(memory_space=pltpu.VMEM),
        scratch_shapes=_two_level_scratch(nchip, chunk + 8, cols)
        + [pltpu.SemaphoreType.DMA((nchip,))] * 4,
        compiler_params=pltpu.CompilerParams(
            collective_id=1, has_side_effects=True, vmem_limit_bytes=12 * 1024 * 1024
        ),
        cost_estimate=pl.CostEstimate(flops=0, bytes_accessed=32 * x.size, transcendentals=0),
    )(x)


def on_device(cont_orbitals, target_orbitals, margin_blocks, dipole_blocks, band_offsets):
    n = lax.axis_size("basis")
    count = band_offsets.shape[0] * BK * n
    cont_padded = with_halo(cont_orbitals, 2)
    margin_cont = band_local(margin_blocks, band_offsets, cont_padded)
    partial_proj_t = lax.dot_general(
        margin_cont, target_orbitals, (((0,), (0,)), ((), ())), preferred_element_type=jnp.float32
    )
    projection_b_t = allreduce_to_bf16(partial_proj_t, n)
    orth_padded, squares = orthogonalize_with_halo(
        target_orbitals, projection_b_t, cont_orbitals, 3
    )
    dipole_cont, cont_orth = band_local(dipole_blocks, band_offsets, orth_padded, True)
    partial_dip = lax.dot_general(
        target_orbitals,
        dipole_cont,
        (((0,), (0,)), ((), ())),
        preferred_element_type=jnp.float32,
    )
    dipole_mo = dipole_scatter(partial_dip, squares, n, count)
    return (cont_orth, dipole_mo)


def solution(mesh):
    return jax.shard_map(
        on_device,
        mesh=mesh,
        in_specs=(
            P("basis", "orb"),
            P("basis", None),
            P("basis", None, None, None),
            P("basis", None, None, None),
            P("basis", None),
        ),
        out_specs=(P("basis", "orb"), P("basis", "orb")),
        check_vma=False,
    )
```

```python
import functools

import jax
import jax.numpy as jnp
from jax import lax
from jax.experimental import pallas as pl
from jax.experimental.pallas import tpu as pltpu
from jax.sharding import PartitionSpec as P

BK = 256
KB = 4
MESH = pl.DeviceIdType.MESH


def padded_2(block, sides, width):
    for axis, dim in sides:
        count = lax.axis_size(axis)
        forward = [(i, i + 1) for i in range(count - 1)]
        backward = [(target, source) for source, target in forward]
        low = lax.ppermute(
            lax.slice_in_dim(block, block.shape[dim] - width, None, axis=dim), axis, forward
        )
        high = lax.ppermute(lax.slice_in_dim(block, 0, width, axis=dim), axis, backward)
        block = jnp.concatenate([low, block, high], axis=dim)
    return block


def halo_kernel(n, field_ref, out_ref, low, high, send_sem, recv_sem, copy_sem):
    rows, width = field_ref.shape
    edge = 2 * BK
    me = lax.axis_index("basis")
    orb = lax.axis_index("orb")
    has_low = me > 0
    has_high = me < n - 1
    middle = pltpu.make_async_copy(field_ref, out_ref.at[pl.ds(edge, rows)], copy_sem.at[0])
    middle.start()
    barrier = pltpu.get_barrier_semaphore()

    @pl.when(has_low)
    def _():
        pl.semaphore_signal(barrier, inc=1, device_id=(me - 1, orb), device_id_type=MESH)

    @pl.when(has_high)
    def _():
        pl.semaphore_signal(barrier, inc=1, device_id=(me + 1, orb), device_id_type=MESH)

    pl.semaphore_wait(barrier, has_low.astype(jnp.int32) + has_high.astype(jnp.int32))
    to_low = pltpu.make_async_remote_copy(
        src_ref=field_ref.at[pl.ds(0, edge)], dst_ref=high,
        send_sem=send_sem.at[0], recv_sem=recv_sem.at[0],
        device_id=(jnp.maximum(me - 1, 0), orb), device_id_type=MESH,
    )
    to_high = pltpu.make_async_remote_copy(
        src_ref=field_ref.at[pl.ds(rows - edge, edge)], dst_ref=low,
        send_sem=send_sem.at[1], recv_sem=recv_sem.at[1],
        device_id=(jnp.minimum(me + 1, n - 1), orb), device_id_type=MESH,
    )

    @pl.when(has_low)
    def _():
        to_low.start()

    @pl.when(has_high)
    def _():
        to_high.start()

    @pl.when(has_high)
    def _():
        to_low.wait_recv()
        out_ref[pl.ds(rows + edge, edge), :] = high[...]

    @pl.when(jnp.logical_not(has_high))
    def _():
        out_ref[pl.ds(rows + edge, edge), :] = jnp.zeros((edge, width), out_ref.dtype)

    @pl.when(has_low)
    def _():
        to_high.wait_recv()
        out_ref[pl.ds(0, edge), :] = low[...]

    @pl.when(jnp.logical_not(has_low))
    def _():
        out_ref[pl.ds(0, edge), :] = jnp.zeros((edge, width), out_ref.dtype)

    @pl.when(has_low)
    def _():
        to_low.wait_send()

    @pl.when(has_high)
    def _():
        to_high.wait_send()

    middle.wait()


def with_halo(field, collective_id):
    rows, width = field.shape
    n = lax.axis_size("basis")
    return pl.pallas_call(
        functools.partial(halo_kernel, n),
        out_shape=jax.ShapeDtypeStruct((rows + 4 * BK, width), field.dtype),
        in_specs=[pl.BlockSpec(memory_space=pltpu.VMEM)],
        out_specs=pl.BlockSpec(memory_space=pltpu.VMEM),
        scratch_shapes=[
            pltpu.VMEM((2 * BK, width), field.dtype),
            pltpu.VMEM((2 * BK, width), field.dtype),
            pltpu.SemaphoreType.DMA((2,)),
            pltpu.SemaphoreType.DMA((2,)),
            pltpu.SemaphoreType.DMA((1,)),
        ],
        cost_estimate=pl.CostEstimate(flops=0, bytes_accessed=4 * field.size * 2, transcendentals=0),
        compiler_params=pltpu.CompilerParams(
            collective_id=collective_id, has_side_effects=True, vmem_limit_bytes=8 * 1024 * 1024
        ),
    )(field)


def orth_halo_kernel(n, tgt_ref, proj_ref, cont_ref, pad_ref, sq_ref, orth_ref, low, high, send_sem, recv_sem):
    rows, width = cont_ref.shape
    edge = 2 * BK
    me = lax.axis_index("basis")
    orb = lax.axis_index("orb")
    has_low = me > 0
    has_high = me < n - 1
    barrier = pltpu.get_barrier_semaphore()

    @pl.when(has_low)
    def _():
        pl.semaphore_signal(barrier, inc=1, device_id=(me - 1, orb), device_id_type=MESH)

    @pl.when(has_high)
    def _():
        pl.semaphore_signal(barrier, inc=1, device_id=(me + 1, orb), device_id_type=MESH)

    def tile(start):
        removed = lax.dot_general(
            tgt_ref[pl.ds(start, edge), :], proj_ref[...], (((1,), (1,)), ((), ())),
            preferred_element_type=jnp.float32,
        )
        orth = (cont_ref[pl.ds(start, edge), :].astype(jnp.float32) - removed).astype(orth_ref.dtype)
        orth_ref[pl.ds(start, edge), :] = orth
        pad_ref[pl.ds(start + edge, edge), :] = orth
        wide = orth.astype(jnp.float32)
        return jnp.sum(wide * wide, axis=0, keepdims=True)

    squares = tile(0) + tile(rows - edge)
    pl.semaphore_wait(barrier, has_low.astype(jnp.int32) + has_high.astype(jnp.int32))
    to_low = pltpu.make_async_remote_copy(
        src_ref=orth_ref.at[pl.ds(0, edge)], dst_ref=high,
        send_sem=send_sem.at[0], recv_sem=recv_sem.at[0],
        device_id=(jnp.maximum(me - 1, 0), orb), device_id_type=MESH,
    )
    to_high = pltpu.make_async_remote_copy(
        src_ref=orth_ref.at[pl.ds(rows - edge, edge)], dst_ref=low,
        send_sem=send_sem.at[1], recv_sem=recv_sem.at[1],
        device_id=(jnp.minimum(me + 1, n - 1), orb), device_id_type=MESH,
    )

    @pl.when(has_low)
    def _():
        to_low.start()

    @pl.when(has_high)
    def _():
        to_high.start()

    for start in range(edge, rows - edge, edge):
        squares = squares + tile(start)
    sq_ref[...] = squares

    @pl.when(has_high)
    def _():
        to_low.wait_recv()
        pad_ref[pl.ds(rows + edge, edge), :] = high[...]

    @pl.when(jnp.logical_not(has_high))
    def _():
        pad_ref[pl.ds(rows + edge, edge), :] = jnp.zeros((edge, width), pad_ref.dtype)

    @pl.when(has_low)
    def _():
        to_high.wait_recv()
        pad_ref[pl.ds(0, edge), :] = low[...]

    @pl.when(jnp.logical_not(has_low))
    def _():
        pad_ref[pl.ds(0, edge), :] = jnp.zeros((edge, width), pad_ref.dtype)

    @pl.when(has_low)
    def _():
        to_low.wait_send()

    @pl.when(has_high)
    def _():
        to_high.wait_send()


def orthogonalize_with_halo(target, projection_b, cont, collective_id):
    rows, nt = target.shape
    width = cont.shape[1]
    n = lax.axis_size("basis")
    vmem = pl.BlockSpec(memory_space=pltpu.VMEM)
    padded, squares = pl.pallas_call(
        functools.partial(orth_halo_kernel, n),
        out_shape=(
            jax.ShapeDtypeStruct((rows + 4 * BK, width), jnp.bfloat16),
            jax.ShapeDtypeStruct((1, width), jnp.float32),
        ),
        in_specs=[vmem, vmem, vmem],
        out_specs=(vmem, vmem),
        scratch_shapes=[
            pltpu.VMEM((rows, width), jnp.bfloat16),
            pltpu.VMEM((2 * BK, width), jnp.bfloat16),
            pltpu.VMEM((2 * BK, width), jnp.bfloat16),
            pltpu.SemaphoreType.DMA((2,)),
            pltpu.SemaphoreType.DMA((2,)),
        ],
        cost_estimate=pl.CostEstimate(
            flops=2 * rows * nt * width,
            bytes_accessed=target.size * 2 + projection_b.size * 2 + 3 * cont.size * 2,
            transcendentals=0,
        ),
        compiler_params=pltpu.CompilerParams(
            collective_id=collective_id, has_side_effects=True, vmem_limit_bytes=24 * 1024 * 1024
        ),
    )(target, projection_b, cont)
    return padded, squares[0]


def band_kernel(rows_per_step, off_ref, blk_ref, field_ref, out_ref, *mid):
    g = pl.program_id(0)
    if mid:
        start = pl.multiple_of((g * rows_per_step + 2) * BK, BK)
        mid[0][...] = field_ref[pl.ds(start, rows_per_step * BK), :]
    for r in range(rows_per_step):
        b = g * rows_per_step + r
        acc = None
        for k in range(KB):
            start = pl.multiple_of((b + 2 + off_ref[k, b]) * BK, BK)
            term = jnp.dot(
                blk_ref[r, k], field_ref[pl.ds(start, BK), :], preferred_element_type=jnp.float32
            )
            acc = term if acc is None else acc + term
        out_ref[pl.ds(r * BK, BK), :] = acc.astype(out_ref.dtype)


def band_local(blocks, offsets, padded, with_middle=False):
    nblk = blocks.shape[0]
    rows, width = padded.shape
    per = 8 if nblk % 8 == 0 else 1
    field = jax.ShapeDtypeStruct((nblk * BK, width), jnp.bfloat16)
    spec = pl.BlockSpec((per * BK, width), lambda g, off: (g, 0))
    return pl.pallas_call(
        functools.partial(band_kernel, per),
        out_shape=(field, field) if with_middle else field,
        grid_spec=pltpu.PrefetchScalarGridSpec(
            num_scalar_prefetch=1,
            grid=(nblk // per,),
            in_specs=[
                pl.BlockSpec((per, KB, BK, BK), lambda g, off: (g, 0, 0, 0)),
                pl.BlockSpec((rows, width), lambda g, off: (0, 0)),
            ],
            out_specs=(spec, spec) if with_middle else spec,
        ),
        cost_estimate=pl.CostEstimate(
            flops=2 * nblk * KB * BK * BK * width,
            bytes_accessed=blocks.size * 2 + padded.size * 2 + nblk * BK * width * 2,
            transcendentals=0,
        ),
        compiler_params=pltpu.CompilerParams(vmem_limit_bytes=24 * 1024 * 1024),
    )(offsets.T, blocks, padded)


def _place():
    me = lax.axis_index("basis")
    orb = lax.axis_index("orb")
    core = lax.rem(me, 2)
    partner = me + 1 - 2 * core
    chip = lax.div(me, 2)
    return orb, core, partner, chip


def _barrier_group(nchip, orb, core, partner, chip):
    barrier = pltpu.get_barrier_semaphore()
    pl.semaphore_signal(barrier, inc=1, device_id=(partner, orb), device_id_type=MESH)
    for j in range(1, nchip):
        peer = 2 * lax.rem(chip + j, nchip) + core
        pl.semaphore_signal(barrier, inc=1, device_id=(peer, orb), device_id_type=MESH)
    pl.semaphore_wait(barrier, nchip)


def _remote(src, dst, ssem, rsem, device, orb):
    return pltpu.make_async_remote_copy(
        src_ref=src, dst_ref=dst, send_sem=ssem, recv_sem=rsem,
        device_id=(device, orb), device_id_type=MESH,
    )


def _two_level_sum(nchip, x_ref, pair_recv, part, chip_recv, p_send, p_recv, c_send, c_recv):
    orb, core, partner, chip = _place()
    _barrier_group(nchip, orb, core, partner, chip)
    pair = []
    for j in list(range(1, nchip)) + [0]:
        dst = lax.rem(chip + j, nchip)
        cp = _remote(x_ref.at[dst, 1 - core], pair_recv.at[dst], p_send.at[j], p_recv.at[dst], partner, orb)
        cp.start()
        pair.append(cp)
    sends = []
    for j in range(1, nchip):
        dst = lax.rem(chip + j, nchip)
        pair[j - 1].wait_recv()
        part[dst] = x_ref[dst, core] + pair_recv[dst]
        cp = _remote(part.at[dst], chip_recv.at[chip], c_send.at[j], c_recv.at[chip], 2 * dst + core, orb)
        cp.start()
        sends.append(cp)
    pair[-1].wait_recv()
    total = x_ref[chip, core] + pair_recv[chip]
    for j in range(1, nchip):
        src = lax.rem(chip + nchip - j, nchip)
        _remote(part.at[src], chip_recv.at[src], c_send.at[j], c_recv.at[src], 2 * src + core, orb).wait_recv()
        total = total + chip_recv[src]
    for cp in pair + sends:
        cp.wait_send()
    return total


def allreduce_kernel(nchip, x_ref, out_ref, pair_recv, part, chip_recv, sendbuf, half, other,
                     p_send, p_recv, c_send, c_recv, g_send, g_recv, h_send, h_recv):
    total = _two_level_sum(nchip, x_ref, pair_recv, part, chip_recv, p_send, p_recv, c_send, c_recv)
    orb, core, partner, chip = _place()
    rounded = total.astype(sendbuf.dtype)
    sendbuf[...] = rounded
    sends = []
    for j in range(1, nchip):
        dst = lax.rem(chip + j, nchip)
        cp = _remote(sendbuf, half.at[chip], g_send.at[j], g_recv.at[chip], 2 * dst + core, orb)
        cp.start()
        sends.append(cp)
    cp = _remote(sendbuf, other.at[chip], h_send.at[0], h_recv.at[chip], partner, orb)
    cp.start()
    sends.append(cp)
    out_ref[chip, core] = rounded
    for j in range(1, nchip):
        src = lax.rem(chip + nchip - j, nchip)
        _remote(sendbuf, half.at[src], g_send.at[j], g_recv.at[src], 2 * src + core, orb).wait_recv()
        cp = _remote(half.at[src], other.at[src], h_send.at[j], h_recv.at[src], partner, orb)
        cp.start()
        sends.append(cp)
        out_ref[src, core] = half[src]
    for j in range(nchip):
        src = lax.rem(chip + nchip - j, nchip)
        _remote(sendbuf, other.at[src], h_send.at[j], h_recv.at[src], partner, orb).wait_recv()
        out_ref[src, 1 - core] = other[src]
    for cp in sends:
        cp.wait_send()


def _two_level_scratch(nchip, rows, cols):
    return [
        pltpu.VMEM((nchip, rows, cols), jnp.float32),
        pltpu.VMEM((nchip, rows, cols), jnp.float32),
        pltpu.VMEM((nchip, rows, cols), jnp.float32),
    ]


def allreduce_to_bf16(partial, n):
    rows, cols = partial.shape
    nchip = n // 2
    chunk = rows // n
    x = partial.reshape(nchip, 2, chunk, cols)
    out = pl.pallas_call(
        functools.partial(allreduce_kernel, nchip),
        out_shape=jax.ShapeDtypeStruct((nchip, 2, chunk, cols), jnp.bfloat16),
        in_specs=[pl.BlockSpec(memory_space=pltpu.VMEM)],
        out_specs=pl.BlockSpec(memory_space=pltpu.VMEM),
        scratch_shapes=_two_level_scratch(nchip, chunk, cols) + [
            pltpu.VMEM((chunk, cols), jnp.bfloat16),
            pltpu.VMEM((nchip, chunk, cols), jnp.bfloat16),
            pltpu.VMEM((nchip, chunk, cols), jnp.bfloat16),
        ] + [pltpu.SemaphoreType.DMA((nchip,))] * 8,
        compiler_params=pltpu.CompilerParams(
            collective_id=0, has_side_effects=True, vmem_limit_bytes=12 * 1024 * 1024
        ),
        cost_estimate=pl.CostEstimate(flops=0, bytes_accessed=64 * x.size, transcendentals=0),
    )(x)
    return out.reshape(rows, cols)


def dipole_kernel(nchip, chunk, count, x_ref, out_ref, pair_recv, part, chip_recv,
                  p_send, p_recv, c_send, c_recv):
    out_ref[...] = _two_level_sum(nchip, x_ref, pair_recv, part, chip_recv, p_send, p_recv, c_send, c_recv)


def dipole_scatter(partial, squares, n, count):
    rows, cols = partial.shape
    nchip = n // 2
    chunk = rows // n
    x = jnp.concatenate(
        [
            partial.reshape(nchip, 2, chunk, cols),
            jnp.broadcast_to(squares[None, None, None, :], (nchip, 2, 8, cols)),
        ],
        axis=2,
    )
    total = pl.pallas_call(
        functools.partial(dipole_kernel, nchip, chunk, count),
        out_shape=jax.ShapeDtypeStruct((chunk + 8, cols), jnp.float32),
        in_specs=[pl.BlockSpec(memory_space=pltpu.VMEM)],
        out_specs=pl.BlockSpec(memory_space=pltpu.VMEM),
        scratch_shapes=_two_level_scratch(nchip, chunk + 8, cols)
        + [pltpu.SemaphoreType.DMA((nchip,))] * 4,
        compiler_params=pltpu.CompilerParams(
            collective_id=1, has_side_effects=True, vmem_limit_bytes=12 * 1024 * 1024
        ),
        cost_estimate=pl.CostEstimate(flops=0, bytes_accessed=32 * x.size, transcendentals=0),
    )(x)
    col_norm = 1.0 / jnp.sqrt(total[chunk] / count + 1e-06)
    return (total[:chunk] * col_norm[None, :]).astype(jnp.bfloat16)


def on_device(cont_orbitals, target_orbitals, margin_blocks, dipole_blocks, band_offsets):
    n = lax.axis_size("basis")
    count = band_offsets.shape[0] * BK * n
    cont_padded = with_halo(cont_orbitals, 2)
    margin_cont = band_local(margin_blocks, band_offsets, cont_padded)
    partial_proj_t = lax.dot_general(
        margin_cont, target_orbitals, (((0,), (0,)), ((), ())), preferred_element_type=jnp.float32
    )
    projection_b_t = allreduce_to_bf16(partial_proj_t, n)
    orth_padded, squares = orthogonalize_with_halo(
        target_orbitals, projection_b_t, cont_orbitals, 3
    )
    dipole_cont, cont_orth = band_local(dipole_blocks, band_offsets, orth_padded, True)
    partial_dip = lax.dot_general(
        target_orbitals,
        dipole_cont,
        (((0,), (0,)), ((), ())),
        preferred_element_type=jnp.float32,
    )
    dipole_mo = dipole_scatter(partial_dip, squares, n, count)
    return (cont_orth, dipole_mo)


def solution(mesh):
    return jax.shard_map(
        on_device,
        mesh=mesh,
        in_specs=(
            P("basis", "orb"),
            P("basis", None),
            P("basis", None, None, None),
            P("basis", None, None, None),
            P("basis", None),
        ),
        out_specs=(P("basis", "orb"), P("basis", "orb")),
        check_vma=False,
    )
```

```python
import functools

import jax
import jax.numpy as jnp
from jax import lax
from jax.experimental import pallas as pl
from jax.experimental.pallas import tpu as pltpu
from jax.sharding import PartitionSpec as P

BK = 256
KB = 4
MESH = pl.DeviceIdType.MESH


def padded_2(block, sides, width):
    for axis, dim in sides:
        count = lax.axis_size(axis)
        forward = [(i, i + 1) for i in range(count - 1)]
        backward = [(target, source) for source, target in forward]
        low = lax.ppermute(
            lax.slice_in_dim(block, block.shape[dim] - width, None, axis=dim), axis, forward
        )
        high = lax.ppermute(lax.slice_in_dim(block, 0, width, axis=dim), axis, backward)
        block = jnp.concatenate([low, block, high], axis=dim)
    return block


def halo_kernel(n, field_ref, out_ref, low, high, send_sem, recv_sem, copy_sem):
    rows, width = field_ref.shape
    edge = 2 * BK
    me = lax.axis_index("basis")
    orb = lax.axis_index("orb")
    has_low = me > 0
    has_high = me < n - 1
    middle = pltpu.make_async_copy(field_ref, out_ref.at[pl.ds(edge, rows)], copy_sem.at[0])
    middle.start()
    barrier = pltpu.get_barrier_semaphore()

    @pl.when(has_low)
    def _():
        pl.semaphore_signal(barrier, inc=1, device_id=(me - 1, orb), device_id_type=MESH)

    @pl.when(has_high)
    def _():
        pl.semaphore_signal(barrier, inc=1, device_id=(me + 1, orb), device_id_type=MESH)

    pl.semaphore_wait(barrier, has_low.astype(jnp.int32) + has_high.astype(jnp.int32))
    to_low = pltpu.make_async_remote_copy(
        src_ref=field_ref.at[pl.ds(0, edge)], dst_ref=high,
        send_sem=send_sem.at[0], recv_sem=recv_sem.at[0],
        device_id=(jnp.maximum(me - 1, 0), orb), device_id_type=MESH,
    )
    to_high = pltpu.make_async_remote_copy(
        src_ref=field_ref.at[pl.ds(rows - edge, edge)], dst_ref=low,
        send_sem=send_sem.at[1], recv_sem=recv_sem.at[1],
        device_id=(jnp.minimum(me + 1, n - 1), orb), device_id_type=MESH,
    )

    @pl.when(has_low)
    def _():
        to_low.start()

    @pl.when(has_high)
    def _():
        to_high.start()

    @pl.when(has_high)
    def _():
        to_low.wait_recv()
        out_ref[pl.ds(rows + edge, edge), :] = high[...]

    @pl.when(jnp.logical_not(has_high))
    def _():
        out_ref[pl.ds(rows + edge, edge), :] = jnp.zeros((edge, width), out_ref.dtype)

    @pl.when(has_low)
    def _():
        to_high.wait_recv()
        out_ref[pl.ds(0, edge), :] = low[...]

    @pl.when(jnp.logical_not(has_low))
    def _():
        out_ref[pl.ds(0, edge), :] = jnp.zeros((edge, width), out_ref.dtype)

    @pl.when(has_low)
    def _():
        to_low.wait_send()

    @pl.when(has_high)
    def _():
        to_high.wait_send()

    middle.wait()


def with_halo(field, collective_id):
    rows, width = field.shape
    n = lax.axis_size("basis")
    return pl.pallas_call(
        functools.partial(halo_kernel, n),
        out_shape=jax.ShapeDtypeStruct((rows + 4 * BK, width), field.dtype),
        in_specs=[pl.BlockSpec(memory_space=pltpu.VMEM)],
        out_specs=pl.BlockSpec(memory_space=pltpu.VMEM),
        scratch_shapes=[
            pltpu.VMEM((2 * BK, width), field.dtype),
            pltpu.VMEM((2 * BK, width), field.dtype),
            pltpu.SemaphoreType.DMA((2,)),
            pltpu.SemaphoreType.DMA((2,)),
            pltpu.SemaphoreType.DMA((1,)),
        ],
        cost_estimate=pl.CostEstimate(flops=0, bytes_accessed=4 * field.size * 2, transcendentals=0),
        compiler_params=pltpu.CompilerParams(
            collective_id=collective_id, has_side_effects=True, vmem_limit_bytes=8 * 1024 * 1024
        ),
    )(field)


def orth_halo_kernel(n, tgt_ref, proj_ref, cont_ref, pad_ref, sq_ref, orth_ref, low, high, send_sem, recv_sem):
    rows, width = cont_ref.shape
    edge = 2 * BK
    me = lax.axis_index("basis")
    orb = lax.axis_index("orb")
    has_low = me > 0
    has_high = me < n - 1
    barrier = pltpu.get_barrier_semaphore()

    @pl.when(has_low)
    def _():
        pl.semaphore_signal(barrier, inc=1, device_id=(me - 1, orb), device_id_type=MESH)

    @pl.when(has_high)
    def _():
        pl.semaphore_signal(barrier, inc=1, device_id=(me + 1, orb), device_id_type=MESH)

    def tile(start):
        removed = lax.dot_general(
            tgt_ref[pl.ds(start, edge), :], proj_ref[...], (((1,), (1,)), ((), ())),
            preferred_element_type=jnp.float32,
        )
        orth = (cont_ref[pl.ds(start, edge), :].astype(jnp.float32) - removed).astype(orth_ref.dtype)
        orth_ref[pl.ds(start, edge), :] = orth
        pad_ref[pl.ds(start + edge, edge), :] = orth
        wide = orth.astype(jnp.float32)
        return jnp.sum(wide * wide, axis=0, keepdims=True)

    squares = tile(0) + tile(rows - edge)
    pl.semaphore_wait(barrier, has_low.astype(jnp.int32) + has_high.astype(jnp.int32))
    to_low = pltpu.make_async_remote_copy(
        src_ref=orth_ref.at[pl.ds(0, edge)], dst_ref=high,
        send_sem=send_sem.at[0], recv_sem=recv_sem.at[0],
        device_id=(jnp.maximum(me - 1, 0), orb), device_id_type=MESH,
    )
    to_high = pltpu.make_async_remote_copy(
        src_ref=orth_ref.at[pl.ds(rows - edge, edge)], dst_ref=low,
        send_sem=send_sem.at[1], recv_sem=recv_sem.at[1],
        device_id=(jnp.minimum(me + 1, n - 1), orb), device_id_type=MESH,
    )

    @pl.when(has_low)
    def _():
        to_low.start()

    @pl.when(has_high)
    def _():
        to_high.start()

    for start in range(edge, rows - edge, edge):
        squares = squares + tile(start)
    sq_ref[...] = squares

    @pl.when(has_high)
    def _():
        to_low.wait_recv()
        pad_ref[pl.ds(rows + edge, edge), :] = high[...]

    @pl.when(jnp.logical_not(has_high))
    def _():
        pad_ref[pl.ds(rows + edge, edge), :] = jnp.zeros((edge, width), pad_ref.dtype)

    @pl.when(has_low)
    def _():
        to_high.wait_recv()
        pad_ref[pl.ds(0, edge), :] = low[...]

    @pl.when(jnp.logical_not(has_low))
    def _():
        pad_ref[pl.ds(0, edge), :] = jnp.zeros((edge, width), pad_ref.dtype)

    @pl.when(has_low)
    def _():
        to_low.wait_send()

    @pl.when(has_high)
    def _():
        to_high.wait_send()


def orthogonalize_with_halo(target, projection_b, cont, collective_id):
    rows, nt = target.shape
    width = cont.shape[1]
    n = lax.axis_size("basis")
    vmem = pl.BlockSpec(memory_space=pltpu.VMEM)
    padded, squares = pl.pallas_call(
        functools.partial(orth_halo_kernel, n),
        out_shape=(
            jax.ShapeDtypeStruct((rows + 4 * BK, width), jnp.bfloat16),
            jax.ShapeDtypeStruct((1, width), jnp.float32),
        ),
        in_specs=[vmem, vmem, vmem],
        out_specs=(vmem, vmem),
        scratch_shapes=[
            pltpu.VMEM((rows, width), jnp.bfloat16),
            pltpu.VMEM((2 * BK, width), jnp.bfloat16),
            pltpu.VMEM((2 * BK, width), jnp.bfloat16),
            pltpu.SemaphoreType.DMA((2,)),
            pltpu.SemaphoreType.DMA((2,)),
        ],
        cost_estimate=pl.CostEstimate(
            flops=2 * rows * nt * width,
            bytes_accessed=target.size * 2 + projection_b.size * 2 + 3 * cont.size * 2,
            transcendentals=0,
        ),
        compiler_params=pltpu.CompilerParams(
            collective_id=collective_id, has_side_effects=True, vmem_limit_bytes=24 * 1024 * 1024
        ),
    )(target, projection_b, cont)
    return padded, squares[0]


def band_kernel(rows_per_step, off_ref, blk_ref, field_ref, out_ref, *mid):
    g = pl.program_id(0)
    if mid:
        start = pl.multiple_of((g * rows_per_step + 2) * BK, BK)
        mid[0][...] = field_ref[pl.ds(start, rows_per_step * BK), :]
    for r in range(rows_per_step):
        b = g * rows_per_step + r
        acc = None
        for k in range(KB):
            start = pl.multiple_of((b + 2 + off_ref[k, b]) * BK, BK)
            term = jnp.dot(
                blk_ref[r, k], field_ref[pl.ds(start, BK), :], preferred_element_type=jnp.float32
            )
            acc = term if acc is None else acc + term
        out_ref[pl.ds(r * BK, BK), :] = acc.astype(out_ref.dtype)


def band_whole_kernel(off_ref, blk_ref, field_ref, out_ref):
    for b in range(blk_ref.shape[0]):
        acc = None
        for k in range(KB):
            start = pl.multiple_of((b + 2 + off_ref[k, b]) * BK, BK)
            term = jnp.dot(blk_ref[b, k], field_ref[pl.ds(start, BK), :], preferred_element_type=jnp.float32)
            acc = term if acc is None else acc + term
        out_ref[pl.ds(b * BK, BK), :] = acc.astype(out_ref.dtype)


def band_whole(blocks, offsets, padded):
    nblk = blocks.shape[0]
    rows, width = padded.shape
    return pl.pallas_call(
        band_whole_kernel,
        out_shape=jax.ShapeDtypeStruct((nblk * BK, width), jnp.bfloat16),
        in_specs=[
            pl.BlockSpec(memory_space=pltpu.SMEM),
            pl.BlockSpec(memory_space=pltpu.VMEM),
            pl.BlockSpec(memory_space=pltpu.VMEM),
        ],
        out_specs=pl.BlockSpec(memory_space=pltpu.VMEM),
        cost_estimate=pl.CostEstimate(
            flops=2 * nblk * KB * BK * BK * width,
            bytes_accessed=blocks.size * 2 + padded.size * 2 + nblk * BK * width * 2,
            transcendentals=0,
        ),
        compiler_params=pltpu.CompilerParams(vmem_limit_bytes=8 * 1024 * 1024),
    )(offsets.T, blocks, padded)


def band_local(blocks, offsets, padded, with_middle=False):
    nblk = blocks.shape[0]
    rows, width = padded.shape
    per = 8 if nblk % 8 == 0 else 1
    field = jax.ShapeDtypeStruct((nblk * BK, width), jnp.bfloat16)
    spec = pl.BlockSpec((per * BK, width), lambda g, off: (g, 0))
    return pl.pallas_call(
        functools.partial(band_kernel, per),
        out_shape=(field, field) if with_middle else field,
        grid_spec=pltpu.PrefetchScalarGridSpec(
            num_scalar_prefetch=1,
            grid=(nblk // per,),
            in_specs=[
                pl.BlockSpec((per, KB, BK, BK), lambda g, off: (g, 0, 0, 0)),
                pl.BlockSpec((rows, width), lambda g, off: (0, 0)),
            ],
            out_specs=(spec, spec) if with_middle else spec,
        ),
        cost_estimate=pl.CostEstimate(
            flops=2 * nblk * KB * BK * BK * width,
            bytes_accessed=blocks.size * 2 + padded.size * 2 + nblk * BK * width * 2,
            transcendentals=0,
        ),
        compiler_params=pltpu.CompilerParams(vmem_limit_bytes=24 * 1024 * 1024),
    )(offsets.T, blocks, padded)


def _place():
    me = lax.axis_index("basis")
    orb = lax.axis_index("orb")
    core = lax.rem(me, 2)
    partner = me + 1 - 2 * core
    chip = lax.div(me, 2)
    return orb, core, partner, chip


def _barrier_group(nchip, orb, core, partner, chip):
    barrier = pltpu.get_barrier_semaphore()
    pl.semaphore_signal(barrier, inc=1, device_id=(partner, orb), device_id_type=MESH)
    for j in range(1, nchip):
        peer = 2 * lax.rem(chip + j, nchip) + core
        pl.semaphore_signal(barrier, inc=1, device_id=(peer, orb), device_id_type=MESH)
    pl.semaphore_wait(barrier, nchip)


def _remote(src, dst, ssem, rsem, device, orb):
    return pltpu.make_async_remote_copy(
        src_ref=src, dst_ref=dst, send_sem=ssem, recv_sem=rsem,
        device_id=(device, orb), device_id_type=MESH,
    )


def _two_level_sum(nchip, x_ref, pair_recv, part, chip_recv, p_send, p_recv, c_send, c_recv):
    orb, core, partner, chip = _place()
    _barrier_group(nchip, orb, core, partner, chip)
    pair = []
    for j in list(range(1, nchip)) + [0]:
        dst = lax.rem(chip + j, nchip)
        cp = _remote(x_ref.at[dst, 1 - core], pair_recv.at[dst], p_send.at[j], p_recv.at[dst], partner, orb)
        cp.start()
        pair.append(cp)
    sends = []
    for j in range(1, nchip):
        dst = lax.rem(chip + j, nchip)
        pair[j - 1].wait_recv()
        part[dst] = x_ref[dst, core] + pair_recv[dst]
        cp = _remote(part.at[dst], chip_recv.at[chip], c_send.at[j], c_recv.at[chip], 2 * dst + core, orb)
        cp.start()
        sends.append(cp)
    pair[-1].wait_recv()
    total = x_ref[chip, core] + pair_recv[chip]
    for j in range(1, nchip):
        src = lax.rem(chip + nchip - j, nchip)
        _remote(part.at[src], chip_recv.at[src], c_send.at[j], c_recv.at[src], 2 * src + core, orb).wait_recv()
        total = total + chip_recv[src]
    for cp in pair + sends:
        cp.wait_send()
    return total


def allreduce_kernel(nchip, x_ref, out_ref, pair_recv, part, chip_recv, sendbuf, half, other,
                     p_send, p_recv, c_send, c_recv, g_send, g_recv, h_send, h_recv):
    total = _two_level_sum(nchip, x_ref, pair_recv, part, chip_recv, p_send, p_recv, c_send, c_recv)
    orb, core, partner, chip = _place()
    rounded = total.astype(sendbuf.dtype)
    sendbuf[...] = rounded
    sends = []
    for j in range(1, nchip):
        dst = lax.rem(chip + j, nchip)
        cp = _remote(sendbuf, half.at[chip], g_send.at[j], g_recv.at[chip], 2 * dst + core, orb)
        cp.start()
        sends.append(cp)
    cp = _remote(sendbuf, other.at[chip], h_send.at[0], h_recv.at[chip], partner, orb)
    cp.start()
    sends.append(cp)
    out_ref[chip, core] = rounded
    for j in range(1, nchip):
        src = lax.rem(chip + nchip - j, nchip)
        _remote(sendbuf, half.at[src], g_send.at[j], g_recv.at[src], 2 * src + core, orb).wait_recv()
        cp = _remote(half.at[src], other.at[src], h_send.at[j], h_recv.at[src], partner, orb)
        cp.start()
        sends.append(cp)
        out_ref[src, core] = half[src]
    for j in range(nchip):
        src = lax.rem(chip + nchip - j, nchip)
        _remote(sendbuf, other.at[src], h_send.at[j], h_recv.at[src], partner, orb).wait_recv()
        out_ref[src, 1 - core] = other[src]
    for cp in sends:
        cp.wait_send()


def _two_level_scratch(nchip, rows, cols):
    return [
        pltpu.VMEM((nchip, rows, cols), jnp.float32),
        pltpu.VMEM((nchip, rows, cols), jnp.float32),
        pltpu.VMEM((nchip, rows, cols), jnp.float32),
    ]


def allreduce_to_bf16(partial, n):
    rows, cols = partial.shape
    nchip = n // 2
    chunk = rows // n
    x = partial.reshape(nchip, 2, chunk, cols)
    out = pl.pallas_call(
        functools.partial(allreduce_kernel, nchip),
        out_shape=jax.ShapeDtypeStruct((nchip, 2, chunk, cols), jnp.bfloat16),
        in_specs=[pl.BlockSpec(memory_space=pltpu.VMEM)],
        out_specs=pl.BlockSpec(memory_space=pltpu.VMEM),
        scratch_shapes=_two_level_scratch(nchip, chunk, cols) + [
            pltpu.VMEM((chunk, cols), jnp.bfloat16),
            pltpu.VMEM((nchip, chunk, cols), jnp.bfloat16),
            pltpu.VMEM((nchip, chunk, cols), jnp.bfloat16),
        ] + [pltpu.SemaphoreType.DMA((nchip,))] * 8,
        compiler_params=pltpu.CompilerParams(
            collective_id=0, has_side_effects=True, vmem_limit_bytes=12 * 1024 * 1024
        ),
        cost_estimate=pl.CostEstimate(flops=0, bytes_accessed=64 * x.size, transcendentals=0),
    )(x)
    return out.reshape(rows, cols)


def dipole_kernel(nchip, chunk, count, x_ref, out_ref, pair_recv, part, chip_recv,
                  p_send, p_recv, c_send, c_recv):
    out_ref[...] = _two_level_sum(nchip, x_ref, pair_recv, part, chip_recv, p_send, p_recv, c_send, c_recv)


def dipole_scatter(partial, squares, n, count):
    rows, cols = partial.shape
    nchip = n // 2
    chunk = rows // n
    x = jnp.concatenate(
        [
            partial.reshape(nchip, 2, chunk, cols),
            jnp.broadcast_to(squares[None, None, None, :], (nchip, 2, 8, cols)),
        ],
        axis=2,
    )
    total = pl.pallas_call(
        functools.partial(dipole_kernel, nchip, chunk, count),
        out_shape=jax.ShapeDtypeStruct((chunk + 8, cols), jnp.float32),
        in_specs=[pl.BlockSpec(memory_space=pltpu.VMEM)],
        out_specs=pl.BlockSpec(memory_space=pltpu.VMEM),
        scratch_shapes=_two_level_scratch(nchip, chunk + 8, cols)
        + [pltpu.SemaphoreType.DMA((nchip,))] * 4,
        compiler_params=pltpu.CompilerParams(
            collective_id=1, has_side_effects=True, vmem_limit_bytes=12 * 1024 * 1024
        ),
        cost_estimate=pl.CostEstimate(flops=0, bytes_accessed=32 * x.size, transcendentals=0),
    )(x)
    col_norm = 1.0 / jnp.sqrt(total[chunk] / count + 1e-06)
    return (total[:chunk] * col_norm[None, :]).astype(jnp.bfloat16)


def on_device(cont_orbitals, target_orbitals, margin_blocks, dipole_blocks, band_offsets):
    n = lax.axis_size("basis")
    count = band_offsets.shape[0] * BK * n
    cont_padded = with_halo(cont_orbitals, 2)
    margin_cont = band_whole(margin_blocks, band_offsets, cont_padded)
    partial_proj_t = lax.dot_general(
        margin_cont, target_orbitals, (((0,), (0,)), ((), ())), preferred_element_type=jnp.float32
    )
    projection_b_t = allreduce_to_bf16(partial_proj_t, n)
    orth_padded, squares = orthogonalize_with_halo(
        target_orbitals, projection_b_t, cont_orbitals, 3
    )
    dipole_cont, cont_orth = band_local(dipole_blocks, band_offsets, orth_padded, True)
    partial_dip = lax.dot_general(
        target_orbitals,
        dipole_cont,
        (((0,), (0,)), ((), ())),
        preferred_element_type=jnp.float32,
    )
    dipole_mo = dipole_scatter(partial_dip, squares, n, count)
    return (cont_orth, dipole_mo)


def solution(mesh):
    return jax.shard_map(
        on_device,
        mesh=mesh,
        in_specs=(
            P("basis", "orb"),
            P("basis", None),
            P("basis", None, None, None),
            P("basis", None, None, None),
            P("basis", None),
        ),
        out_specs=(P("basis", "orb"), P("basis", "orb")),
        check_vma=False,
    )
```

```python
import functools

import jax
import jax.numpy as jnp
from jax import lax
from jax.experimental import pallas as pl
from jax.experimental.pallas import tpu as pltpu
from jax.sharding import PartitionSpec as P

BK = 256
KB = 4
MESH = pl.DeviceIdType.MESH


def padded_2(block, sides, width):
    for axis, dim in sides:
        count = lax.axis_size(axis)
        forward = [(i, i + 1) for i in range(count - 1)]
        backward = [(target, source) for source, target in forward]
        low = lax.ppermute(
            lax.slice_in_dim(block, block.shape[dim] - width, None, axis=dim), axis, forward
        )
        high = lax.ppermute(lax.slice_in_dim(block, 0, width, axis=dim), axis, backward)
        block = jnp.concatenate([low, block, high], axis=dim)
    return block


def halo_kernel(n, field_ref, out_ref, low, high, send_sem, recv_sem, copy_sem):
    rows, width = field_ref.shape
    edge = 2 * BK
    me = lax.axis_index("basis")
    orb = lax.axis_index("orb")
    has_low = me > 0
    has_high = me < n - 1
    middle = pltpu.make_async_copy(field_ref, out_ref.at[pl.ds(edge, rows)], copy_sem.at[0])
    middle.start()
    barrier = pltpu.get_barrier_semaphore()

    @pl.when(has_low)
    def _():
        pl.semaphore_signal(barrier, inc=1, device_id=(me - 1, orb), device_id_type=MESH)

    @pl.when(has_high)
    def _():
        pl.semaphore_signal(barrier, inc=1, device_id=(me + 1, orb), device_id_type=MESH)

    pl.semaphore_wait(barrier, has_low.astype(jnp.int32) + has_high.astype(jnp.int32))
    to_low = pltpu.make_async_remote_copy(
        src_ref=field_ref.at[pl.ds(0, edge)], dst_ref=high,
        send_sem=send_sem.at[0], recv_sem=recv_sem.at[0],
        device_id=(jnp.maximum(me - 1, 0), orb), device_id_type=MESH,
    )
    to_high = pltpu.make_async_remote_copy(
        src_ref=field_ref.at[pl.ds(rows - edge, edge)], dst_ref=low,
        send_sem=send_sem.at[1], recv_sem=recv_sem.at[1],
        device_id=(jnp.minimum(me + 1, n - 1), orb), device_id_type=MESH,
    )

    @pl.when(has_low)
    def _():
        to_low.start()

    @pl.when(has_high)
    def _():
        to_high.start()

    @pl.when(has_high)
    def _():
        to_low.wait_recv()
        out_ref[pl.ds(rows + edge, edge), :] = high[...]

    @pl.when(jnp.logical_not(has_high))
    def _():
        out_ref[pl.ds(rows + edge, edge), :] = jnp.zeros((edge, width), out_ref.dtype)

    @pl.when(has_low)
    def _():
        to_high.wait_recv()
        out_ref[pl.ds(0, edge), :] = low[...]

    @pl.when(jnp.logical_not(has_low))
    def _():
        out_ref[pl.ds(0, edge), :] = jnp.zeros((edge, width), out_ref.dtype)

    @pl.when(has_low)
    def _():
        to_low.wait_send()

    @pl.when(has_high)
    def _():
        to_high.wait_send()

    middle.wait()


def with_halo(field, collective_id):
    rows, width = field.shape
    n = lax.axis_size("basis")
    return pl.pallas_call(
        functools.partial(halo_kernel, n),
        out_shape=jax.ShapeDtypeStruct((rows + 4 * BK, width), field.dtype),
        in_specs=[pl.BlockSpec(memory_space=pltpu.VMEM)],
        out_specs=pl.BlockSpec(memory_space=pltpu.VMEM),
        scratch_shapes=[
            pltpu.VMEM((2 * BK, width), field.dtype),
            pltpu.VMEM((2 * BK, width), field.dtype),
            pltpu.SemaphoreType.DMA((2,)),
            pltpu.SemaphoreType.DMA((2,)),
            pltpu.SemaphoreType.DMA((1,)),
        ],
        cost_estimate=pl.CostEstimate(flops=0, bytes_accessed=4 * field.size * 2, transcendentals=0),
        compiler_params=pltpu.CompilerParams(
            collective_id=collective_id, has_side_effects=True, vmem_limit_bytes=8 * 1024 * 1024
        ),
    )(field)


def orth_halo_kernel(n, tgt_ref, proj_ref, cont_ref, pad_ref, sq_ref, orth_ref, low, high, send_sem, recv_sem):
    rows, width = cont_ref.shape
    edge = 2 * BK
    me = lax.axis_index("basis")
    orb = lax.axis_index("orb")
    has_low = me > 0
    has_high = me < n - 1
    barrier = pltpu.get_barrier_semaphore()

    @pl.when(has_low)
    def _():
        pl.semaphore_signal(barrier, inc=1, device_id=(me - 1, orb), device_id_type=MESH)

    @pl.when(has_high)
    def _():
        pl.semaphore_signal(barrier, inc=1, device_id=(me + 1, orb), device_id_type=MESH)

    def tile(start):
        removed = lax.dot_general(
            tgt_ref[pl.ds(start, edge), :], proj_ref[...], (((1,), (1,)), ((), ())),
            preferred_element_type=jnp.float32,
        )
        orth = (cont_ref[pl.ds(start, edge), :].astype(jnp.float32) - removed).astype(orth_ref.dtype)
        orth_ref[pl.ds(start, edge), :] = orth
        pad_ref[pl.ds(start + edge, edge), :] = orth
        wide = orth.astype(jnp.float32)
        return jnp.sum(wide * wide, axis=0, keepdims=True)

    squares = tile(0) + tile(rows - edge)
    pl.semaphore_wait(barrier, has_low.astype(jnp.int32) + has_high.astype(jnp.int32))
    to_low = pltpu.make_async_remote_copy(
        src_ref=orth_ref.at[pl.ds(0, edge)], dst_ref=high,
        send_sem=send_sem.at[0], recv_sem=recv_sem.at[0],
        device_id=(jnp.maximum(me - 1, 0), orb), device_id_type=MESH,
    )
    to_high = pltpu.make_async_remote_copy(
        src_ref=orth_ref.at[pl.ds(rows - edge, edge)], dst_ref=low,
        send_sem=send_sem.at[1], recv_sem=recv_sem.at[1],
        device_id=(jnp.minimum(me + 1, n - 1), orb), device_id_type=MESH,
    )

    @pl.when(has_low)
    def _():
        to_low.start()

    @pl.when(has_high)
    def _():
        to_high.start()

    for start in range(edge, rows - edge, edge):
        squares = squares + tile(start)
    sq_ref[...] = squares

    @pl.when(has_high)
    def _():
        to_low.wait_recv()
        pad_ref[pl.ds(rows + edge, edge), :] = high[...]

    @pl.when(jnp.logical_not(has_high))
    def _():
        pad_ref[pl.ds(rows + edge, edge), :] = jnp.zeros((edge, width), pad_ref.dtype)

    @pl.when(has_low)
    def _():
        to_high.wait_recv()
        pad_ref[pl.ds(0, edge), :] = low[...]

    @pl.when(jnp.logical_not(has_low))
    def _():
        pad_ref[pl.ds(0, edge), :] = jnp.zeros((edge, width), pad_ref.dtype)

    @pl.when(has_low)
    def _():
        to_low.wait_send()

    @pl.when(has_high)
    def _():
        to_high.wait_send()


def orthogonalize_with_halo(target, projection_b, cont, collective_id):
    rows, nt = target.shape
    width = cont.shape[1]
    n = lax.axis_size("basis")
    vmem = pl.BlockSpec(memory_space=pltpu.VMEM)
    padded, squares = pl.pallas_call(
        functools.partial(orth_halo_kernel, n),
        out_shape=(
            jax.ShapeDtypeStruct((rows + 4 * BK, width), jnp.bfloat16),
            jax.ShapeDtypeStruct((1, width), jnp.float32),
        ),
        in_specs=[vmem, vmem, vmem],
        out_specs=(vmem, vmem),
        scratch_shapes=[
            pltpu.VMEM((rows, width), jnp.bfloat16),
            pltpu.VMEM((2 * BK, width), jnp.bfloat16),
            pltpu.VMEM((2 * BK, width), jnp.bfloat16),
            pltpu.SemaphoreType.DMA((2,)),
            pltpu.SemaphoreType.DMA((2,)),
        ],
        cost_estimate=pl.CostEstimate(
            flops=2 * rows * nt * width,
            bytes_accessed=target.size * 2 + projection_b.size * 2 + 3 * cont.size * 2,
            transcendentals=0,
        ),
        compiler_params=pltpu.CompilerParams(
            collective_id=collective_id, has_side_effects=True, vmem_limit_bytes=24 * 1024 * 1024
        ),
    )(target, projection_b, cont)
    return padded, squares[0]


def band_kernel(rows_per_step, off_ref, blk_ref, field_ref, out_ref, *mid):
    g = pl.program_id(0)
    if mid:
        start = pl.multiple_of((g * rows_per_step + 2) * BK, BK)
        mid[0][...] = field_ref[pl.ds(start, rows_per_step * BK), :]
    for r in range(rows_per_step):
        b = g * rows_per_step + r
        acc = None
        for k in range(KB):
            start = pl.multiple_of((b + 2 + off_ref[k, b]) * BK, BK)
            term = jnp.dot(
                blk_ref[r, k], field_ref[pl.ds(start, BK), :], preferred_element_type=jnp.float32
            )
            acc = term if acc is None else acc + term
        out_ref[pl.ds(r * BK, BK), :] = acc.astype(out_ref.dtype)


def band_whole_kernel(off_ref, blk_ref, field_ref, low_ref, high_ref, out_ref):
    nblk = blk_ref.shape[0]
    for b in range(nblk):
        if b < 2:
            src, base = low_ref, 2
        elif b >= nblk - 2:
            src, base = high_ref, 4 - nblk
        else:
            src, base = field_ref, 0
        acc = None
        for k in range(KB):
            start = pl.multiple_of((b + base + off_ref[k, b]) * BK, BK)
            term = jnp.dot(blk_ref[b, k], src[pl.ds(start, BK), :], preferred_element_type=jnp.float32)
            acc = term if acc is None else acc + term
        out_ref[pl.ds(b * BK, BK), :] = acc.astype(out_ref.dtype)


def band_whole(blocks, offsets, field, edges):
    nblk = blocks.shape[0]
    rows, width = field.shape
    vmem = pl.BlockSpec(memory_space=pltpu.VMEM)
    return pl.pallas_call(
        band_whole_kernel,
        out_shape=jax.ShapeDtypeStruct((nblk * BK, width), jnp.bfloat16),
        in_specs=[pl.BlockSpec(memory_space=pltpu.SMEM), vmem, vmem, vmem, vmem],
        out_specs=vmem,
        cost_estimate=pl.CostEstimate(
            flops=2 * nblk * KB * BK * BK * width,
            bytes_accessed=blocks.size * 2 + 2 * field.size * 2,
            transcendentals=0,
        ),
        compiler_params=pltpu.CompilerParams(vmem_limit_bytes=8 * 1024 * 1024),
    )(offsets.T, blocks, field, *edges)


def edge_kernel(n, field_ref, low_out, high_out, low, high, send_sem, recv_sem):
    rows, width = field_ref.shape
    edge = 2 * BK
    me = lax.axis_index("basis")
    orb = lax.axis_index("orb")
    has_low = me > 0
    has_high = me < n - 1
    barrier = pltpu.get_barrier_semaphore()

    @pl.when(has_low)
    def _():
        pl.semaphore_signal(barrier, inc=1, device_id=(me - 1, orb), device_id_type=MESH)

    @pl.when(has_high)
    def _():
        pl.semaphore_signal(barrier, inc=1, device_id=(me + 1, orb), device_id_type=MESH)

    pl.semaphore_wait(barrier, has_low.astype(jnp.int32) + has_high.astype(jnp.int32))
    to_low = pltpu.make_async_remote_copy(
        src_ref=field_ref.at[pl.ds(0, edge)], dst_ref=high,
        send_sem=send_sem.at[0], recv_sem=recv_sem.at[0],
        device_id=(jnp.maximum(me - 1, 0), orb), device_id_type=MESH,
    )
    to_high = pltpu.make_async_remote_copy(
        src_ref=field_ref.at[pl.ds(rows - edge, edge)], dst_ref=low,
        send_sem=send_sem.at[1], recv_sem=recv_sem.at[1],
        device_id=(jnp.minimum(me + 1, n - 1), orb), device_id_type=MESH,
    )

    @pl.when(has_low)
    def _():
        to_low.start()

    @pl.when(has_high)
    def _():
        to_high.start()

    low_out[pl.ds(edge, 2 * edge), :] = field_ref[pl.ds(0, 2 * edge), :]
    high_out[pl.ds(0, 2 * edge), :] = field_ref[pl.ds(rows - 2 * edge, 2 * edge), :]

    @pl.when(has_high)
    def _():
        to_low.wait_recv()
        high_out[pl.ds(2 * edge, edge), :] = high[...]

    @pl.when(jnp.logical_not(has_high))
    def _():
        high_out[pl.ds(2 * edge, edge), :] = jnp.zeros((edge, width), high_out.dtype)

    @pl.when(has_low)
    def _():
        to_high.wait_recv()
        low_out[pl.ds(0, edge), :] = low[...]

    @pl.when(jnp.logical_not(has_low))
    def _():
        low_out[pl.ds(0, edge), :] = jnp.zeros((edge, width), low_out.dtype)

    @pl.when(has_low)
    def _():
        to_low.wait_send()

    @pl.when(has_high)
    def _():
        to_high.wait_send()


def edges_of(field, collective_id):
    rows, width = field.shape
    n = lax.axis_size("basis")
    part = jax.ShapeDtypeStruct((6 * BK, width), field.dtype)
    vmem = pl.BlockSpec(memory_space=pltpu.VMEM)
    return pl.pallas_call(
        functools.partial(edge_kernel, n),
        out_shape=(part, part),
        in_specs=[vmem],
        out_specs=(vmem, vmem),
        scratch_shapes=[
            pltpu.VMEM((2 * BK, width), field.dtype),
            pltpu.VMEM((2 * BK, width), field.dtype),
            pltpu.SemaphoreType.DMA((2,)),
            pltpu.SemaphoreType.DMA((2,)),
        ],
        cost_estimate=pl.CostEstimate(flops=0, bytes_accessed=12 * BK * width * 2, transcendentals=0),
        compiler_params=pltpu.CompilerParams(
            collective_id=collective_id, has_side_effects=True, vmem_limit_bytes=8 * 1024 * 1024
        ),
    )(field)


def band_local(blocks, offsets, padded, with_middle=False):
    nblk = blocks.shape[0]
    rows, width = padded.shape
    per = 8 if nblk % 8 == 0 else 1
    field = jax.ShapeDtypeStruct((nblk * BK, width), jnp.bfloat16)
    spec = pl.BlockSpec((per * BK, width), lambda g, off: (g, 0))
    return pl.pallas_call(
        functools.partial(band_kernel, per),
        out_shape=(field, field) if with_middle else field,
        grid_spec=pltpu.PrefetchScalarGridSpec(
            num_scalar_prefetch=1,
            grid=(nblk // per,),
            in_specs=[
                pl.BlockSpec((per, KB, BK, BK), lambda g, off: (g, 0, 0, 0)),
                pl.BlockSpec((rows, width), lambda g, off: (0, 0)),
            ],
            out_specs=(spec, spec) if with_middle else spec,
        ),
        cost_estimate=pl.CostEstimate(
            flops=2 * nblk * KB * BK * BK * width,
            bytes_accessed=blocks.size * 2 + padded.size * 2 + nblk * BK * width * 2,
            transcendentals=0,
        ),
        compiler_params=pltpu.CompilerParams(vmem_limit_bytes=24 * 1024 * 1024),
    )(offsets.T, blocks, padded)


def _place():
    me = lax.axis_index("basis")
    orb = lax.axis_index("orb")
    core = lax.rem(me, 2)
    partner = me + 1 - 2 * core
    chip = lax.div(me, 2)
    return orb, core, partner, chip


def _barrier_group(nchip, orb, core, partner, chip):
    barrier = pltpu.get_barrier_semaphore()
    pl.semaphore_signal(barrier, inc=1, device_id=(partner, orb), device_id_type=MESH)
    for j in range(1, nchip):
        peer = 2 * lax.rem(chip + j, nchip) + core
        pl.semaphore_signal(barrier, inc=1, device_id=(peer, orb), device_id_type=MESH)
    pl.semaphore_wait(barrier, nchip)


def _remote(src, dst, ssem, rsem, device, orb):
    return pltpu.make_async_remote_copy(
        src_ref=src, dst_ref=dst, send_sem=ssem, recv_sem=rsem,
        device_id=(device, orb), device_id_type=MESH,
    )


def _two_level_sum(nchip, x_ref, pair_recv, part, chip_recv, p_send, p_recv, c_send, c_recv):
    orb, core, partner, chip = _place()
    _barrier_group(nchip, orb, core, partner, chip)
    pair = []
    for j in list(range(1, nchip)) + [0]:
        dst = lax.rem(chip + j, nchip)
        cp = _remote(x_ref.at[dst, 1 - core], pair_recv.at[dst], p_send.at[j], p_recv.at[dst], partner, orb)
        cp.start()
        pair.append(cp)
    sends = []
    for j in range(1, nchip):
        dst = lax.rem(chip + j, nchip)
        pair[j - 1].wait_recv()
        part[dst] = x_ref[dst, core] + pair_recv[dst]
        cp = _remote(part.at[dst], chip_recv.at[chip], c_send.at[j], c_recv.at[chip], 2 * dst + core, orb)
        cp.start()
        sends.append(cp)
    pair[-1].wait_recv()
    total = x_ref[chip, core] + pair_recv[chip]
    for j in range(1, nchip):
        src = lax.rem(chip + nchip - j, nchip)
        _remote(part.at[src], chip_recv.at[src], c_send.at[j], c_recv.at[src], 2 * src + core, orb).wait_recv()
        total = total + chip_recv[src]
    for cp in pair + sends:
        cp.wait_send()
    return total


def allreduce_kernel(nchip, x_ref, out_ref, pair_recv, part, chip_recv, sendbuf, half, other,
                     p_send, p_recv, c_send, c_recv, g_send, g_recv, h_send, h_recv):
    total = _two_level_sum(nchip, x_ref, pair_recv, part, chip_recv, p_send, p_recv, c_send, c_recv)
    orb, core, partner, chip = _place()
    rounded = total.astype(sendbuf.dtype)
    sendbuf[...] = rounded
    sends = []
    for j in range(1, nchip):
        dst = lax.rem(chip + j, nchip)
        cp = _remote(sendbuf, half.at[chip], g_send.at[j], g_recv.at[chip], 2 * dst + core, orb)
        cp.start()
        sends.append(cp)
    cp = _remote(sendbuf, other.at[chip], h_send.at[0], h_recv.at[chip], partner, orb)
    cp.start()
    sends.append(cp)
    out_ref[chip, core] = rounded
    for j in range(1, nchip):
        src = lax.rem(chip + nchip - j, nchip)
        _remote(sendbuf, half.at[src], g_send.at[j], g_recv.at[src], 2 * src + core, orb).wait_recv()
        cp = _remote(half.at[src], other.at[src], h_send.at[j], h_recv.at[src], partner, orb)
        cp.start()
        sends.append(cp)
        out_ref[src, core] = half[src]
    for j in range(nchip):
        src = lax.rem(chip + nchip - j, nchip)
        _remote(sendbuf, other.at[src], h_send.at[j], h_recv.at[src], partner, orb).wait_recv()
        out_ref[src, 1 - core] = other[src]
    for cp in sends:
        cp.wait_send()


def _two_level_scratch(nchip, rows, cols):
    return [
        pltpu.VMEM((nchip, rows, cols), jnp.float32),
        pltpu.VMEM((nchip, rows, cols), jnp.float32),
        pltpu.VMEM((nchip, rows, cols), jnp.float32),
    ]


def allreduce_to_bf16(partial, n):
    rows, cols = partial.shape
    nchip = n // 2
    chunk = rows // n
    x = partial.reshape(nchip, 2, chunk, cols)
    out = pl.pallas_call(
        functools.partial(allreduce_kernel, nchip),
        out_shape=jax.ShapeDtypeStruct((nchip, 2, chunk, cols), jnp.bfloat16),
        in_specs=[pl.BlockSpec(memory_space=pltpu.VMEM)],
        out_specs=pl.BlockSpec(memory_space=pltpu.VMEM),
        scratch_shapes=_two_level_scratch(nchip, chunk, cols) + [
            pltpu.VMEM((chunk, cols), jnp.bfloat16),
            pltpu.VMEM((nchip, chunk, cols), jnp.bfloat16),
            pltpu.VMEM((nchip, chunk, cols), jnp.bfloat16),
        ] + [pltpu.SemaphoreType.DMA((nchip,))] * 8,
        compiler_params=pltpu.CompilerParams(
            collective_id=0, has_side_effects=True, vmem_limit_bytes=12 * 1024 * 1024
        ),
        cost_estimate=pl.CostEstimate(flops=0, bytes_accessed=64 * x.size, transcendentals=0),
    )(x)
    return out.reshape(rows, cols)


def dipole_kernel(nchip, chunk, count, x_ref, out_ref, pair_recv, part, chip_recv,
                  p_send, p_recv, c_send, c_recv):
    out_ref[...] = _two_level_sum(nchip, x_ref, pair_recv, part, chip_recv, p_send, p_recv, c_send, c_recv)


def dipole_scatter(partial, squares, n, count):
    rows, cols = partial.shape
    nchip = n // 2
    chunk = rows // n
    x = jnp.concatenate(
        [
            partial.reshape(nchip, 2, chunk, cols),
            jnp.broadcast_to(squares[None, None, None, :], (nchip, 2, 8, cols)),
        ],
        axis=2,
    )
    total = pl.pallas_call(
        functools.partial(dipole_kernel, nchip, chunk, count),
        out_shape=jax.ShapeDtypeStruct((chunk + 8, cols), jnp.float32),
        in_specs=[pl.BlockSpec(memory_space=pltpu.VMEM)],
        out_specs=pl.BlockSpec(memory_space=pltpu.VMEM),
        scratch_shapes=_two_level_scratch(nchip, chunk + 8, cols)
        + [pltpu.SemaphoreType.DMA((nchip,))] * 4,
        compiler_params=pltpu.CompilerParams(
            collective_id=1, has_side_effects=True, vmem_limit_bytes=12 * 1024 * 1024
        ),
        cost_estimate=pl.CostEstimate(flops=0, bytes_accessed=32 * x.size, transcendentals=0),
    )(x)
    col_norm = 1.0 / jnp.sqrt(total[chunk] / count + 1e-06)
    return (total[:chunk] * col_norm[None, :]).astype(jnp.bfloat16)


def on_device(cont_orbitals, target_orbitals, margin_blocks, dipole_blocks, band_offsets):
    n = lax.axis_size("basis")
    count = band_offsets.shape[0] * BK * n
    cont_edges = edges_of(cont_orbitals, 2)
    margin_cont = band_whole(margin_blocks, band_offsets, cont_orbitals, cont_edges)
    partial_proj_t = lax.dot_general(
        margin_cont, target_orbitals, (((0,), (0,)), ((), ())), preferred_element_type=jnp.float32
    )
    projection_b_t = allreduce_to_bf16(partial_proj_t, n)
    orth_padded, squares = orthogonalize_with_halo(
        target_orbitals, projection_b_t, cont_orbitals, 3
    )
    dipole_cont, cont_orth = band_local(dipole_blocks, band_offsets, orth_padded, True)
    partial_dip = lax.dot_general(
        target_orbitals,
        dipole_cont,
        (((0,), (0,)), ((), ())),
        preferred_element_type=jnp.float32,
    )
    dipole_mo = dipole_scatter(partial_dip, squares, n, count)
    return (cont_orth, dipole_mo)


def solution(mesh):
    return jax.shard_map(
        on_device,
        mesh=mesh,
        in_specs=(
            P("basis", "orb"),
            P("basis", None),
            P("basis", None, None, None),
            P("basis", None, None, None),
            P("basis", None),
        ),
        out_specs=(P("basis", "orb"), P("basis", "orb")),
        check_vma=False,
    )
```

```python
import functools

import jax
import jax.numpy as jnp
from jax import lax
from jax.experimental import pallas as pl
from jax.experimental.pallas import tpu as pltpu
from jax.sharding import PartitionSpec as P

BK = 256
KB = 4
MESH = pl.DeviceIdType.MESH


def padded_2(block, sides, width):
    for axis, dim in sides:
        count = lax.axis_size(axis)
        forward = [(i, i + 1) for i in range(count - 1)]
        backward = [(target, source) for source, target in forward]
        low = lax.ppermute(
            lax.slice_in_dim(block, block.shape[dim] - width, None, axis=dim), axis, forward
        )
        high = lax.ppermute(lax.slice_in_dim(block, 0, width, axis=dim), axis, backward)
        block = jnp.concatenate([low, block, high], axis=dim)
    return block


def halo_kernel(n, field_ref, out_ref, low, high, send_sem, recv_sem, copy_sem):
    rows, width = field_ref.shape
    edge = 2 * BK
    me = lax.axis_index("basis")
    orb = lax.axis_index("orb")
    has_low = me > 0
    has_high = me < n - 1
    middle = pltpu.make_async_copy(field_ref, out_ref.at[pl.ds(edge, rows)], copy_sem.at[0])
    middle.start()
    barrier = pltpu.get_barrier_semaphore()

    @pl.when(has_low)
    def _():
        pl.semaphore_signal(barrier, inc=1, device_id=(me - 1, orb), device_id_type=MESH)

    @pl.when(has_high)
    def _():
        pl.semaphore_signal(barrier, inc=1, device_id=(me + 1, orb), device_id_type=MESH)

    pl.semaphore_wait(barrier, has_low.astype(jnp.int32) + has_high.astype(jnp.int32))
    to_low = pltpu.make_async_remote_copy(
        src_ref=field_ref.at[pl.ds(0, edge)], dst_ref=high,
        send_sem=send_sem.at[0], recv_sem=recv_sem.at[0],
        device_id=(jnp.maximum(me - 1, 0), orb), device_id_type=MESH,
    )
    to_high = pltpu.make_async_remote_copy(
        src_ref=field_ref.at[pl.ds(rows - edge, edge)], dst_ref=low,
        send_sem=send_sem.at[1], recv_sem=recv_sem.at[1],
        device_id=(jnp.minimum(me + 1, n - 1), orb), device_id_type=MESH,
    )

    @pl.when(has_low)
    def _():
        to_low.start()

    @pl.when(has_high)
    def _():
        to_high.start()

    @pl.when(has_high)
    def _():
        to_low.wait_recv()
        out_ref[pl.ds(rows + edge, edge), :] = high[...]

    @pl.when(jnp.logical_not(has_high))
    def _():
        out_ref[pl.ds(rows + edge, edge), :] = jnp.zeros((edge, width), out_ref.dtype)

    @pl.when(has_low)
    def _():
        to_high.wait_recv()
        out_ref[pl.ds(0, edge), :] = low[...]

    @pl.when(jnp.logical_not(has_low))
    def _():
        out_ref[pl.ds(0, edge), :] = jnp.zeros((edge, width), out_ref.dtype)

    @pl.when(has_low)
    def _():
        to_low.wait_send()

    @pl.when(has_high)
    def _():
        to_high.wait_send()

    middle.wait()


def with_halo(field, collective_id):
    rows, width = field.shape
    n = lax.axis_size("basis")
    return pl.pallas_call(
        functools.partial(halo_kernel, n),
        out_shape=jax.ShapeDtypeStruct((rows + 4 * BK, width), field.dtype),
        in_specs=[pl.BlockSpec(memory_space=pltpu.VMEM)],
        out_specs=pl.BlockSpec(memory_space=pltpu.VMEM),
        scratch_shapes=[
            pltpu.VMEM((2 * BK, width), field.dtype),
            pltpu.VMEM((2 * BK, width), field.dtype),
            pltpu.SemaphoreType.DMA((2,)),
            pltpu.SemaphoreType.DMA((2,)),
            pltpu.SemaphoreType.DMA((1,)),
        ],
        cost_estimate=pl.CostEstimate(flops=0, bytes_accessed=4 * field.size * 2, transcendentals=0),
        compiler_params=pltpu.CompilerParams(
            collective_id=collective_id, has_side_effects=True, vmem_limit_bytes=8 * 1024 * 1024
        ),
    )(field)


def orth_halo_kernel(n, tgt_ref, proj_ref, cont_ref, pad_ref, sq_ref, orth_ref, low, high, send_sem, recv_sem):
    rows, width = cont_ref.shape
    edge = 2 * BK
    me = lax.axis_index("basis")
    orb = lax.axis_index("orb")
    has_low = me > 0
    has_high = me < n - 1
    barrier = pltpu.get_barrier_semaphore()

    @pl.when(has_low)
    def _():
        pl.semaphore_signal(barrier, inc=1, device_id=(me - 1, orb), device_id_type=MESH)

    @pl.when(has_high)
    def _():
        pl.semaphore_signal(barrier, inc=1, device_id=(me + 1, orb), device_id_type=MESH)

    def tile(start):
        removed = lax.dot_general(
            tgt_ref[pl.ds(start, edge), :], proj_ref[...], (((1,), (1,)), ((), ())),
            preferred_element_type=jnp.float32,
        )
        orth = (cont_ref[pl.ds(start, edge), :].astype(jnp.float32) - removed).astype(orth_ref.dtype)
        orth_ref[pl.ds(start, edge), :] = orth
        pad_ref[pl.ds(start + edge, edge), :] = orth
        wide = orth.astype(jnp.float32)
        return jnp.sum(wide * wide, axis=0, keepdims=True)

    squares = tile(0) + tile(rows - edge)
    pl.semaphore_wait(barrier, has_low.astype(jnp.int32) + has_high.astype(jnp.int32))
    to_low = pltpu.make_async_remote_copy(
        src_ref=orth_ref.at[pl.ds(0, edge)], dst_ref=high,
        send_sem=send_sem.at[0], recv_sem=recv_sem.at[0],
        device_id=(jnp.maximum(me - 1, 0), orb), device_id_type=MESH,
    )
    to_high = pltpu.make_async_remote_copy(
        src_ref=orth_ref.at[pl.ds(rows - edge, edge)], dst_ref=low,
        send_sem=send_sem.at[1], recv_sem=recv_sem.at[1],
        device_id=(jnp.minimum(me + 1, n - 1), orb), device_id_type=MESH,
    )

    @pl.when(has_low)
    def _():
        to_low.start()

    @pl.when(has_high)
    def _():
        to_high.start()

    for start in range(edge, rows - edge, edge):
        squares = squares + tile(start)
    sq_ref[...] = squares

    @pl.when(has_high)
    def _():
        to_low.wait_recv()
        pad_ref[pl.ds(rows + edge, edge), :] = high[...]

    @pl.when(jnp.logical_not(has_high))
    def _():
        pad_ref[pl.ds(rows + edge, edge), :] = jnp.zeros((edge, width), pad_ref.dtype)

    @pl.when(has_low)
    def _():
        to_high.wait_recv()
        pad_ref[pl.ds(0, edge), :] = low[...]

    @pl.when(jnp.logical_not(has_low))
    def _():
        pad_ref[pl.ds(0, edge), :] = jnp.zeros((edge, width), pad_ref.dtype)

    @pl.when(has_low)
    def _():
        to_low.wait_send()

    @pl.when(has_high)
    def _():
        to_high.wait_send()


def orthogonalize_with_halo(target, projection_b, cont, collective_id):
    rows, nt = target.shape
    width = cont.shape[1]
    n = lax.axis_size("basis")
    vmem = pl.BlockSpec(memory_space=pltpu.VMEM)
    padded, squares = pl.pallas_call(
        functools.partial(orth_halo_kernel, n),
        out_shape=(
            jax.ShapeDtypeStruct((rows + 4 * BK, width), jnp.bfloat16),
            jax.ShapeDtypeStruct((1, width), jnp.float32),
        ),
        in_specs=[vmem, vmem, vmem],
        out_specs=(vmem, vmem),
        scratch_shapes=[
            pltpu.VMEM((rows, width), jnp.bfloat16),
            pltpu.VMEM((2 * BK, width), jnp.bfloat16),
            pltpu.VMEM((2 * BK, width), jnp.bfloat16),
            pltpu.SemaphoreType.DMA((2,)),
            pltpu.SemaphoreType.DMA((2,)),
        ],
        cost_estimate=pl.CostEstimate(
            flops=2 * rows * nt * width,
            bytes_accessed=target.size * 2 + projection_b.size * 2 + 3 * cont.size * 2,
            transcendentals=0,
        ),
        compiler_params=pltpu.CompilerParams(
            collective_id=collective_id, has_side_effects=True, vmem_limit_bytes=24 * 1024 * 1024
        ),
    )(target, projection_b, cont)
    return padded, squares[0]


def band_kernel(rows_per_step, off_ref, blk_ref, field_ref, out_ref, *mid):
    g = pl.program_id(0)
    if mid:
        start = pl.multiple_of((g * rows_per_step + 2) * BK, BK)
        mid[0][...] = field_ref[pl.ds(start, rows_per_step * BK), :]
    for r in range(rows_per_step):
        b = g * rows_per_step + r
        acc = None
        for k in range(KB):
            start = pl.multiple_of((b + 2 + off_ref[k, b]) * BK, BK)
            term = jnp.dot(
                blk_ref[r, k], field_ref[pl.ds(start, BK), :], preferred_element_type=jnp.float32
            )
            acc = term if acc is None else acc + term
        out_ref[pl.ds(r * BK, BK), :] = acc.astype(out_ref.dtype)


def band_whole_kernel(off_ref, blk_ref, field_ref, out_ref):
    for b in range(blk_ref.shape[0]):
        acc = None
        for k in range(KB):
            start = pl.multiple_of((b + 2 + off_ref[k, b]) * BK, BK)
            term = jnp.dot(blk_ref[b, k], field_ref[pl.ds(start, BK), :], preferred_element_type=jnp.float32)
            acc = term if acc is None else acc + term
        out_ref[pl.ds(b * BK, BK), :] = acc.astype(out_ref.dtype)


def band_whole(blocks, offsets, padded):
    nblk = blocks.shape[0]
    rows, width = padded.shape
    return pl.pallas_call(
        band_whole_kernel,
        out_shape=jax.ShapeDtypeStruct((nblk * BK, width), jnp.bfloat16),
        in_specs=[
            pl.BlockSpec(memory_space=pltpu.SMEM),
            pl.BlockSpec(memory_space=pltpu.VMEM),
            pl.BlockSpec(memory_space=pltpu.VMEM),
        ],
        out_specs=pl.BlockSpec(memory_space=pltpu.VMEM),
        cost_estimate=pl.CostEstimate(
            flops=2 * nblk * KB * BK * BK * width,
            bytes_accessed=blocks.size * 2 + padded.size * 2 + nblk * BK * width * 2,
            transcendentals=0,
        ),
        compiler_params=pltpu.CompilerParams(vmem_limit_bytes=8 * 1024 * 1024),
    )(offsets.T, blocks, padded)


def band_mid_kernel(off_ref, blk_ref, field_ref, out_ref, mid_ref, sem):
    nblk = blk_ref.shape[0]
    copy = pltpu.make_async_copy(field_ref.at[pl.ds(2 * BK, nblk * BK)], mid_ref, sem.at[0])
    copy.start()
    band_whole_kernel(off_ref, blk_ref, field_ref, out_ref)
    copy.wait()


def band_with_middle(blocks, offsets, padded):
    nblk = blocks.shape[0]
    rows, width = padded.shape
    field = jax.ShapeDtypeStruct((nblk * BK, width), jnp.bfloat16)
    return pl.pallas_call(
        band_mid_kernel,
        out_shape=(field, field),
        in_specs=[
            pl.BlockSpec(memory_space=pltpu.SMEM),
            pl.BlockSpec(memory_space=pltpu.VMEM),
            pl.BlockSpec(memory_space=pltpu.VMEM),
        ],
        out_specs=(pl.BlockSpec(memory_space=pltpu.VMEM), pl.BlockSpec(memory_space=pl.ANY)),
        scratch_shapes=[pltpu.SemaphoreType.DMA((1,))],
        cost_estimate=pl.CostEstimate(
            flops=2 * nblk * KB * BK * BK * width,
            bytes_accessed=blocks.size * 2 + padded.size * 2 + 2 * nblk * BK * width * 2,
            transcendentals=0,
        ),
        compiler_params=pltpu.CompilerParams(vmem_limit_bytes=8 * 1024 * 1024),
    )(offsets.T, blocks, padded)


def band_local(blocks, offsets, padded, with_middle=False):
    nblk = blocks.shape[0]
    rows, width = padded.shape
    per = 8 if nblk % 8 == 0 else 1
    field = jax.ShapeDtypeStruct((nblk * BK, width), jnp.bfloat16)
    spec = pl.BlockSpec((per * BK, width), lambda g, off: (g, 0))
    return pl.pallas_call(
        functools.partial(band_kernel, per),
        out_shape=(field, field) if with_middle else field,
        grid_spec=pltpu.PrefetchScalarGridSpec(
            num_scalar_prefetch=1,
            grid=(nblk // per,),
            in_specs=[
                pl.BlockSpec((per, KB, BK, BK), lambda g, off: (g, 0, 0, 0)),
                pl.BlockSpec((rows, width), lambda g, off: (0, 0)),
            ],
            out_specs=(spec, spec) if with_middle else spec,
        ),
        cost_estimate=pl.CostEstimate(
            flops=2 * nblk * KB * BK * BK * width,
            bytes_accessed=blocks.size * 2 + padded.size * 2 + nblk * BK * width * 2,
            transcendentals=0,
        ),
        compiler_params=pltpu.CompilerParams(vmem_limit_bytes=24 * 1024 * 1024),
    )(offsets.T, blocks, padded)


def _place():
    me = lax.axis_index("basis")
    orb = lax.axis_index("orb")
    core = lax.rem(me, 2)
    partner = me + 1 - 2 * core
    chip = lax.div(me, 2)
    return orb, core, partner, chip


def _barrier_group(nchip, orb, core, partner, chip):
    barrier = pltpu.get_barrier_semaphore()
    pl.semaphore_signal(barrier, inc=1, device_id=(partner, orb), device_id_type=MESH)
    for j in range(1, nchip):
        peer = 2 * lax.rem(chip + j, nchip) + core
        pl.semaphore_signal(barrier, inc=1, device_id=(peer, orb), device_id_type=MESH)
    pl.semaphore_wait(barrier, nchip)


def _remote(src, dst, ssem, rsem, device, orb):
    return pltpu.make_async_remote_copy(
        src_ref=src, dst_ref=dst, send_sem=ssem, recv_sem=rsem,
        device_id=(device, orb), device_id_type=MESH,
    )


def _two_level_sum(nchip, x_ref, pair_recv, part, chip_recv, p_send, p_recv, c_send, c_recv):
    orb, core, partner, chip = _place()
    _barrier_group(nchip, orb, core, partner, chip)
    pair = []
    for j in list(range(1, nchip)) + [0]:
        dst = lax.rem(chip + j, nchip)
        cp = _remote(x_ref.at[dst, 1 - core], pair_recv.at[dst], p_send.at[j], p_recv.at[dst], partner, orb)
        cp.start()
        pair.append(cp)
    sends = []
    for j in range(1, nchip):
        dst = lax.rem(chip + j, nchip)
        pair[j - 1].wait_recv()
        part[dst] = x_ref[dst, core] + pair_recv[dst]
        cp = _remote(part.at[dst], chip_recv.at[chip], c_send.at[j], c_recv.at[chip], 2 * dst + core, orb)
        cp.start()
        sends.append(cp)
    pair[-1].wait_recv()
    total = x_ref[chip, core] + pair_recv[chip]
    for j in range(1, nchip):
        src = lax.rem(chip + nchip - j, nchip)
        _remote(part.at[src], chip_recv.at[src], c_send.at[j], c_recv.at[src], 2 * src + core, orb).wait_recv()
        total = total + chip_recv[src]
    for cp in pair + sends:
        cp.wait_send()
    return total


def allreduce_kernel(nchip, x_ref, out_ref, pair_recv, part, chip_recv, sendbuf, half, other,
                     p_send, p_recv, c_send, c_recv, g_send, g_recv, h_send, h_recv):
    total = _two_level_sum(nchip, x_ref, pair_recv, part, chip_recv, p_send, p_recv, c_send, c_recv)
    orb, core, partner, chip = _place()
    rounded = total.astype(sendbuf.dtype)
    sendbuf[...] = rounded
    sends = []
    for j in range(1, nchip):
        dst = lax.rem(chip + j, nchip)
        cp = _remote(sendbuf, half.at[chip], g_send.at[j], g_recv.at[chip], 2 * dst + core, orb)
        cp.start()
        sends.append(cp)
    cp = _remote(sendbuf, other.at[chip], h_send.at[0], h_recv.at[chip], partner, orb)
    cp.start()
    sends.append(cp)
    out_ref[chip, core] = rounded
    for j in range(1, nchip):
        src = lax.rem(chip + nchip - j, nchip)
        _remote(sendbuf, half.at[src], g_send.at[j], g_recv.at[src], 2 * src + core, orb).wait_recv()
        cp = _remote(half.at[src], other.at[src], h_send.at[j], h_recv.at[src], partner, orb)
        cp.start()
        sends.append(cp)
        out_ref[src, core] = half[src]
    for j in range(nchip):
        src = lax.rem(chip + nchip - j, nchip)
        _remote(sendbuf, other.at[src], h_send.at[j], h_recv.at[src], partner, orb).wait_recv()
        out_ref[src, 1 - core] = other[src]
    for cp in sends:
        cp.wait_send()


def _two_level_scratch(nchip, rows, cols):
    return [
        pltpu.VMEM((nchip, rows, cols), jnp.float32),
        pltpu.VMEM((nchip, rows, cols), jnp.float32),
        pltpu.VMEM((nchip, rows, cols), jnp.float32),
    ]


def allreduce_to_bf16(partial, n):
    rows, cols = partial.shape
    nchip = n // 2
    chunk = rows // n
    x = partial.reshape(nchip, 2, chunk, cols)
    out = pl.pallas_call(
        functools.partial(allreduce_kernel, nchip),
        out_shape=jax.ShapeDtypeStruct((nchip, 2, chunk, cols), jnp.bfloat16),
        in_specs=[pl.BlockSpec(memory_space=pltpu.VMEM)],
        out_specs=pl.BlockSpec(memory_space=pltpu.VMEM),
        scratch_shapes=_two_level_scratch(nchip, chunk, cols) + [
            pltpu.VMEM((chunk, cols), jnp.bfloat16),
            pltpu.VMEM((nchip, chunk, cols), jnp.bfloat16),
            pltpu.VMEM((nchip, chunk, cols), jnp.bfloat16),
        ] + [pltpu.SemaphoreType.DMA((nchip,))] * 8,
        compiler_params=pltpu.CompilerParams(
            collective_id=0, has_side_effects=True, vmem_limit_bytes=12 * 1024 * 1024
        ),
        cost_estimate=pl.CostEstimate(flops=0, bytes_accessed=64 * x.size, transcendentals=0),
    )(x)
    return out.reshape(rows, cols)


def dipole_kernel(nchip, chunk, count, x_ref, out_ref, pair_recv, part, chip_recv,
                  p_send, p_recv, c_send, c_recv):
    out_ref[...] = _two_level_sum(nchip, x_ref, pair_recv, part, chip_recv, p_send, p_recv, c_send, c_recv)


def dipole_scatter(partial, squares, n, count):
    rows, cols = partial.shape
    nchip = n // 2
    chunk = rows // n
    x = jnp.concatenate(
        [
            partial.reshape(nchip, 2, chunk, cols),
            jnp.broadcast_to(squares[None, None, None, :], (nchip, 2, 8, cols)),
        ],
        axis=2,
    )
    total = pl.pallas_call(
        functools.partial(dipole_kernel, nchip, chunk, count),
        out_shape=jax.ShapeDtypeStruct((chunk + 8, cols), jnp.float32),
        in_specs=[pl.BlockSpec(memory_space=pltpu.VMEM)],
        out_specs=pl.BlockSpec(memory_space=pltpu.VMEM),
        scratch_shapes=_two_level_scratch(nchip, chunk + 8, cols)
        + [pltpu.SemaphoreType.DMA((nchip,))] * 4,
        compiler_params=pltpu.CompilerParams(
            collective_id=1, has_side_effects=True, vmem_limit_bytes=12 * 1024 * 1024
        ),
        cost_estimate=pl.CostEstimate(flops=0, bytes_accessed=32 * x.size, transcendentals=0),
    )(x)
    col_norm = 1.0 / jnp.sqrt(total[chunk] / count + 1e-06)
    return (total[:chunk] * col_norm[None, :]).astype(jnp.bfloat16)


def on_device(cont_orbitals, target_orbitals, margin_blocks, dipole_blocks, band_offsets):
    n = lax.axis_size("basis")
    count = band_offsets.shape[0] * BK * n
    cont_padded = with_halo(cont_orbitals, 2)
    margin_cont = band_whole(margin_blocks, band_offsets, cont_padded)
    partial_proj_t = lax.dot_general(
        margin_cont, target_orbitals, (((0,), (0,)), ((), ())), preferred_element_type=jnp.float32
    )
    projection_b_t = allreduce_to_bf16(partial_proj_t, n)
    orth_padded, squares = orthogonalize_with_halo(
        target_orbitals, projection_b_t, cont_orbitals, 3
    )
    dipole_cont, cont_orth = band_with_middle(dipole_blocks, band_offsets, orth_padded)
    partial_dip = lax.dot_general(
        target_orbitals,
        dipole_cont,
        (((0,), (0,)), ((), ())),
        preferred_element_type=jnp.float32,
    )
    dipole_mo = dipole_scatter(partial_dip, squares, n, count)
    return (cont_orth, dipole_mo)


def solution(mesh):
    return jax.shard_map(
        on_device,
        mesh=mesh,
        in_specs=(
            P("basis", "orb"),
            P("basis", None),
            P("basis", None, None, None),
            P("basis", None, None, None),
            P("basis", None),
        ),
        out_specs=(P("basis", "orb"), P("basis", "orb")),
        check_vma=False,
    )
```

```python
import functools

import jax
import jax.numpy as jnp
from jax import lax
from jax.experimental import pallas as pl
from jax.experimental.pallas import tpu as pltpu
from jax.sharding import PartitionSpec as P

BK = 256
KB = 4
MESH = pl.DeviceIdType.MESH


def padded_2(block, sides, width):
    for axis, dim in sides:
        count = lax.axis_size(axis)
        forward = [(i, i + 1) for i in range(count - 1)]
        backward = [(target, source) for source, target in forward]
        low = lax.ppermute(
            lax.slice_in_dim(block, block.shape[dim] - width, None, axis=dim), axis, forward
        )
        high = lax.ppermute(lax.slice_in_dim(block, 0, width, axis=dim), axis, backward)
        block = jnp.concatenate([low, block, high], axis=dim)
    return block


def halo_kernel(n, field_ref, out_ref, low, high, send_sem, recv_sem, copy_sem):
    rows, width = field_ref.shape
    edge = 2 * BK
    me = lax.axis_index("basis")
    orb = lax.axis_index("orb")
    has_low = me > 0
    has_high = me < n - 1
    middle = pltpu.make_async_copy(field_ref, out_ref.at[pl.ds(edge, rows)], copy_sem.at[0])
    middle.start()
    barrier = pltpu.get_barrier_semaphore()

    @pl.when(has_low)
    def _():
        pl.semaphore_signal(barrier, inc=1, device_id=(me - 1, orb), device_id_type=MESH)

    @pl.when(has_high)
    def _():
        pl.semaphore_signal(barrier, inc=1, device_id=(me + 1, orb), device_id_type=MESH)

    pl.semaphore_wait(barrier, has_low.astype(jnp.int32) + has_high.astype(jnp.int32))
    to_low = pltpu.make_async_remote_copy(
        src_ref=field_ref.at[pl.ds(0, edge)], dst_ref=high,
        send_sem=send_sem.at[0], recv_sem=recv_sem.at[0],
        device_id=(jnp.maximum(me - 1, 0), orb), device_id_type=MESH,
    )
    to_high = pltpu.make_async_remote_copy(
        src_ref=field_ref.at[pl.ds(rows - edge, edge)], dst_ref=low,
        send_sem=send_sem.at[1], recv_sem=recv_sem.at[1],
        device_id=(jnp.minimum(me + 1, n - 1), orb), device_id_type=MESH,
    )

    @pl.when(has_low)
    def _():
        to_low.start()

    @pl.when(has_high)
    def _():
        to_high.start()

    @pl.when(has_high)
    def _():
        to_low.wait_recv()
        out_ref[pl.ds(rows + edge, edge), :] = high[...]

    @pl.when(jnp.logical_not(has_high))
    def _():
        out_ref[pl.ds(rows + edge, edge), :] = jnp.zeros((edge, width), out_ref.dtype)

    @pl.when(has_low)
    def _():
        to_high.wait_recv()
        out_ref[pl.ds(0, edge), :] = low[...]

    @pl.when(jnp.logical_not(has_low))
    def _():
        out_ref[pl.ds(0, edge), :] = jnp.zeros((edge, width), out_ref.dtype)

    @pl.when(has_low)
    def _():
        to_low.wait_send()

    @pl.when(has_high)
    def _():
        to_high.wait_send()

    middle.wait()


def with_halo(field, collective_id):
    rows, width = field.shape
    n = lax.axis_size("basis")
    return pl.pallas_call(
        functools.partial(halo_kernel, n),
        out_shape=jax.ShapeDtypeStruct((rows + 4 * BK, width), field.dtype),
        in_specs=[pl.BlockSpec(memory_space=pltpu.VMEM)],
        out_specs=pl.BlockSpec(memory_space=pltpu.VMEM),
        scratch_shapes=[
            pltpu.VMEM((2 * BK, width), field.dtype),
            pltpu.VMEM((2 * BK, width), field.dtype),
            pltpu.SemaphoreType.DMA((2,)),
            pltpu.SemaphoreType.DMA((2,)),
            pltpu.SemaphoreType.DMA((1,)),
        ],
        cost_estimate=pl.CostEstimate(flops=0, bytes_accessed=4 * field.size * 2, transcendentals=0),
        compiler_params=pltpu.CompilerParams(
            collective_id=collective_id, has_side_effects=True, vmem_limit_bytes=8 * 1024 * 1024
        ),
    )(field)


def orth_halo_kernel(n, tgt_ref, proj_ref, cont_ref, pad_ref, sq_ref, orth_ref, low, high, send_sem, recv_sem,
                     proj_t):
    rows, width = cont_ref.shape
    proj_t[...] = proj_ref[...].T
    edge = 2 * BK
    me = lax.axis_index("basis")
    orb = lax.axis_index("orb")
    has_low = me > 0
    has_high = me < n - 1
    barrier = pltpu.get_barrier_semaphore()

    @pl.when(has_low)
    def _():
        pl.semaphore_signal(barrier, inc=1, device_id=(me - 1, orb), device_id_type=MESH)

    @pl.when(has_high)
    def _():
        pl.semaphore_signal(barrier, inc=1, device_id=(me + 1, orb), device_id_type=MESH)

    def tile(start):
        removed = jnp.dot(tgt_ref[pl.ds(start, edge), :], proj_t[...], preferred_element_type=jnp.float32)
        orth = (cont_ref[pl.ds(start, edge), :].astype(jnp.float32) - removed).astype(orth_ref.dtype)
        orth_ref[pl.ds(start, edge), :] = orth
        pad_ref[pl.ds(start + edge, edge), :] = orth
        wide = orth.astype(jnp.float32)
        return jnp.sum(wide * wide, axis=0, keepdims=True)

    squares = tile(0) + tile(rows - edge)
    pl.semaphore_wait(barrier, has_low.astype(jnp.int32) + has_high.astype(jnp.int32))
    to_low = pltpu.make_async_remote_copy(
        src_ref=orth_ref.at[pl.ds(0, edge)], dst_ref=high,
        send_sem=send_sem.at[0], recv_sem=recv_sem.at[0],
        device_id=(jnp.maximum(me - 1, 0), orb), device_id_type=MESH,
    )
    to_high = pltpu.make_async_remote_copy(
        src_ref=orth_ref.at[pl.ds(rows - edge, edge)], dst_ref=low,
        send_sem=send_sem.at[1], recv_sem=recv_sem.at[1],
        device_id=(jnp.minimum(me + 1, n - 1), orb), device_id_type=MESH,
    )

    @pl.when(has_low)
    def _():
        to_low.start()

    @pl.when(has_high)
    def _():
        to_high.start()

    for start in range(edge, rows - edge, edge):
        squares = squares + tile(start)
    sq_ref[...] = squares

    @pl.when(has_high)
    def _():
        to_low.wait_recv()
        pad_ref[pl.ds(rows + edge, edge), :] = high[...]

    @pl.when(jnp.logical_not(has_high))
    def _():
        pad_ref[pl.ds(rows + edge, edge), :] = jnp.zeros((edge, width), pad_ref.dtype)

    @pl.when(has_low)
    def _():
        to_high.wait_recv()
        pad_ref[pl.ds(0, edge), :] = low[...]

    @pl.when(jnp.logical_not(has_low))
    def _():
        pad_ref[pl.ds(0, edge), :] = jnp.zeros((edge, width), pad_ref.dtype)

    @pl.when(has_low)
    def _():
        to_low.wait_send()

    @pl.when(has_high)
    def _():
        to_high.wait_send()


def orthogonalize_with_halo(target, projection_b, cont, collective_id):
    rows, nt = target.shape
    width = cont.shape[1]
    n = lax.axis_size("basis")
    vmem = pl.BlockSpec(memory_space=pltpu.VMEM)
    padded, squares = pl.pallas_call(
        functools.partial(orth_halo_kernel, n),
        out_shape=(
            jax.ShapeDtypeStruct((rows + 4 * BK, width), jnp.bfloat16),
            jax.ShapeDtypeStruct((1, width), jnp.float32),
        ),
        in_specs=[vmem, vmem, vmem],
        out_specs=(vmem, vmem),
        scratch_shapes=[
            pltpu.VMEM((rows, width), jnp.bfloat16),
            pltpu.VMEM((2 * BK, width), jnp.bfloat16),
            pltpu.VMEM((2 * BK, width), jnp.bfloat16),
            pltpu.SemaphoreType.DMA((2,)),
            pltpu.SemaphoreType.DMA((2,)),
            pltpu.VMEM((nt, width), jnp.bfloat16),
        ],
        cost_estimate=pl.CostEstimate(
            flops=2 * rows * nt * width,
            bytes_accessed=target.size * 2 + projection_b.size * 2 + 3 * cont.size * 2,
            transcendentals=0,
        ),
        compiler_params=pltpu.CompilerParams(
            collective_id=collective_id, has_side_effects=True, vmem_limit_bytes=24 * 1024 * 1024
        ),
    )(target, projection_b, cont)
    return padded, squares[0]


def band_kernel(rows_per_step, off_ref, blk_ref, field_ref, out_ref, *mid):
    g = pl.program_id(0)
    if mid:
        start = pl.multiple_of((g * rows_per_step + 2) * BK, BK)
        mid[0][...] = field_ref[pl.ds(start, rows_per_step * BK), :]
    for r in range(rows_per_step):
        b = g * rows_per_step + r
        acc = None
        for k in range(KB):
            start = pl.multiple_of((b + 2 + off_ref[k, b]) * BK, BK)
            term = jnp.dot(
                blk_ref[r, k], field_ref[pl.ds(start, BK), :], preferred_element_type=jnp.float32
            )
            acc = term if acc is None else acc + term
        out_ref[pl.ds(r * BK, BK), :] = acc.astype(out_ref.dtype)


def band_whole_kernel(off_ref, blk_ref, field_ref, out_ref):
    for b in range(blk_ref.shape[0]):
        acc = None
        for k in range(KB):
            start = pl.multiple_of((b + 2 + off_ref[k, b]) * BK, BK)
            term = jnp.dot(blk_ref[b, k], field_ref[pl.ds(start, BK), :], preferred_element_type=jnp.float32)
            acc = term if acc is None else acc + term
        out_ref[pl.ds(b * BK, BK), :] = acc.astype(out_ref.dtype)


def band_whole(blocks, offsets, padded):
    nblk = blocks.shape[0]
    rows, width = padded.shape
    return pl.pallas_call(
        band_whole_kernel,
        out_shape=jax.ShapeDtypeStruct((nblk * BK, width), jnp.bfloat16),
        in_specs=[
            pl.BlockSpec(memory_space=pltpu.SMEM),
            pl.BlockSpec(memory_space=pltpu.VMEM),
            pl.BlockSpec(memory_space=pltpu.VMEM),
        ],
        out_specs=pl.BlockSpec(memory_space=pltpu.VMEM),
        cost_estimate=pl.CostEstimate(
            flops=2 * nblk * KB * BK * BK * width,
            bytes_accessed=blocks.size * 2 + padded.size * 2 + nblk * BK * width * 2,
            transcendentals=0,
        ),
        compiler_params=pltpu.CompilerParams(vmem_limit_bytes=8 * 1024 * 1024),
    )(offsets.T, blocks, padded)


def band_local(blocks, offsets, padded, with_middle=False):
    nblk = blocks.shape[0]
    rows, width = padded.shape
    per = 8 if nblk % 8 == 0 else 1
    field = jax.ShapeDtypeStruct((nblk * BK, width), jnp.bfloat16)
    spec = pl.BlockSpec((per * BK, width), lambda g, off: (g, 0))
    return pl.pallas_call(
        functools.partial(band_kernel, per),
        out_shape=(field, field) if with_middle else field,
        grid_spec=pltpu.PrefetchScalarGridSpec(
            num_scalar_prefetch=1,
            grid=(nblk // per,),
            in_specs=[
                pl.BlockSpec((per, KB, BK, BK), lambda g, off: (g, 0, 0, 0)),
                pl.BlockSpec((rows, width), lambda g, off: (0, 0)),
            ],
            out_specs=(spec, spec) if with_middle else spec,
        ),
        cost_estimate=pl.CostEstimate(
            flops=2 * nblk * KB * BK * BK * width,
            bytes_accessed=blocks.size * 2 + padded.size * 2 + nblk * BK * width * 2,
            transcendentals=0,
        ),
        compiler_params=pltpu.CompilerParams(vmem_limit_bytes=24 * 1024 * 1024),
    )(offsets.T, blocks, padded)


def _place():
    me = lax.axis_index("basis")
    orb = lax.axis_index("orb")
    core = lax.rem(me, 2)
    partner = me + 1 - 2 * core
    chip = lax.div(me, 2)
    return orb, core, partner, chip


def _barrier_group(nchip, orb, core, partner, chip):
    barrier = pltpu.get_barrier_semaphore()
    pl.semaphore_signal(barrier, inc=1, device_id=(partner, orb), device_id_type=MESH)
    for j in range(1, nchip):
        peer = 2 * lax.rem(chip + j, nchip) + core
        pl.semaphore_signal(barrier, inc=1, device_id=(peer, orb), device_id_type=MESH)
    pl.semaphore_wait(barrier, nchip)


def _remote(src, dst, ssem, rsem, device, orb):
    return pltpu.make_async_remote_copy(
        src_ref=src, dst_ref=dst, send_sem=ssem, recv_sem=rsem,
        device_id=(device, orb), device_id_type=MESH,
    )


def _two_level_sum(nchip, x_ref, pair_recv, part, chip_recv, p_send, p_recv, c_send, c_recv):
    orb, core, partner, chip = _place()
    _barrier_group(nchip, orb, core, partner, chip)
    pair = []
    for j in list(range(1, nchip)) + [0]:
        dst = lax.rem(chip + j, nchip)
        cp = _remote(x_ref.at[dst, 1 - core], pair_recv.at[dst], p_send.at[j], p_recv.at[dst], partner, orb)
        cp.start()
        pair.append(cp)
    sends = []
    for j in range(1, nchip):
        dst = lax.rem(chip + j, nchip)
        pair[j - 1].wait_recv()
        part[dst] = x_ref[dst, core] + pair_recv[dst]
        cp = _remote(part.at[dst], chip_recv.at[chip], c_send.at[j], c_recv.at[chip], 2 * dst + core, orb)
        cp.start()
        sends.append(cp)
    pair[-1].wait_recv()
    total = x_ref[chip, core] + pair_recv[chip]
    for j in range(1, nchip):
        src = lax.rem(chip + nchip - j, nchip)
        _remote(part.at[src], chip_recv.at[src], c_send.at[j], c_recv.at[src], 2 * src + core, orb).wait_recv()
        total = total + chip_recv[src]
    for cp in pair + sends:
        cp.wait_send()
    return total


def allreduce_kernel(nchip, x_ref, out_ref, pair_recv, part, chip_recv, sendbuf, half, other,
                     p_send, p_recv, c_send, c_recv, g_send, g_recv, h_send, h_recv):
    total = _two_level_sum(nchip, x_ref, pair_recv, part, chip_recv, p_send, p_recv, c_send, c_recv)
    orb, core, partner, chip = _place()
    rounded = total.astype(sendbuf.dtype)
    sendbuf[...] = rounded
    sends = []
    for j in range(1, nchip):
        dst = lax.rem(chip + j, nchip)
        cp = _remote(sendbuf, half.at[chip], g_send.at[j], g_recv.at[chip], 2 * dst + core, orb)
        cp.start()
        sends.append(cp)
    cp = _remote(sendbuf, other.at[chip], h_send.at[0], h_recv.at[chip], partner, orb)
    cp.start()
    sends.append(cp)
    out_ref[chip, core] = rounded
    for j in range(1, nchip):
        src = lax.rem(chip + nchip - j, nchip)
        _remote(sendbuf, half.at[src], g_send.at[j], g_recv.at[src], 2 * src + core, orb).wait_recv()
        cp = _remote(half.at[src], other.at[src], h_send.at[j], h_recv.at[src], partner, orb)
        cp.start()
        sends.append(cp)
        out_ref[src, core] = half[src]
    for j in range(nchip):
        src = lax.rem(chip + nchip - j, nchip)
        _remote(sendbuf, other.at[src], h_send.at[j], h_recv.at[src], partner, orb).wait_recv()
        out_ref[src, 1 - core] = other[src]
    for cp in sends:
        cp.wait_send()


def _two_level_scratch(nchip, rows, cols):
    return [
        pltpu.VMEM((nchip, rows, cols), jnp.float32),
        pltpu.VMEM((nchip, rows, cols), jnp.float32),
        pltpu.VMEM((nchip, rows, cols), jnp.float32),
    ]


def allreduce_to_bf16(partial, n):
    rows, cols = partial.shape
    nchip = n // 2
    chunk = rows // n
    x = partial.reshape(nchip, 2, chunk, cols)
    out = pl.pallas_call(
        functools.partial(allreduce_kernel, nchip),
        out_shape=jax.ShapeDtypeStruct((nchip, 2, chunk, cols), jnp.bfloat16),
        in_specs=[pl.BlockSpec(memory_space=pltpu.VMEM)],
        out_specs=pl.BlockSpec(memory_space=pltpu.VMEM),
        scratch_shapes=_two_level_scratch(nchip, chunk, cols) + [
            pltpu.VMEM((chunk, cols), jnp.bfloat16),
            pltpu.VMEM((nchip, chunk, cols), jnp.bfloat16),
            pltpu.VMEM((nchip, chunk, cols), jnp.bfloat16),
        ] + [pltpu.SemaphoreType.DMA((nchip,))] * 8,
        compiler_params=pltpu.CompilerParams(
            collective_id=0, has_side_effects=True, vmem_limit_bytes=12 * 1024 * 1024
        ),
        cost_estimate=pl.CostEstimate(flops=0, bytes_accessed=64 * x.size, transcendentals=0),
    )(x)
    return out.reshape(rows, cols)


def dipole_kernel(nchip, chunk, count, x_ref, out_ref, pair_recv, part, chip_recv,
                  p_send, p_recv, c_send, c_recv):
    out_ref[...] = _two_level_sum(nchip, x_ref, pair_recv, part, chip_recv, p_send, p_recv, c_send, c_recv)


def dipole_scatter(partial, squares, n, count):
    rows, cols = partial.shape
    nchip = n // 2
    chunk = rows // n
    x = jnp.concatenate(
        [
            partial.reshape(nchip, 2, chunk, cols),
            jnp.broadcast_to(squares[None, None, None, :], (nchip, 2, 8, cols)),
        ],
        axis=2,
    )
    total = pl.pallas_call(
        functools.partial(dipole_kernel, nchip, chunk, count),
        out_shape=jax.ShapeDtypeStruct((chunk + 8, cols), jnp.float32),
        in_specs=[pl.BlockSpec(memory_space=pltpu.VMEM)],
        out_specs=pl.BlockSpec(memory_space=pltpu.VMEM),
        scratch_shapes=_two_level_scratch(nchip, chunk + 8, cols)
        + [pltpu.SemaphoreType.DMA((nchip,))] * 4,
        compiler_params=pltpu.CompilerParams(
            collective_id=1, has_side_effects=True, vmem_limit_bytes=12 * 1024 * 1024
        ),
        cost_estimate=pl.CostEstimate(flops=0, bytes_accessed=32 * x.size, transcendentals=0),
    )(x)
    col_norm = 1.0 / jnp.sqrt(total[chunk] / count + 1e-06)
    return (total[:chunk] * col_norm[None, :]).astype(jnp.bfloat16)


def on_device(cont_orbitals, target_orbitals, margin_blocks, dipole_blocks, band_offsets):
    n = lax.axis_size("basis")
    count = band_offsets.shape[0] * BK * n
    cont_padded = with_halo(cont_orbitals, 2)
    margin_cont = band_whole(margin_blocks, band_offsets, cont_padded)
    partial_proj_t = lax.dot_general(
        margin_cont, target_orbitals, (((0,), (0,)), ((), ())), preferred_element_type=jnp.float32
    )
    projection_b_t = allreduce_to_bf16(partial_proj_t, n)
    orth_padded, squares = orthogonalize_with_halo(
        target_orbitals, projection_b_t, cont_orbitals, 3
    )
    dipole_cont, cont_orth = band_local(dipole_blocks, band_offsets, orth_padded, True)
    partial_dip = lax.dot_general(
        target_orbitals,
        dipole_cont,
        (((0,), (0,)), ((), ())),
        preferred_element_type=jnp.float32,
    )
    dipole_mo = dipole_scatter(partial_dip, squares, n, count)
    return (cont_orth, dipole_mo)


def solution(mesh):
    return jax.shard_map(
        on_device,
        mesh=mesh,
        in_specs=(
            P("basis", "orb"),
            P("basis", None),
            P("basis", None, None, None),
            P("basis", None, None, None),
            P("basis", None),
        ),
        out_specs=(P("basis", "orb"), P("basis", "orb")),
        check_vma=False,
    )
```
